32 devices in a mesh: groups: 2 (over y), gx: 4 (over x, core), vert: 4 (over z).
Axes of the slice: x: 2, y: 2, z: 4, core: 2. Of those that a mesh axis runs over, the one named last changes fastest.
Arguments:
- distribution: float32 [64, 16, 16, 2048], P(('groups', 'gx'), None, None, 'vert'), parts along dimension 0, may hold values from 0.05 to 2
- velocity_order: int32 [2048], P('vert'), may hold values from 0 to 2047, each once
- cell_codes: int32 [64, 16, 16], P(('groups', 'gx')), parts along dimension 0, may hold values from 0 to 2, as said below
- knudsen: float32 [2], P('groups'), parts along dimension 0, may hold values from 0.05 to 1
- inflow: float32 [8], P('groups'), parts along dimension 0, may hold values from 0.5 to 1.5
Outputs:
- evolved: float32 [64, 16, 16, 2048], P(('groups', 'gx'), None, None, 'vert'), parts along dimension 0
The draws below stay inside these ranges and needn't reach their ends.
There are 2 independent parts, one for each index of `groups`. The reference program is written for one: setup_inputs(seed, part) draws one part's arguments, and reference() takes and returns one part's arrays. A program takes and returns all parts, laid end to end along the dimension named above; an argument that names none is the same for every part. Nothing has to cross between parts.
Inputs may be any that keep to these rules, and one draw needn't show every extreme that they name: `velocity_order`: names each of the 2048 velocity grid points once. `cell_codes`: 0 marks an open cell, 1 an inflow cell, 2 a wall cell.
All inputs are finite; a program needn't handle non-finite values.
Results may differ from the reference program's by a relative error of at most 0.0003.
Values sent between devices are 32-bit elements; how exact they have to be, the bound alone decides.
No kernel may reach another device: no remote copies, remote signals or barrier semaphores. Data moves between devices by JAX's collectives and lax.ppermute only.
A program may use at most 128 MiB of HBM per device.

```python
import math
import jax
import jax.numpy as jnp
from jax import lax

NY = 16
NZ = 16
VGX = 16
VGY = 16
VGZ = 8
STEPS = 3
V = 2048
NX = 32


def draw_cell_codes(key, part):
    raw = jax.random.randint(key, (NX, NY, NZ), 0, 16)
    return jnp.where(raw == 14, 1, jnp.where(raw == 15, 2, 0)).astype(jnp.int32)


def level_of(own_key, shape, split, low, high):
    def one(position, blocks):
        steps = jax.random.uniform(jax.random.fold_in(jax.random.fold_in(own_key, 6), position), (blocks,), jnp.float32, low / len(split), high / len(split))
        return jnp.repeat(jnp.exp(steps), shape[position] // blocks).reshape((-1,) + (1,) * (len(shape) - position - 1))

    factor_of = one(*split[0])
    for cut in split[1:]:
        factor_of = factor_of * one(*cut)
    return factor_of


def setup_inputs(seed: int = 0, part: int = 0) -> dict:
    streams_of = jax.random.split(jax.random.key(seed), 6)
    own_keys = jax.random.split(jax.random.fold_in(streams_of[5], part), 6)
    return {
        "distribution": jnp.clip(jnp.exp(math.log(2.0) - 3.6888794 * jax.random.uniform(own_keys[0], (NX, NY, NZ, V), jnp.float32) ** level_of(own_keys[0], (NX, NY, NZ, V), ((0, 4), (3, 4)), -0.2, 0.2)), 0.05, 2.0),
        "velocity_order": jax.random.permutation(streams_of[1], V).astype(jnp.int32),
        "cell_codes": draw_cell_codes(jax.random.fold_in(jax.random.fold_in(streams_of[5], part), 71), part),
        "knudsen": jnp.clip(jnp.exp(jax.random.uniform(own_keys[3], (1,), jnp.float32, math.log(0.05), math.log(1.0))), 0.05, 1.0),
        "inflow": jnp.clip(jax.random.uniform(own_keys[4], (4,), jnp.float32, 0.5, 1.5), 0.5, 1.5),
    }


def grid_velocity(index, count):
    return (index.astype(jnp.float32) + 0.5 - count / 2) * (6.0 / count)


def velocity_parts(order):
    plane = VGY * VGZ
    first = grid_velocity(order // plane, VGX)
    second = grid_velocity((order // VGZ) % VGY, VGY)
    third = grid_velocity(order % VGZ, VGZ)
    return first, second, third


def minmod(lower, upper):
    return 0.5 * (jnp.sign(lower) + jnp.sign(upper)) * jnp.minimum(jnp.abs(lower), jnp.abs(upper))


def face_change(padded, courant, dim):
    count = padded.shape[dim] - 4
    left = lax.slice_in_dim(padded, 0, count + 2, axis=dim)
    centre = lax.slice_in_dim(padded, 1, count + 3, axis=dim)
    right = lax.slice_in_dim(padded, 2, count + 4, axis=dim)
    slope = minmod(centre - left, right - centre)
    low_cell = lax.slice_in_dim(centre, 0, count + 1, axis=dim)
    high_cell = lax.slice_in_dim(centre, 1, count + 2, axis=dim)
    low_slope = lax.slice_in_dim(slope, 0, count + 1, axis=dim)
    high_slope = lax.slice_in_dim(slope, 1, count + 2, axis=dim)
    ahead = jnp.maximum(courant, 0.0)
    behind = jnp.minimum(courant, 0.0)
    flux = ahead * (low_cell + 0.5 * (1.0 - courant) * low_slope) + behind * (high_cell - 0.5 * (1.0 + courant) * high_slope)
    return lax.slice_in_dim(flux, 1, count + 1, axis=dim) - lax.slice_in_dim(flux, 0, count, axis=dim)


def reference(distribution, velocity_order, cell_codes, knudsen, inflow):
    first, second, third = velocity_parts(velocity_order)
    table = jnp.stack([jnp.ones_like(first), first, second, third, 0.5 * (first * first + second * second + third * third)], axis=1)
    inflow_shape = jnp.exp(-((first - inflow[1]) ** 2 + second * second + third * third) / (2.0 * inflow[2]))
    inflow_state = inflow[0] * inflow_shape / jnp.mean(inflow_shape)
    wall_shape = jnp.exp(-(first * first + second * second + third * third) / (2.0 * inflow[3]))
    wall_norm = jnp.mean(wall_shape)
    codes = cell_codes[..., None]
    state = distribution
    for step in range(STEPS):
        padded_x = jnp.pad(state, ((2, 2), (0, 0), (0, 0), (0, 0)))
        padded_y = jnp.pad(state, ((0, 0), (2, 2), (0, 0), (0, 0)), mode="wrap")
        padded_z = jnp.pad(state, ((0, 0), (0, 0), (2, 2), (0, 0)), mode="wrap")
        moved = state - face_change(padded_x, 0.1 * first, 0)
        moved = moved - face_change(padded_y, second / 30.0, 1)
        moved = moved - face_change(padded_z, third / 30.0, 2)
        kinetic_integrals = jnp.dot(moved.reshape(-1, V), table, precision=lax.Precision.HIGHEST, preferred_element_type=jnp.float32) / V
        kinetic_integrals = kinetic_integrals.T.reshape(5, NX, NY, NZ)
        particle_concentration = kinetic_integrals[0]
        mean_flow_xaxis = kinetic_integrals[1] / particle_concentration
        mean_flow_yaxis = kinetic_integrals[2] / particle_concentration
        mean_flow_zaxis = kinetic_integrals[3] / particle_concentration
        kinetic_heat_level = (2.0 * kinetic_integrals[4] / particle_concentration - (mean_flow_xaxis ** 2 + mean_flow_yaxis ** 2 + mean_flow_zaxis ** 2)) / 3.0
        maxwellian_width = ((first - mean_flow_xaxis[..., None]) ** 2 + (second - mean_flow_yaxis[..., None]) ** 2 + (third - mean_flow_zaxis[..., None]) ** 2)
        extent_tuple = jnp.exp(-maxwellian_width / (2.0 * kinetic_heat_level[..., None]))
        norm = jnp.mean(extent_tuple, axis=-1)
        equilibrium = particle_concentration[..., None] * extent_tuple / norm[..., None]
        rate = 0.5 * particle_concentration / (particle_concentration + knudsen[0])
        relaxed = moved + rate[..., None] * (equilibrium - moved)
        wall = particle_concentration[..., None] * wall_shape / wall_norm
        state = jnp.where(codes == 1, inflow_state, jnp.where(codes == 2, wall, relaxed))
    return state
```

```python
import functools

import jax
import jax.numpy as jnp
from jax import lax
from jax.experimental import pallas as pl
from jax.experimental.pallas import tpu as pltpu
from jax.sharding import PartitionSpec as P

VGX = 16
VGY = 16
VGZ = 8
STEPS = 3
LANES = 128
SUB = 8
FEATURES = 32
UNIT = 3.0 / 16.0
LOG2E = 1.4426950408889634
VMEM_LIMIT = 48 * 1024 * 1024
F32 = jnp.float32
BF16 = jnp.bfloat16


def minmod(lower, upper):
    return jnp.maximum(
        jnp.minimum(lower, upper), jnp.minimum(jnp.maximum(lower, upper), 0.0)
    )


def x_pass(load, rows, store, coef):
    first, last = rows[0], rows[-1]
    reach, lean = coef[0], coef[1]
    ahead = coef[2] > 0.0

    def one(y, carry):
        for t in range(2):
            cells = {n: load(n, y, t) for n in range(first - 2, last + 3)}
            steps = {n: cells[n + 1] - cells[n] for n in range(first - 2, last + 2)}
            faces = {
                n: cells[n] + lean * minmod(steps[n - 1], steps[n])
                for n in range(first - 1, last + 2)
            }
            for n in rows:
                source = jnp.where(ahead, faces[n - 1], faces[n + 1])
                store(n, y, t, cells[n] - reach * (faces[n] - source))
        return carry

    lax.fori_loop(0, 16, one, 0)


def yz_pass(load, update, coef):
    reach_y, lean_y, ahead_y = coef[3], coef[4], coef[5] > 0.0
    reach_z, lean_z, ahead_z = coef[6], coef[7], coef[8] > 0.0
    place = lax.broadcasted_iota(jnp.int32, (SUB, LANES), 0)
    top, bottom = place == SUB - 1, place == 0
    crossing = (ahead_z & bottom) | (jnp.logical_not(ahead_z) & top)
    count = 16
    cells = {}
    steps = {}
    faces = {}

    def cell(y, t):
        y %= count
        if (y, t) not in cells:
            cells[y, t] = load(y, t)
        return cells[y, t]

    def step(y, t):
        y %= count
        if (y, t) not in steps:
            steps[y, t] = cell(y + 1, t) - cell(y, t)
        return steps[y, t]

    def face(y, t):
        y %= count
        if (y, t) not in faces:
            faces[y, t] = cell(y, t) + lean_y * minmod(step(y - 1, t), step(y, t))
        return faces[y, t]

    def up(v):
        return pltpu.roll(v, SUB - 1, 0)

    def down(v):
        return pltpu.roll(v, 1, 0)

    for y in range(count):
        changes = [
            reach_y * (face(y, t) - jnp.where(ahead_y, face(y - 1, t), face(y + 1, t)))
            for t in range(2)
        ]
        low, high = cell(y, 0), cell(y, 1)
        up_low, up_high = up(low), up(high)
        step_low = jnp.where(top, up_high, up_low) - low
        step_high = jnp.where(top, up_low, up_high) - high
        down_low, down_high = down(step_low), down(step_high)
        face_low = low + lean_z * minmod(
            jnp.where(bottom, down_high, down_low), step_low
        )
        face_high = high + lean_z * minmod(
            jnp.where(bottom, down_low, down_high), step_high
        )
        turn_low = jnp.where(ahead_z, down(face_low), up(face_low))
        turn_high = jnp.where(ahead_z, down(face_high), up(face_high))
        changes[0] += reach_z * (face_low - jnp.where(crossing, turn_high, turn_low))
        changes[1] += reach_z * (face_high - jnp.where(crossing, turn_low, turn_high))
        for t in range(2):
            update(y, t, changes[t])


def row_moments(block, weights):
    flat = block.reshape(256, LANES)
    high = flat.astype(BF16)
    rest = (flat - high.astype(F32)).astype(BF16)
    contract = (((1,), (1,)), ((), ()))
    total = lax.dot_general(weights, high, contract, preferred_element_type=F32)
    total += lax.dot_general(weights, rest, contract, preferred_element_type=F32)
    return total[:SUB]


def write_moments(out, place, value):
    for m in range(4):
        out[m, pl.ds(place, 1), :] = value[m : m + 1]
    out[4, pl.ds(place, 1), :] = value[4:5] + value[5:6]


def three_parts(value):
    high = value.astype(BF16).astype(F32)
    rest = value - high
    middle = rest.astype(BF16).astype(F32)
    low = (rest - middle).astype(BF16).astype(F32)
    return high, middle, low


def spread_features(params, wide, tall, rows):
    alpha, beta_x, beta_y, beta_z, gamma, keep = params
    alpha = jnp.where(gamma == 0.0, -10000.0, alpha)
    zero = jnp.zeros_like(alpha)
    columns = []
    for value in (alpha, beta_x, beta_y, beta_z, gamma, gamma, keep):
        columns.extend(three_parts(value))
    columns.extend([zero] * (FEATURES - len(columns)))
    for k, value in enumerate(columns):
        for r in range(rows):
            wide[r, k : k + 1, :] = value[r : r + 1]
    for r in range(rows):
        tall[r] = wide[r].T.astype(BF16)


def relax_row(features, table, source):
    product = jnp.dot(features, table, preferred_element_type=F32)
    block = source.reshape(256, LANES)
    block = product[:, LANES:] * block + jnp.exp2(product[:, :LANES])
    return block.reshape(16, 2, SUB, LANES)


def param_kernel(total, count, *refs):
    parts = refs[:count]
    codes, knudsen, inflow, out, out_low, out_high = refs[count:]
    sums = [parts[0][m] for m in range(5)]
    for part in parts[1:]:
        sums = [s + part[m] for m, s in enumerate(sums)]
    density = sums[0] * (1.0 / total)
    scale = UNIT / sums[0]
    u_x, u_y, u_z = (sums[m] * scale for m in (1, 2, 3))
    heat = (UNIT * sums[4] * scale - (u_x * u_x + u_y * u_y + u_z * u_z)) * (1.0 / 3.0)
    rate = 0.5 * density / (density + knudsen[0])
    code = codes[...]
    flowing, wall = code == 1, code == 2
    closed = flowing | wall
    u_x = jnp.where(flowing, inflow[1], jnp.where(wall, 0.0, u_x))
    u_y = jnp.where(closed, 0.0, u_y)
    u_z = jnp.where(closed, 0.0, u_z)
    heat = jnp.where(flowing, inflow[2], jnp.where(wall, inflow[3], heat))
    amount = jnp.where(flowing, inflow[0], jnp.where(wall, density, rate * density))
    keep = jnp.where(closed, 0.0, 1.0 - rate)
    g = (-0.5 * LOG2E) / heat

    def line(u, n, unit):
        s = None
        for i in range(n):
            gap = (i + 0.5 - n / 2) * unit - u
            e = jnp.exp2(g * (gap * gap))
            s = e if s is None else s + e
        return s

    norm = line(u_x, VGX, 6.0 / VGX) * line(u_y, VGY, 6.0 / VGY)
    norm = norm * line(u_z, VGZ, 6.0 / VGZ) * (1.0 / total)
    alpha = (jnp.log(amount) - jnp.log(norm)) * LOG2E
    alpha = alpha + g * (u_x * u_x + u_y * u_y + u_z * u_z)
    lean = (-2.0 * UNIT) * g
    params = (alpha, lean * u_x, lean * u_y, lean * u_z, g * (UNIT * UNIT), keep)
    rows = code.shape[0]
    for k, value in enumerate(params):
        out[k] = value
        out_low[k] = value[:2]
        out_high[k] = value[rows - 2 :]


def inner_kernel(relax, rows, *refs):
    if relax:
        (m_low, m_mid, m_high, params, table, coef_ref, weights, state, out, sums,
         wide, tall, acc) = refs
    else:
        state, coef_ref, weights, out, sums, acc = refs
    chunk, chunks = pl.program_id(0), pl.num_programs(0)
    inner = rows - 4
    if relax:

        @pl.when(chunk == 0)
        def _():
            spread_features([params[k] for k in range(6)], wide, tall, rows)

        columns = table[0]
        for r in range(2):
            state[r] = relax_row(tall[r], columns, m_low[r])

        def middle(r, carry):
            state[r + 2] = relax_row(tall[r + 2], columns, m_mid[r])
            return carry

        lax.fori_loop(0, inner, middle, 0)
        for r in range(2):
            state[rows - 2 + r] = relax_row(tall[rows - 2 + r], columns, m_high[r])
    coef = [coef_ref[k] for k in range(9)]

    def store(n, y, t, v):
        out[n - 2, y, t] = v

    x_pass(lambda n, y, t: state[n, y, t], list(range(2, rows - 2)), store, coef)

    def one(r, carry):
        def update(y, t, v):
            out[r, y, t] = out[r, y, t] - v

        yz_pass(lambda y, t: state[r + 2, y, t], update, coef)
        part = row_moments(out[r], weights[...])

        @pl.when(chunk == 0)
        def _():
            acc[r] = part

        @pl.when(chunk > 0)
        def _():
            acc[r] = acc[r] + part

        return carry

    lax.fori_loop(0, inner, one, 0)

    @pl.when(chunk == chunks - 1)
    def _():
        for r in range(inner):
            write_moments(sums, r, acc[r])


def edge_kernel(relax, rows, *refs):
    if relax:
        (h_low, h_high, p_low, p_high, table, state, coef_ref, weights, inner_sums,
         out_low, out_high, sums, wide, tall, halo, acc) = refs
    else:
        (h_low, h_high, state, coef_ref, weights, inner_sums,
         out_low, out_high, sums, acc) = refs
    chunk, chunks = pl.program_id(0), pl.num_programs(0)
    if relax:

        @pl.when(chunk == 0)
        def _():
            spread_features([p_low[k] for k in range(6)], wide, tall.at[0], 2)
            spread_features([p_high[k] for k in range(6)], wide, tall.at[1], 2)

        columns = table[0]
        for r in range(2):
            halo[0, r] = relax_row(tall[0, r], columns, h_low[r])
            halo[1, r] = relax_row(tall[1, r], columns, h_high[r])
        low, high = halo.at[0], halo.at[1]
    else:
        low, high = h_low, h_high
    coef = [coef_ref[k] for k in range(9)]

    def load(n, y, t):
        if n < 0:
            return low[n + 2, y, t]
        if n >= rows:
            return high[n - rows, y, t]
        return state[n, y, t]

    for side, first, out in ((0, 0, out_low), (1, rows - 2, out_high)):

        def store(n, y, t, v, first=first, out=out):
            out[n - first, y, t] = v

        x_pass(load, [first, first + 1], store, coef)

        def one(r, carry, side=side, first=first, out=out):
            def update(y, t, v):
                out[r, y, t] = out[r, y, t] - v

            yz_pass(lambda y, t: state[r + first, y, t], update, coef)
            part = row_moments(out[r], weights[...])
            place = r + 2 * side

            @pl.when(chunk == 0)
            def _():
                acc[place] = part

            @pl.when(chunk > 0)
            def _():
                acc[place] = acc[place] + part

            return carry

        lax.fori_loop(0, 2, one, 0)

    @pl.when(chunk == chunks - 1)
    def _():
        for m in range(5):
            sums[m, 2 : rows - 2, :] = inner_sums[m]
        for r in range(2):
            write_moments(sums, r, acc[r])
            write_moments(sums, rows - 2 + r, acc[2 + r])


def final_kernel(rows, *refs):
    m_low, m_mid, m_high, params, table, out, wide, tall = refs

    @pl.when(pl.program_id(0) == 0)
    def _():
        spread_features([params[k] for k in range(6)], wide, tall, rows)

    columns = table[0]
    for r in range(2):
        out[r] = relax_row(tall[r], columns, m_low[r])
        out[rows - 2 + r] = relax_row(tall[rows - 2 + r], columns, m_high[r])

    def middle(r, carry):
        out[r + 2] = relax_row(tall[r + 2], columns, m_mid[r])
        return carry

    lax.fori_loop(0, rows - 4, middle, 0)


def body(distribution, velocity_order, cell_codes, knudsen, inflow):
    rows, count_y, count_z, width = distribution.shape
    peers = lax.axis_size("vert")
    total = width * peers
    chunks = width // LANES
    state = distribution.reshape(rows, count_y, 2, SUB, width)
    codes = cell_codes.reshape(rows, count_y * count_z)

    plane = VGY * VGZ
    n_x = 2 * (velocity_order // plane) - (VGX - 1)
    n_y = 2 * (velocity_order // VGZ % VGY) - (VGY - 1)
    n_z = 2 * (2 * (velocity_order % VGZ) - (VGZ - 1))
    square = n_x * n_x + n_y * n_y + n_z * n_z
    ones = jnp.ones_like(n_x)
    low_part = square % 8
    whole = jnp.stack([ones, n_x, n_y, n_z, square - low_part, low_part]).astype(F32)
    weights = jnp.pad(whole, ((0, 10), (0, 0))).astype(BF16)
    exponent = jnp.repeat(whole, 3, axis=0)
    exponent = jnp.pad(exponent, ((0, FEATURES - 18), (0, 0)))
    exponent = exponent.reshape(FEATURES, chunks, LANES)
    place = lax.broadcasted_iota(jnp.int32, (FEATURES, chunks, LANES), 0)
    factor = jnp.where((place >= 18) & (place < 21), 1.0, 0.0)
    table = jnp.concatenate([exponent, factor], axis=2)
    table = table.transpose(1, 0, 2).astype(BF16)
    coef = []
    for n, scale in ((n_x, 0.1), (n_y, 1.0 / 30.0), (n_z, 1.0 / 30.0)):
        courant = n.astype(F32) * UNIT * scale
        sign = jnp.where(n > 0, 1.0, -1.0)
        reach = jnp.abs(courant)
        coef.extend([reach, 0.5 * sign * (1.0 - reach), sign])
    coef = jnp.broadcast_to(jnp.stack(coef)[:, None, :], (9, SUB, width))

    def slab(n):
        return pl.BlockSpec((n, count_y, 2, SUB, LANES), lambda c: (0, 0, 0, 0, c))

    def slab_shape(n):
        return jax.ShapeDtypeStruct((n, count_y, 2, SUB, width), F32)

    cells = count_y * count_z
    whole_sums = pl.BlockSpec((5, rows, cells), lambda c: (0, 0, 0))
    inner_sums = pl.BlockSpec((5, rows - 4, cells), lambda c: (0, 0, 0))
    param_spec = pl.BlockSpec((6, rows, cells), lambda c: (0, 0, 0))
    edge_params = pl.BlockSpec((6, 2, cells), lambda c: (0, 0, 0))
    table_spec = pl.BlockSpec((1, FEATURES, 2 * LANES), lambda c: (c, 0, 0))
    coef_spec = pl.BlockSpec((9, SUB, LANES), lambda c: (0, 0, c))
    weight_spec = pl.BlockSpec((16, LANES), lambda c: (0, c))
    limits = pltpu.CompilerParams(
        dimension_semantics=("arbitrary",), vmem_limit_bytes=VMEM_LIMIT
    )

    def feature_scratch(n):
        return [pltpu.VMEM((n, FEATURES, cells), F32), pltpu.VMEM((n, cells, FEATURES), BF16)]

    def inner(relax, args):
        acc = pltpu.VMEM((rows - 4, SUB, cells), F32)
        sums = jax.ShapeDtypeStruct((5, rows - 4, cells), F32)
        if relax:
            return pl.pallas_call(
                functools.partial(inner_kernel, True, rows),
                grid=(chunks,),
                in_specs=[slab(2), slab(rows - 4), slab(2), param_spec, table_spec, coef_spec, weight_spec],
                out_specs=[slab(rows), slab(rows - 4), inner_sums],
                out_shape=[slab_shape(rows), slab_shape(rows - 4), sums],
                scratch_shapes=feature_scratch(rows) + [acc],
                compiler_params=limits,
                name="inner_relax",
            )(*args, table, coef, weights)
        return pl.pallas_call(
            functools.partial(inner_kernel, False, rows),
            grid=(chunks,),
            in_specs=[slab(rows), coef_spec, weight_spec],
            out_specs=[slab(rows - 4), inner_sums],
            out_shape=[slab_shape(rows - 4), sums],
            scratch_shapes=[acc],
            compiler_params=limits,
            name="inner_first",
        )(*args, coef, weights)

    def edge(relax, halos, params, state, sums):
        acc = pltpu.VMEM((4, SUB, cells), F32)
        out_specs = [slab(2), slab(2), whole_sums]
        out_shape = [slab_shape(2), slab_shape(2), jax.ShapeDtypeStruct((5, rows, cells), F32)]
        tail = [slab(rows), coef_spec, weight_spec, inner_sums]
        if relax:
            return pl.pallas_call(
                functools.partial(edge_kernel, True, rows),
                grid=(chunks,),
                in_specs=[slab(2), slab(2), edge_params, edge_params, table_spec] + tail,
                out_specs=out_specs,
                out_shape=out_shape,
                scratch_shapes=[
                    pltpu.VMEM((2, FEATURES, cells), F32),
                    pltpu.VMEM((2, 2, cells, FEATURES), BF16),
                    pltpu.VMEM((2, 2, count_y, 2, SUB, LANES), F32),
                    acc,
                ],
                compiler_params=limits,
                name="edge_relax",
            )(*halos, *params, table, state, coef, weights, sums)
        return pl.pallas_call(
            functools.partial(edge_kernel, False, rows),
            grid=(chunks,),
            in_specs=[slab(2), slab(2)] + tail,
            out_specs=out_specs,
            out_shape=out_shape,
            scratch_shapes=[acc],
            compiler_params=limits,
            name="edge_first",
        )(*halos, state, coef, weights, sums)

    smem = pl.BlockSpec(memory_space=pltpu.SMEM)
    vmem = pl.BlockSpec(memory_space=pltpu.VMEM)

    def cell_params(parts):
        return pl.pallas_call(
            functools.partial(param_kernel, total, len(parts)),
            in_specs=[vmem] * (len(parts) + 1) + [smem, smem],
            out_specs=[vmem] * 3,
            out_shape=[
                jax.ShapeDtypeStruct((6, n, cells), F32) for n in (rows, 2, 2)
            ],
            name="cell_params",
        )(*parts, codes, knudsen, inflow)

    def final(args):
        return pl.pallas_call(
            functools.partial(final_kernel, rows),
            grid=(chunks,),
            in_specs=[slab(2), slab(rows - 4), slab(2), param_spec, table_spec],
            out_specs=slab(rows),
            out_shape=slab_shape(rows),
            scratch_shapes=feature_scratch(rows),
            compiler_params=limits,
            name="final_relax",
        )(*args, table)

    line = lax.axis_size("gx")
    forward = [(i, i + 1) for i in range(line - 1)]
    backward = [(i + 1, i) for i in range(line - 1)]

    def exchange(low, high):
        return lax.ppermute(high, "gx", forward), lax.ppermute(low, "gx", backward)

    def gather(part):
        parts = [part]
        for shift in range(1, peers):
            pairs = [(i, (i + shift) % peers) for i in range(peers)]
            parts.append(lax.ppermute(part, "vert", pairs))
        return parts

    halos = exchange(state[:2], state[rows - 2 :])
    m_mid, sums = inner(False, (state,))
    m_low, m_high, sums = edge(False, halos, None, state, sums)
    for step in range(1, STEPS + 1):
        if step < STEPS:
            halos = exchange(m_low, m_high)
        params, p_low, p_high = cell_params(gather(sums))
        if step == STEPS:
            break
        p_halos = exchange(p_low, p_high)
        state, m_mid, sums = inner(True, (m_low, m_mid, m_high, params))
        m_low, m_high, sums = edge(True, halos, p_halos, state, sums)
    result = final((m_low, m_mid, m_high, params))
    return result.reshape(rows, count_y, count_z, width)


def solution(mesh):
    placed = (
        P(("groups", "gx"), None, None, "vert"),
        P("vert"),
        P(("groups", "gx"), None, None),
        P("groups"),
        P("groups"),
    )
    return jax.shard_map(
        body,
        mesh=mesh,
        in_specs=placed,
        out_specs=P(("groups", "gx"), None, None, "vert"),
        check_vma=False,
    )
```

```python
import functools

import jax
import jax.numpy as jnp
from jax import lax
from jax.experimental import pallas as pl
from jax.experimental.pallas import tpu as pltpu
from jax.sharding import PartitionSpec as P

VGX = 16
VGY = 16
VGZ = 8
STEPS = 3
LANES = 128
SUB = 8
FEATURES = 32
UNIT = 3.0 / 16.0
LOG2E = 1.4426950408889634
VMEM_LIMIT = 14 * 1024 * 1024
F32 = jnp.float32
BF16 = jnp.bfloat16


def minmod(lower, upper):
    return jnp.maximum(
        jnp.minimum(lower, upper), jnp.minimum(jnp.maximum(lower, upper), 0.0)
    )


def x_pass(load, rows, store, coef):
    first, last = rows[0], rows[-1]
    reach, lean = coef[0], coef[1]
    ahead = coef[2] > 0.0

    def one(y, carry):
        for t in range(2):
            cells = {n: load(n, y, t) for n in range(first - 2, last + 3)}
            steps = {n: cells[n + 1] - cells[n] for n in range(first - 2, last + 2)}
            faces = {
                n: cells[n] + lean * minmod(steps[n - 1], steps[n])
                for n in range(first - 1, last + 2)
            }
            for n in rows:
                source = jnp.where(ahead, faces[n - 1], faces[n + 1])
                store(n, y, t, cells[n] - reach * (faces[n] - source))
        return carry

    lax.fori_loop(0, 16, one, 0)


def yz_pass(load, update, coef):
    reach_y, lean_y, ahead_y = coef[3], coef[4], coef[5] > 0.0
    reach_z, lean_z, ahead_z = coef[6], coef[7], coef[8] > 0.0
    place = lax.broadcasted_iota(jnp.int32, (SUB, LANES), 0)
    top, bottom = place == SUB - 1, place == 0
    crossing = (ahead_z & bottom) | (jnp.logical_not(ahead_z) & top)
    count = 16
    cells = {}
    steps = {}
    faces = {}

    def cell(y, t):
        y %= count
        if (y, t) not in cells:
            cells[y, t] = load(y, t)
        return cells[y, t]

    def step(y, t):
        y %= count
        if (y, t) not in steps:
            steps[y, t] = cell(y + 1, t) - cell(y, t)
        return steps[y, t]

    def face(y, t):
        y %= count
        if (y, t) not in faces:
            faces[y, t] = cell(y, t) + lean_y * minmod(step(y - 1, t), step(y, t))
        return faces[y, t]

    def up(v):
        return pltpu.roll(v, SUB - 1, 0)

    def down(v):
        return pltpu.roll(v, 1, 0)

    for y in range(count):
        changes = [
            reach_y * (face(y, t) - jnp.where(ahead_y, face(y - 1, t), face(y + 1, t)))
            for t in range(2)
        ]
        low, high = cell(y, 0), cell(y, 1)
        up_low, up_high = up(low), up(high)
        step_low = jnp.where(top, up_high, up_low) - low
        step_high = jnp.where(top, up_low, up_high) - high
        down_low, down_high = down(step_low), down(step_high)
        face_low = low + lean_z * minmod(
            jnp.where(bottom, down_high, down_low), step_low
        )
        face_high = high + lean_z * minmod(
            jnp.where(bottom, down_low, down_high), step_high
        )
        turn_low = jnp.where(ahead_z, down(face_low), up(face_low))
        turn_high = jnp.where(ahead_z, down(face_high), up(face_high))
        changes[0] += reach_z * (face_low - jnp.where(crossing, turn_high, turn_low))
        changes[1] += reach_z * (face_high - jnp.where(crossing, turn_low, turn_high))
        for t in range(2):
            update(y, t, changes[t])


def row_moments(block, weights):
    flat = block.reshape(256, LANES)
    high = flat.astype(BF16)
    rest = (flat - high.astype(F32)).astype(BF16)
    contract = (((1,), (1,)), ((), ()))
    total = lax.dot_general(weights, high, contract, preferred_element_type=F32)
    total += lax.dot_general(weights, rest, contract, preferred_element_type=F32)
    return total[:SUB]


def write_moments(out, place, value):
    for m in range(4):
        out[m, pl.ds(place, 1), :] = value[m : m + 1]
    out[4, pl.ds(place, 1), :] = value[4:5] + value[5:6]


def three_parts(value):
    high = value.astype(BF16).astype(F32)
    rest = value - high
    middle = rest.astype(BF16).astype(F32)
    low = (rest - middle).astype(BF16).astype(F32)
    return high, middle, low


def spread_features(params, wide, tall, rows):
    alpha, beta_x, beta_y, beta_z, gamma, keep = params
    alpha = jnp.where(gamma == 0.0, -10000.0, alpha)
    zero = jnp.zeros_like(alpha)
    columns = []
    for value in (alpha, beta_x, beta_y, beta_z, gamma, gamma, keep):
        columns.extend(three_parts(value))
    columns.extend([zero] * (FEATURES - len(columns)))
    for k, value in enumerate(columns):
        for r in range(rows):
            wide[r, k : k + 1, :] = value[r : r + 1]
    for r in range(rows):
        tall[r] = wide[r].T.astype(BF16)


def relax_row(features, table, source):
    product = jnp.dot(features, table, preferred_element_type=F32)
    block = source.reshape(256, LANES)
    block = product[:, LANES:] * block + jnp.exp2(product[:, :LANES])
    return block.reshape(16, 2, SUB, LANES)


def param_kernel(total, count, *refs):
    parts = refs[:count]
    codes, knudsen, inflow, out, out_low, out_high = refs[count:]
    sums = [parts[0][m] for m in range(5)]
    for part in parts[1:]:
        sums = [s + part[m] for m, s in enumerate(sums)]
    density = sums[0] * (1.0 / total)
    scale = UNIT / sums[0]
    u_x, u_y, u_z = (sums[m] * scale for m in (1, 2, 3))
    heat = (UNIT * sums[4] * scale - (u_x * u_x + u_y * u_y + u_z * u_z)) * (1.0 / 3.0)
    rate = 0.5 * density / (density + knudsen[0])
    code = codes[...]
    flowing, wall = code == 1, code == 2
    closed = flowing | wall
    u_x = jnp.where(flowing, inflow[1], jnp.where(wall, 0.0, u_x))
    u_y = jnp.where(closed, 0.0, u_y)
    u_z = jnp.where(closed, 0.0, u_z)
    heat = jnp.where(flowing, inflow[2], jnp.where(wall, inflow[3], heat))
    amount = jnp.where(flowing, inflow[0], jnp.where(wall, density, rate * density))
    keep = jnp.where(closed, 0.0, 1.0 - rate)
    g = (-0.5 * LOG2E) / heat

    def line(u, n, unit):
        s = None
        for i in range(n):
            gap = (i + 0.5 - n / 2) * unit - u
            e = jnp.exp2(g * (gap * gap))
            s = e if s is None else s + e
        return s

    norm = line(u_x, VGX, 6.0 / VGX) * line(u_y, VGY, 6.0 / VGY)
    norm = norm * line(u_z, VGZ, 6.0 / VGZ) * (1.0 / total)
    alpha = (jnp.log(amount) - jnp.log(norm)) * LOG2E
    alpha = alpha + g * (u_x * u_x + u_y * u_y + u_z * u_z)
    lean = (-2.0 * UNIT) * g
    params = (alpha, lean * u_x, lean * u_y, lean * u_z, g * (UNIT * UNIT), keep)
    rows = code.shape[0]
    for k, value in enumerate(params):
        out[k] = value
        out_low[k] = value[:2]
        out_high[k] = value[rows - 2 :]


def inner_kernel(relax, rows, *refs):
    if relax:
        (m_low, m_mid, m_high, params, table, coef_ref, weights, state, out, sums,
         wide, tall, acc) = refs
    else:
        state, coef_ref, weights, out, sums, acc = refs
    chunk, chunks = pl.program_id(0), pl.num_programs(0)
    inner = rows - 4
    if relax:

        @pl.when(chunk == 0)
        def _():
            spread_features([params[k] for k in range(6)], wide, tall, rows)

        columns = table[0]
        for r in range(2):
            state[r] = relax_row(tall[r], columns, m_low[r])

        def middle(r, carry):
            state[r + 2] = relax_row(tall[r + 2], columns, m_mid[r])
            return carry

        lax.fori_loop(0, inner, middle, 0)
        for r in range(2):
            state[rows - 2 + r] = relax_row(tall[rows - 2 + r], columns, m_high[r])
    coef = [coef_ref[k] for k in range(9)]

    def store(n, y, t, v):
        out[n - 2, y, t] = v

    x_pass(lambda n, y, t: state[n, y, t], list(range(2, rows - 2)), store, coef)

    def one(r, carry):
        def update(y, t, v):
            out[r, y, t] = out[r, y, t] - v

        yz_pass(lambda y, t: state[r + 2, y, t], update, coef)
        part = row_moments(out[r], weights[...])

        @pl.when(chunk == 0)
        def _():
            acc[r] = part

        @pl.when(chunk > 0)
        def _():
            acc[r] = acc[r] + part

        return carry

    lax.fori_loop(0, inner, one, 0)

    @pl.when(chunk == chunks - 1)
    def _():
        for r in range(inner):
            write_moments(sums, r, acc[r])


def edge_kernel(relax, rows, *refs):
    if relax:
        (h_low, h_high, p_low, p_high, table, state, coef_ref, weights, inner_sums,
         out_low, out_high, sums, wide, tall, halo, acc) = refs
    else:
        (h_low, h_high, state, coef_ref, weights, inner_sums,
         out_low, out_high, sums, acc) = refs
    chunk, chunks = pl.program_id(0), pl.num_programs(0)
    if relax:

        @pl.when(chunk == 0)
        def _():
            spread_features([p_low[k] for k in range(6)], wide, tall.at[0], 2)
            spread_features([p_high[k] for k in range(6)], wide, tall.at[1], 2)

        columns = table[0]
        for r in range(2):
            halo[0, r] = relax_row(tall[0, r], columns, h_low[r])
            halo[1, r] = relax_row(tall[1, r], columns, h_high[r])
        low, high = halo.at[0], halo.at[1]
    else:
        low, high = h_low, h_high
    coef = [coef_ref[k] for k in range(9)]

    def load(n, y, t):
        if n < 0:
            return low[n + 2, y, t]
        if n >= rows:
            return high[n - rows, y, t]
        return state[n, y, t]

    for side, first, out in ((0, 0, out_low), (1, rows - 2, out_high)):

        def store(n, y, t, v, first=first, out=out):
            out[n - first, y, t] = v

        x_pass(load, [first, first + 1], store, coef)

        def one(r, carry, side=side, first=first, out=out):
            def update(y, t, v):
                out[r, y, t] = out[r, y, t] - v

            yz_pass(lambda y, t: state[r + first, y, t], update, coef)
            part = row_moments(out[r], weights[...])
            place = r + 2 * side

            @pl.when(chunk == 0)
            def _():
                acc[place] = part

            @pl.when(chunk > 0)
            def _():
                acc[place] = acc[place] + part

            return carry

        lax.fori_loop(0, 2, one, 0)

    @pl.when(chunk == chunks - 1)
    def _():
        for m in range(5):
            sums[m, 2 : rows - 2, :] = inner_sums[m]
        for r in range(2):
            write_moments(sums, r, acc[r])
            write_moments(sums, rows - 2 + r, acc[2 + r])


def final_kernel(rows, *refs):
    m_low, m_mid, m_high, params, table, out, wide, tall = refs

    @pl.when(pl.program_id(0) == 0)
    def _():
        spread_features([params[k] for k in range(6)], wide, tall, rows)

    columns = table[0]
    for r in range(2):
        out[r] = relax_row(tall[r], columns, m_low[r])
        out[rows - 2 + r] = relax_row(tall[rows - 2 + r], columns, m_high[r])

    def middle(r, carry):
        out[r + 2] = relax_row(tall[r + 2], columns, m_mid[r])
        return carry

    lax.fori_loop(0, rows - 4, middle, 0)


def body(distribution, velocity_order, cell_codes, knudsen, inflow):
    rows, count_y, count_z, width = distribution.shape
    peers = lax.axis_size("vert")
    total = width * peers
    chunks = width // LANES
    state = distribution.reshape(rows, count_y, 2, SUB, width)
    codes = cell_codes.reshape(rows, count_y * count_z)

    plane = VGY * VGZ
    n_x = 2 * (velocity_order // plane) - (VGX - 1)
    n_y = 2 * (velocity_order // VGZ % VGY) - (VGY - 1)
    n_z = 2 * (2 * (velocity_order % VGZ) - (VGZ - 1))
    square = n_x * n_x + n_y * n_y + n_z * n_z
    ones = jnp.ones_like(n_x)
    low_part = square % 8
    whole = jnp.stack([ones, n_x, n_y, n_z, square - low_part, low_part]).astype(F32)
    weights = jnp.pad(whole, ((0, 10), (0, 0))).astype(BF16)
    exponent = jnp.repeat(whole, 3, axis=0)
    exponent = jnp.pad(exponent, ((0, FEATURES - 18), (0, 0)))
    exponent = exponent.reshape(FEATURES, chunks, LANES)
    place = lax.broadcasted_iota(jnp.int32, (FEATURES, chunks, LANES), 0)
    factor = jnp.where((place >= 18) & (place < 21), 1.0, 0.0)
    table = jnp.concatenate([exponent, factor], axis=2)
    table = table.transpose(1, 0, 2).astype(BF16)
    coef = []
    for n, scale in ((n_x, 0.1), (n_y, 1.0 / 30.0), (n_z, 1.0 / 30.0)):
        courant = n.astype(F32) * UNIT * scale
        sign = jnp.where(n > 0, 1.0, -1.0)
        reach = jnp.abs(courant)
        coef.extend([reach, 0.5 * sign * (1.0 - reach), sign])
    coef = jnp.broadcast_to(jnp.stack(coef)[:, None, :], (9, SUB, width))

    def slab(n):
        return pl.BlockSpec((n, count_y, 2, SUB, LANES), lambda c: (0, 0, 0, 0, c))

    def slab_shape(n):
        return jax.ShapeDtypeStruct((n, count_y, 2, SUB, width), F32)

    cells = count_y * count_z
    whole_sums = pl.BlockSpec((5, rows, cells), lambda c: (0, 0, 0))
    inner_sums = pl.BlockSpec((5, rows - 4, cells), lambda c: (0, 0, 0))
    param_spec = pl.BlockSpec((6, rows, cells), lambda c: (0, 0, 0))
    edge_params = pl.BlockSpec((6, 2, cells), lambda c: (0, 0, 0))
    table_spec = pl.BlockSpec((1, FEATURES, 2 * LANES), lambda c: (c, 0, 0))
    coef_spec = pl.BlockSpec((9, SUB, LANES), lambda c: (0, 0, c))
    weight_spec = pl.BlockSpec((16, LANES), lambda c: (0, c))
    limits = pltpu.CompilerParams(
        dimension_semantics=("arbitrary",), vmem_limit_bytes=VMEM_LIMIT
    )

    def feature_scratch(n):
        return [pltpu.VMEM((n, FEATURES, cells), F32), pltpu.VMEM((n, cells, FEATURES), BF16)]

    def inner(relax, args):
        acc = pltpu.VMEM((rows - 4, SUB, cells), F32)
        sums = jax.ShapeDtypeStruct((5, rows - 4, cells), F32)
        if relax:
            return pl.pallas_call(
                functools.partial(inner_kernel, True, rows),
                grid=(chunks,),
                in_specs=[slab(2), slab(rows - 4), slab(2), param_spec, table_spec, coef_spec, weight_spec],
                out_specs=[slab(rows), slab(rows - 4), inner_sums],
                out_shape=[slab_shape(rows), slab_shape(rows - 4), sums],
                scratch_shapes=feature_scratch(rows) + [acc],
                compiler_params=limits,
                name="inner_relax",
            )(*args, table, coef, weights)
        return pl.pallas_call(
            functools.partial(inner_kernel, False, rows),
            grid=(chunks,),
            in_specs=[slab(rows), coef_spec, weight_spec],
            out_specs=[slab(rows - 4), inner_sums],
            out_shape=[slab_shape(rows - 4), sums],
            scratch_shapes=[acc],
            compiler_params=limits,
            name="inner_first",
        )(*args, coef, weights)

    def edge(relax, halos, params, state, sums):
        acc = pltpu.VMEM((4, SUB, cells), F32)
        out_specs = [slab(2), slab(2), whole_sums]
        out_shape = [slab_shape(2), slab_shape(2), jax.ShapeDtypeStruct((5, rows, cells), F32)]
        tail = [slab(rows), coef_spec, weight_spec, inner_sums]
        if relax:
            return pl.pallas_call(
                functools.partial(edge_kernel, True, rows),
                grid=(chunks,),
                in_specs=[slab(2), slab(2), edge_params, edge_params, table_spec] + tail,
                out_specs=out_specs,
                out_shape=out_shape,
                scratch_shapes=[
                    pltpu.VMEM((2, FEATURES, cells), F32),
                    pltpu.VMEM((2, 2, cells, FEATURES), BF16),
                    pltpu.VMEM((2, 2, count_y, 2, SUB, LANES), F32),
                    acc,
                ],
                compiler_params=limits,
                name="edge_relax",
            )(*halos, *params, table, state, coef, weights, sums)
        return pl.pallas_call(
            functools.partial(edge_kernel, False, rows),
            grid=(chunks,),
            in_specs=[slab(2), slab(2)] + tail,
            out_specs=out_specs,
            out_shape=out_shape,
            scratch_shapes=[acc],
            compiler_params=limits,
            name="edge_first",
        )(*halos, state, coef, weights, sums)

    smem = pl.BlockSpec(memory_space=pltpu.SMEM)
    vmem = pl.BlockSpec(memory_space=pltpu.VMEM)

    def cell_params(parts):
        return pl.pallas_call(
            functools.partial(param_kernel, total, len(parts)),
            in_specs=[vmem] * (len(parts) + 1) + [smem, smem],
            out_specs=[vmem] * 3,
            out_shape=[
                jax.ShapeDtypeStruct((6, n, cells), F32) for n in (rows, 2, 2)
            ],
            compiler_params=pltpu.CompilerParams(vmem_limit_bytes=4 * 1024 * 1024),
            name="cell_params",
        )(*parts, codes, knudsen, inflow)

    def final(args):
        return pl.pallas_call(
            functools.partial(final_kernel, rows),
            grid=(chunks,),
            in_specs=[slab(2), slab(rows - 4), slab(2), param_spec, table_spec],
            out_specs=slab(rows),
            out_shape=slab_shape(rows),
            scratch_shapes=feature_scratch(rows),
            compiler_params=limits,
            name="final_relax",
        )(*args, table)

    line = lax.axis_size("gx")
    forward = [(i, i + 1) for i in range(line - 1)]
    backward = [(i + 1, i) for i in range(line - 1)]

    def exchange(low, high):
        return lax.ppermute(high, "gx", forward), lax.ppermute(low, "gx", backward)

    def gather(part):
        parts = [part]
        for shift in range(1, peers):
            pairs = [(i, (i + shift) % peers) for i in range(peers)]
            parts.append(lax.ppermute(part, "vert", pairs))
        return parts

    halos = exchange(state[:2], state[rows - 2 :])
    m_mid, sums = inner(False, (state,))
    m_low, m_high, sums = edge(False, halos, None, state, sums)
    for step in range(1, STEPS + 1):
        if step < STEPS:
            halos = exchange(m_low, m_high)
        params, p_low, p_high = cell_params(gather(sums))
        if step == STEPS:
            break
        p_halos = exchange(p_low, p_high)
        state, m_mid, sums = inner(True, (m_low, m_mid, m_high, params))
        m_low, m_high, sums = edge(True, halos, p_halos, state, sums)
    result = final((m_low, m_mid, m_high, params))
    return result.reshape(rows, count_y, count_z, width)


def solution(mesh):
    placed = (
        P(("groups", "gx"), None, None, "vert"),
        P("vert"),
        P(("groups", "gx"), None, None),
        P("groups"),
        P("groups"),
    )
    return jax.shard_map(
        body,
        mesh=mesh,
        in_specs=placed,
        out_specs=P(("groups", "gx"), None, None, "vert"),
        check_vma=False,
    )
```

```python
import functools

import jax
import jax.numpy as jnp
from jax import lax
from jax.experimental import pallas as pl
from jax.experimental.pallas import tpu as pltpu
from jax.sharding import PartitionSpec as P

VGX = 16
VGY = 16
VGZ = 8
STEPS = 3
LANES = 128
SUB = 8
FEATURES = 32
PAIR = 2 * LANES
UNIT = 3.0 / 16.0
LOG2E = 1.4426950408889634
LIMIT_MIB = 10
F32 = jnp.float32
BF16 = jnp.bfloat16


def minmod(lower, upper):
    return jnp.maximum(
        jnp.minimum(lower, upper), jnp.minimum(jnp.maximum(lower, upper), 0.0)
    )


def lanes_of(chunk):
    return pl.ds(pl.multiple_of(chunk * LANES, LANES), LANES)


def coefs_of(coef_ref, lanes):
    return [coef_ref[k, :, lanes] for k in range(9)]


def x_row(cells, rows, store, coef):
    reach, lean, ahead = coef[0], coef[1], coef[2] > 0.0
    first, last = rows[0], rows[-1]
    steps = {n: cells[n + 1] - cells[n] for n in range(first - 2, last + 2)}
    faces = {
        n: cells[n] + lean * minmod(steps[n - 1], steps[n])
        for n in range(first - 1, last + 2)
    }
    for n in rows:
        source = jnp.where(ahead, faces[n - 1], faces[n + 1])
        store(n, cells[n] - reach * (faces[n] - source))


def yz_row(source, out, row, lanes, coef, ring, face_ring):
    reach_y, lean_y, ahead_y = coef[3], coef[4], coef[5] > 0.0
    reach_z, lean_z, ahead_z = coef[6], coef[7], coef[8] > 0.0
    count = 16
    cells, steps, faces, z_faces = {}, {}, {}, {}

    def cell(y, t):
        y %= count
        if (y, t) not in cells:
            cells[y, t] = source[row, y, t, :, lanes]
        return cells[y, t]

    def step(y, t):
        y %= count
        if (y, t) not in steps:
            steps[y, t] = cell(y + 1, t) - cell(y, t)
        return steps[y, t]

    def face(y, t):
        y %= count
        if (y, t) not in faces:
            faces[y, t] = cell(y, t) + lean_y * minmod(step(y - 1, t), step(y, t))
        return faces[y, t]

    def lay(y):
        for t in range(2):
            ring[y, 8 + 8 * t : 16 + 8 * t, :] = cell(y, t)
        ring[y, 7:8, :] = source[row, y, 1, 7:8, lanes]
        ring[y, 24:25, :] = source[row, y, 0, 0:1, lanes]

    def lay_faces(y):
        for t in range(2):
            below = ring[y, 7 + 8 * t : 15 + 8 * t, :]
            above = ring[y, 9 + 8 * t : 17 + 8 * t, :]
            here = cell(y, t)
            z_faces[y, t] = here + lean_z * minmod(here - below, above - here)
            face_ring[y, 8 + 8 * t : 16 + 8 * t, :] = z_faces[y, t]
        face_ring[y, 7:8, :] = face_ring[y, 23:24, :]
        face_ring[y, 24:25, :] = face_ring[y, 8:9, :]

    def finish(y):
        for t in range(2):
            below = face_ring[y, 7 + 8 * t : 15 + 8 * t, :]
            above = face_ring[y, 9 + 8 * t : 17 + 8 * t, :]
            v = out[row, y, t, :, lanes]
            v -= reach_z * (z_faces[y, t] - jnp.where(ahead_z, below, above))
            upwind = jnp.where(ahead_y, face(y - 1, t), face(y + 1, t))
            v -= reach_y * (face(y, t) - upwind)
            out[row, y, t, :, lanes] = v

    for y in range(count + 2):
        if y < count:
            lay(y)
        if 0 <= y - 1 < count:
            lay_faces(y - 1)
        if 0 <= y - 2 < count:
            finish(y - 2)


def row_moments(block, weights):
    flat = block.reshape(256, LANES)
    high = flat.astype(BF16)
    rest = (flat - high.astype(F32)).astype(BF16)
    contract = (((1,), (1,)), ((), ()))
    total = lax.dot_general(weights, high, contract, preferred_element_type=F32)
    total += lax.dot_general(weights, rest, contract, preferred_element_type=F32)
    return total[:SUB]


def write_moments(out, place, value):
    for m in range(4):
        out[m, pl.ds(place, 1), :] = value[m : m + 1]
    out[4, pl.ds(place, 1), :] = value[4:5] + value[5:6]


def yz_rows(chunks, groups, coef_ref, weights, acc, ring, face_ring):
    for source, out, rows, place in groups:

        def one(i, carry, source=source, out=out, rows=rows, place=place):
            chunk, row = i // rows, i % rows
            lanes = lanes_of(chunk)
            yz_row(source, out, row, lanes, coefs_of(coef_ref, lanes), ring, face_ring)
            part = row_moments(out[row, :, :, :, lanes], weights[:, lanes])
            acc[place + row] = acc[place + row] + part
            return carry

        lax.fori_loop(0, chunks * rows, one, 0)


def three_parts(value):
    high = value.astype(BF16).astype(F32)
    rest = value - high
    middle = rest.astype(BF16).astype(F32)
    low = (rest - middle).astype(BF16).astype(F32)
    return high, middle, low


def spread_features(params, wide, tall, rows):
    alpha, beta_x, beta_y, beta_z, gamma, keep = params
    alpha = jnp.where(gamma == 0.0, -10000.0, alpha)
    zero = jnp.zeros_like(alpha)
    columns = []
    for value in (alpha, beta_x, beta_y, beta_z, gamma, gamma, keep):
        columns.extend(three_parts(value))
    columns.extend([zero] * (FEATURES - len(columns)))
    for k, value in enumerate(columns):
        for r in range(rows):
            wide[r, k : k + 1, :] = value[r : r + 1]
    for r in range(rows):
        tall[r] = wide[r].T.astype(BF16)


def relax_rows(source, out, tall, first, rows, table, factor, kept):
    width = source.shape[-1]

    def one(row, carry):
        features = tall[first + row]
        keep = jnp.dot(features, factor[...], preferred_element_type=F32)
        kept[...] = keep.reshape(16, 2, SUB, LANES)
        for pair in range(width // PAIR):
            power = jnp.dot(
                features, table[:, pair * PAIR : (pair + 1) * PAIR], preferred_element_type=F32
            )
            for half in range(2):
                lanes = pl.ds(pair * PAIR + half * LANES, LANES)
                shape = jnp.exp2(power[:, half * LANES : (half + 1) * LANES])
                shape = shape.reshape(16, 2, SUB, LANES)
                out[row, :, :, :, lanes] = kept[...] * source[row, :, :, :, lanes] + shape
        return carry

    lax.fori_loop(0, rows, one, 0)


def param_kernel(total, count, *refs):
    parts = refs[:count]
    codes, knudsen, inflow, out, out_low, out_high = refs[count:]
    sums = [parts[0][m] for m in range(5)]
    for part in parts[1:]:
        sums = [s + part[m] for m, s in enumerate(sums)]
    density = sums[0] * (1.0 / total)
    scale = UNIT / sums[0]
    u_x, u_y, u_z = (sums[m] * scale for m in (1, 2, 3))
    heat = (UNIT * sums[4] * scale - (u_x * u_x + u_y * u_y + u_z * u_z)) * (1.0 / 3.0)
    rate = 0.5 * density / (density + knudsen[0])
    code = codes[...]
    flowing, wall = code == 1, code == 2
    closed = flowing | wall
    u_x = jnp.where(flowing, inflow[1], jnp.where(wall, 0.0, u_x))
    u_y = jnp.where(closed, 0.0, u_y)
    u_z = jnp.where(closed, 0.0, u_z)
    heat = jnp.where(flowing, inflow[2], jnp.where(wall, inflow[3], heat))
    amount = jnp.where(flowing, inflow[0], jnp.where(wall, density, rate * density))
    keep = jnp.where(closed, 0.0, 1.0 - rate)
    g = (-0.5 * LOG2E) / heat

    def line(u, n, unit):
        s = None
        for i in range(n):
            gap = (i + 0.5 - n / 2) * unit - u
            e = jnp.exp2(g * (gap * gap))
            s = e if s is None else s + e
        return s

    norm = line(u_x, VGX, 6.0 / VGX) * line(u_y, VGY, 6.0 / VGY)
    norm = norm * line(u_z, VGZ, 6.0 / VGZ) * (1.0 / total)
    alpha = (jnp.log(amount) - jnp.log(norm)) * LOG2E
    alpha = alpha + g * (u_x * u_x + u_y * u_y + u_z * u_z)
    lean = (-2.0 * UNIT) * g
    params = (alpha, lean * u_x, lean * u_y, lean * u_z, g * (UNIT * UNIT), keep)
    rows = code.shape[0]
    for k, value in enumerate(params):
        out[k] = value
        out_low[k] = value[:2]
        out_high[k] = value[rows - 2 :]


def load_kernel(flags, state, cross, middle, inside, sems):
    rows = state.shape[0]
    copies = []
    for r in range(rows):
        place = jnp.where(flags[0] > 0, rows - 1 - r, r)
        if r < 2:
            target = cross.at[r]
        elif r < rows - 2:
            target = middle.at[r - 2]
        else:
            target = inside.at[r - rows + 2]
        copies.append(pltpu.make_async_copy(state.at[place], target, sems.at[r]))
    for copy in copies:
        copy.start()
    for copy in copies:
        copy.wait()


def inner_kernel(relax, rows, *refs):
    if relax:
        (m_cross, m_mid, m_in, params, table, factor, coef_ref, weights,
         cross, middle, inside, out, sums, wide, tall, kept, acc, ring, face_ring) = refs
        spread_features([params[k] for k in range(6)], wide, tall, rows)
        relax_rows(m_cross, cross, tall, 0, 2, table, factor, kept)
        relax_rows(m_mid, middle, tall, 2, rows - 4, table, factor, kept)
        relax_rows(m_in, inside, tall, rows - 2, 2, table, factor, kept)
    else:
        (cross, middle, inside, coef_ref, weights, out, sums, acc, ring, face_ring) = refs
    chunks = middle.shape[-1] // LANES
    inner = rows - 4
    acc[...] = jnp.zeros_like(acc)

    def along_x(i, carry):
        chunk, y = i // 16, i % 16
        lanes = lanes_of(chunk)
        coef = coefs_of(coef_ref, lanes)
        for t in range(2):
            cells = {}
            for n in range(rows):
                if n < 2:
                    cells[n] = cross[n, y, t, :, lanes]
                elif n < rows - 2:
                    cells[n] = middle[n - 2, y, t, :, lanes]
                else:
                    cells[n] = inside[n - rows + 2, y, t, :, lanes]

            def store(n, v, t=t):
                out[n - 2, y, t, :, lanes] = v

            x_row(cells, list(range(2, rows - 2)), store, coef)
        return carry

    lax.fori_loop(0, chunks * 16, along_x, 0, unroll=2)
    yz_rows(chunks, [(middle, out, inner, 0)], coef_ref, weights, acc, ring, face_ring)
    for r in range(inner):
        write_moments(sums, r, acc[r])


def edge_kernel(relax, rows, *refs):
    if relax:
        (flags, h_cross, h_in, p_cross, p_in, table, factor, cross, middle, inside, coef_ref,
         weights, inner_sums, out_cross, out_in, sums,
         wide, tall, kept, low, high, acc, ring, face_ring) = refs
        spread_features([p_cross[k] for k in range(6)], wide, tall, 2)
        relax_rows(h_cross, low, tall, 0, 2, table, factor, kept)
        spread_features([p_in[k] for k in range(6)], wide, tall, 2)
        relax_rows(h_in, high, tall, 0, 2, table, factor, kept)
    else:
        (flags, low, high, cross, middle, inside, coef_ref, weights, inner_sums,
         out_cross, out_in, sums, acc, ring, face_ring) = refs
    chunks = middle.shape[-1] // LANES
    acc[...] = jnp.zeros_like(acc)
    present = jnp.where(flags[1] > 0, 1.0, 0.0)

    def along_x(i, carry):
        chunk, y = i // 16, i % 16
        lanes = lanes_of(chunk)
        coef = coefs_of(coef_ref, lanes)
        for t in range(2):
            cells = {}
            for n in range(2):
                cells[-1 - n] = low[n, y, t, :, lanes] * present
                cells[n] = cross[n, y, t, :, lanes]
                cells[2 + n] = middle[n, y, t, :, lanes]

            def store(n, v, t=t):
                out_cross[n, y, t, :, lanes] = v

            x_row(cells, [0, 1], store, coef)
            cells = {}
            for n in range(2):
                cells[rows - 4 + n] = middle[rows - 6 + n, y, t, :, lanes]
                cells[rows - 2 + n] = inside[n, y, t, :, lanes]
                cells[rows + n] = high[1 - n, y, t, :, lanes]

            def store_in(n, v, t=t):
                out_in[n - rows + 2, y, t, :, lanes] = v

            x_row(cells, [rows - 2, rows - 1], store_in, coef)
        return carry

    lax.fori_loop(0, chunks * 16, along_x, 0)
    groups = [(cross, out_cross, 2, 0), (inside, out_in, 2, 2)]
    yz_rows(chunks, groups, coef_ref, weights, acc, ring, face_ring)
    for m in range(5):
        sums[m, 2 : rows - 2, :] = inner_sums[m]
    for r in range(2):
        write_moments(sums, r, acc[r])
        write_moments(sums, rows - 2 + r, acc[2 + r])


def final_kernel(rows, flags, m_cross, m_mid, m_in, params, table, factor, out,
                 wide, tall, kept, cross, middle, inside, sems):
    spread_features([params[k] for k in range(6)], wide, tall, rows)
    copies = []
    for source, target, first, count in (
        (m_cross, cross, 0, 2), (m_mid, middle, 2, rows - 4), (m_in, inside, rows - 2, 2)
    ):
        relax_rows(source, target, tall, first, count, table, factor, kept)
        for n in range(count):
            r = first + n
            place = jnp.where(flags[0] > 0, rows - 1 - r, r)
            copy = pltpu.make_async_copy(target.at[n], out.at[place], sems.at[r])
            copy.start()
            copies.append(copy)
    for copy in copies:
        copy.wait()


def body(distribution, velocity_order, cell_codes, knudsen, inflow):
    rows, count_y, count_z, width = distribution.shape
    peers = lax.axis_size("vert")
    line = lax.axis_size("gx")
    total = width * peers
    cells = count_y * count_z
    state = distribution.reshape(rows, count_y, 2, SUB, width)

    place = lax.axis_index("gx")
    mirrored = place % 2
    present = jnp.where((place == 0) | (place == line - 1), 0, 1)
    flags = jnp.stack([mirrored, present]).astype(jnp.int32)
    codes = cell_codes.reshape(rows, cells)
    codes = jnp.where(mirrored > 0, codes[::-1], codes)

    plane = VGY * VGZ
    n_x = 2 * (velocity_order // plane) - (VGX - 1)
    n_y = 2 * (velocity_order // VGZ % VGY) - (VGY - 1)
    n_z = 2 * (2 * (velocity_order % VGZ) - (VGZ - 1))
    square = n_x * n_x + n_y * n_y + n_z * n_z
    ones = jnp.ones_like(n_x)
    low_part = square % 8
    whole = jnp.stack([ones, n_x, n_y, n_z, square - low_part, low_part]).astype(F32)
    weights = jnp.pad(whole, ((0, 10), (0, 0))).astype(BF16)
    table = jnp.repeat(whole, 3, axis=0)
    table = jnp.pad(table, ((0, FEATURES - 18), (0, 0))).astype(BF16)
    slot = lax.broadcasted_iota(jnp.int32, (FEATURES, LANES), 0)
    factor = jnp.where((slot >= 18) & (slot < 21), 1.0, 0.0).astype(BF16)
    coef = []
    for n, scale in ((jnp.where(mirrored > 0, -n_x, n_x), 0.1), (n_y, 1.0 / 30.0), (n_z, 1.0 / 30.0)):
        reach = jnp.abs(n.astype(F32) * UNIT * scale)
        sign = jnp.where(n > 0, 1.0, -1.0)
        coef.extend([reach, 0.5 * sign * (1.0 - reach), sign])
    coef = jnp.broadcast_to(jnp.stack(coef)[:, None, :], (9, SUB, width))

    vmem = pl.BlockSpec(memory_space=pltpu.VMEM)
    smem = pl.BlockSpec(memory_space=pltpu.SMEM)
    hbm = pl.BlockSpec(memory_space=pl.ANY)

    def slab(n):
        return jax.ShapeDtypeStruct((n, count_y, 2, SUB, width), F32)

    def slab_scratch(n):
        return pltpu.VMEM((n, count_y, 2, SUB, width), F32)

    def feature_scratch(n):
        return [
            pltpu.VMEM((n, FEATURES, cells), F32),
            pltpu.VMEM((n, cells, FEATURES), BF16),
            pltpu.VMEM((count_y, 2, SUB, LANES), F32),
        ]

    def ring_scratch(n):
        return [pltpu.VMEM((n, SUB, cells), F32)] + [pltpu.VMEM((count_y, 32, LANES), F32)] * 2

    def limits(mib):
        return pltpu.CompilerParams(vmem_limit_bytes=mib * 1024 * 1024)

    def load():
        return pl.pallas_call(
            load_kernel,
            in_specs=[smem, hbm],
            out_specs=[vmem] * 3,
            out_shape=[slab(2), slab(rows - 4), slab(2)],
            scratch_shapes=[pltpu.SemaphoreType.DMA((rows,))],
            compiler_params=limits(6),
            name="load_rows",
        )(flags, state)

    def inner(relax, state, params):
        out_shape = [slab(rows - 4), jax.ShapeDtypeStruct((5, rows - 4, cells), F32)]
        scratch = ring_scratch(rows - 4)
        if relax:
            out_shape = [slab(2), slab(rows - 4), slab(2)] + out_shape
            scratch = feature_scratch(rows) + scratch
            args = (*state, params, table, factor, coef, weights)
        else:
            args = (*state, coef, weights)
        return pl.pallas_call(
            functools.partial(inner_kernel, relax, rows),
            in_specs=[vmem] * len(args),
            out_specs=[vmem] * len(out_shape),
            out_shape=out_shape,
            scratch_shapes=scratch,
            compiler_params=limits(LIMIT_MIB),
            name="inner_relax" if relax else "inner_first",
        )(*args)

    def edge(relax, halos, params, state, sums):
        scratch = ring_scratch(4)
        if relax:
            scratch = feature_scratch(2) + [slab_scratch(2)] * 2 + scratch
            args = (*halos, *params, table, factor, *state, coef, weights, sums)
        else:
            args = (*halos, *state, coef, weights, sums)
        return pl.pallas_call(
            functools.partial(edge_kernel, relax, rows),
            in_specs=[smem] + [vmem] * len(args),
            out_specs=[vmem] * 3,
            out_shape=[slab(2), slab(2), jax.ShapeDtypeStruct((5, rows, cells), F32)],
            scratch_shapes=scratch,
            compiler_params=limits(LIMIT_MIB),
            name="edge_relax" if relax else "edge_first",
        )(flags, *args)

    def cell_params(parts):
        return pl.pallas_call(
            functools.partial(param_kernel, total, len(parts)),
            in_specs=[vmem] * (len(parts) + 1) + [smem, smem],
            out_specs=[vmem] * 3,
            out_shape=[jax.ShapeDtypeStruct((6, n, cells), F32) for n in (rows, 2, 2)],
            compiler_params=limits(4),
            name="cell_params",
        )(*parts, codes, knudsen, inflow)

    def final(moved, params):
        return pl.pallas_call(
            functools.partial(final_kernel, rows),
            in_specs=[smem] + [vmem] * 6,
            out_specs=hbm,
            out_shape=slab(rows),
            scratch_shapes=feature_scratch(rows)
            + [slab_scratch(2), slab_scratch(rows - 4), slab_scratch(2)]
            + [pltpu.SemaphoreType.DMA((rows,))],
            compiler_params=limits(LIMIT_MIB),
            name="final_relax",
        )(flags, *moved, params, table, factor)

    across = [(0, 0), (line - 1, line - 1)]
    for i in range(1, line - 1, 2):
        across += [(i, i + 1), (i + 1, i)]
    within = []
    for i in range(0, line, 2):
        within += [(i, i + 1), (i + 1, i)]

    def exchange(cross, inside):
        return lax.ppermute(cross, "gx", across), lax.ppermute(inside, "gx", within)

    def gather(part):
        parts = [part]
        for shift in range(1, peers):
            pairs = [(i, (i + shift) % peers) for i in range(peers)]
            parts.append(lax.ppermute(part, "vert", pairs))
        return parts

    cross, middle, inside = load()
    halos = exchange(cross, inside)
    m_mid, sums = inner(False, (cross, middle, inside), None)
    m_cross, m_in, sums = edge(False, halos, None, (cross, middle, inside), sums)
    for _ in range(1, STEPS):
        halos = exchange(m_cross, m_in)
        params, p_cross, p_in = cell_params(gather(sums))
        p_halos = exchange(p_cross, p_in)
        moved = (m_cross, m_mid, m_in)
        cross, middle, inside, m_mid, sums = inner(True, moved, params)
        m_cross, m_in, sums = edge(True, halos, p_halos, (cross, middle, inside), sums)
    params, _, _ = cell_params(gather(sums))
    result = final((m_cross, m_mid, m_in), params)
    return result.reshape(rows, count_y, count_z, width)


def solution(mesh):
    placed = (
        P(("groups", "gx"), None, None, "vert"),
        P("vert"),
        P(("groups", "gx"), None, None),
        P("groups"),
        P("groups"),
    )
    return jax.shard_map(
        body,
        mesh=mesh,
        in_specs=placed,
        out_specs=P(("groups", "gx"), None, None, "vert"),
        check_vma=False,
    )
```

```python
import functools

import jax
import jax.numpy as jnp
from jax import lax
from jax.experimental import pallas as pl
from jax.experimental.pallas import tpu as pltpu
from jax.sharding import PartitionSpec as P

VGX = 16
VGY = 16
VGZ = 8
STEPS = 3
LANES = 128
SUB = 8
FEATURES = 32
PAIR = 2 * LANES
UNIT = 3.0 / 16.0
LOG2E = 1.4426950408889634
LIMIT_MIB = 10
F32 = jnp.float32
BF16 = jnp.bfloat16


def minmod(lower, upper):
    return jnp.maximum(
        jnp.minimum(lower, upper), jnp.minimum(jnp.maximum(lower, upper), 0.0)
    )


def lanes_of(chunk):
    return pl.ds(pl.multiple_of(chunk * LANES, LANES), LANES)


def coefs_of(coef_ref, lanes):
    return [coef_ref[k, :, lanes] for k in range(9)]


def x_row(cells, rows, store, coef, change=False):
    reach, lean, ahead = coef[0], coef[1], coef[2] > 0.0
    first, last = rows[0], rows[-1]
    steps = {n: cells[n + 1] - cells[n] for n in range(first - 2, last + 2)}
    faces = {
        n: cells[n] + lean * minmod(steps[n - 1], steps[n])
        for n in range(first - 1, last + 2)
    }
    for n in rows:
        source = jnp.where(ahead, faces[n - 1], faces[n + 1])
        v = reach * (faces[n] - source)
        store(n, v if change else cells[n] - v)


def yz_row(source, out, fresh, row, lanes, coef, ring, face_ring):
    reach_y, lean_y, ahead_y = coef[3], coef[4], coef[5] > 0.0
    reach_z, lean_z, ahead_z = coef[6], coef[7], coef[8] > 0.0
    count = 16
    cells, steps, faces, z_faces = {}, {}, {}, {}

    def cell(y, t):
        y %= count
        if (y, t) not in cells:
            cells[y, t] = source[row, y, t, :, lanes]
        return cells[y, t]

    def step(y, t):
        y %= count
        if (y, t) not in steps:
            steps[y, t] = cell(y + 1, t) - cell(y, t)
        return steps[y, t]

    def face(y, t):
        y %= count
        if (y, t) not in faces:
            faces[y, t] = cell(y, t) + lean_y * minmod(step(y - 1, t), step(y, t))
        return faces[y, t]

    def lay(y):
        for t in range(2):
            ring[y, 8 + 8 * t : 16 + 8 * t, :] = cell(y, t)
        ring[y, 7:8, :] = source[row, y, 1, 7:8, lanes]
        ring[y, 24:25, :] = source[row, y, 0, 0:1, lanes]

    def lay_faces(y):
        for t in range(2):
            below = ring[y, 7 + 8 * t : 15 + 8 * t, :]
            above = ring[y, 9 + 8 * t : 17 + 8 * t, :]
            here = cell(y, t)
            z_faces[y, t] = here + lean_z * minmod(here - below, above - here)
            face_ring[y, 8 + 8 * t : 16 + 8 * t, :] = z_faces[y, t]
        face_ring[y, 7:8, :] = face_ring[y, 23:24, :]
        face_ring[y, 24:25, :] = face_ring[y, 8:9, :]

    def finish(y):
        for t in range(2):
            below = face_ring[y, 7 + 8 * t : 15 + 8 * t, :]
            above = face_ring[y, 9 + 8 * t : 17 + 8 * t, :]
            v = cell(y, t) if fresh else out[row, y, t, :, lanes]
            v -= reach_z * (z_faces[y, t] - jnp.where(ahead_z, below, above))
            upwind = jnp.where(ahead_y, face(y - 1, t), face(y + 1, t))
            v -= reach_y * (face(y, t) - upwind)
            out[row, y, t, :, lanes] = v

    for y in range(count + 2):
        if y < count:
            lay(y)
        if 0 <= y - 1 < count:
            lay_faces(y - 1)
        if 0 <= y - 2 < count:
            finish(y - 2)


def row_moments(out, count, weights, sums, first):
    width = out.shape[-1]
    for r in range(count):
        flat = out[r].reshape(256, width)
        high = flat.astype(BF16)
        rest = (flat - high.astype(F32)).astype(BF16)
        both = jnp.concatenate([high, rest], axis=1)
        contract = (((1,), (1,)), ((), ()))
        part = lax.dot_general(weights[...], both, contract, preferred_element_type=F32)
        place = first + r
        for m in range(4):
            sums[m, place : place + 1, :] = part[m : m + 1]
        sums[4, place : place + 1, :] = part[4:5] + part[5:6]


def yz_rows(source, out, fresh, rows, coef_ref, ring, face_ring):
    chunks = source.shape[-1] // LANES

    def one(i, carry):
        chunk, row = i // rows, i % rows
        lanes = lanes_of(chunk)
        coef = coefs_of(coef_ref, lanes)
        yz_row(source, out, fresh, row, lanes, coef, ring, face_ring)
        return carry

    lax.fori_loop(0, chunks * rows, one, 0)


def three_parts(value):
    high = value.astype(BF16).astype(F32)
    rest = value - high
    middle = rest.astype(BF16).astype(F32)
    low = (rest - middle).astype(BF16).astype(F32)
    return high, middle, low


def spread_features(params, wide, tall, rows):
    alpha, beta_x, beta_y, beta_z, gamma, keep = params
    alpha = jnp.where(gamma == 0.0, -10000.0, alpha)
    zero = jnp.zeros_like(alpha)
    columns = []
    for value in (alpha, beta_x, beta_y, beta_z, gamma, gamma, keep):
        columns.extend(three_parts(value))
    columns.extend([zero] * (FEATURES - len(columns)))
    for k, value in enumerate(columns):
        for r in range(rows):
            wide[r, k : k + 1, :] = value[r : r + 1]
    for r in range(rows):
        tall[r] = wide[r].T.astype(BF16)


def relax_rows(source, out, tall, first, rows, table, factor, kept):
    width = source.shape[-1]

    def two(i, carry):
        for u in range(2):
            keep = jnp.dot(tall[first + 2 * i + u], factor[...], preferred_element_type=F32)
            kept[u] = keep.reshape(16, 2, SUB, LANES)
        for u in range(2):
            row = 2 * i + u
            for pair in range(width // PAIR):
                columns = table[:, pair * PAIR : (pair + 1) * PAIR]
                power = jnp.dot(tall[first + row], columns, preferred_element_type=F32)
                for half in range(2):
                    lanes = pl.ds(pair * PAIR + half * LANES, LANES)
                    shape = jnp.exp2(power[:, half * LANES : (half + 1) * LANES])
                    shape = shape.reshape(16, 2, SUB, LANES)
                    out[row, :, :, :, lanes] = kept[u] * source[row, :, :, :, lanes] + shape
        return carry

    lax.fori_loop(0, rows // 2, two, 0)


def param_kernel(total, count, *refs):
    parts = refs[:count]
    codes, knudsen, inflow, out, out_low, out_high = refs[count:]
    sums = [parts[0][m] for m in range(5)]
    for part in parts[1:]:
        sums = [s + part[m] for m, s in enumerate(sums)]
    density = sums[0] * (1.0 / total)
    scale = UNIT / sums[0]
    u_x, u_y, u_z = (sums[m] * scale for m in (1, 2, 3))
    heat = (UNIT * sums[4] * scale - (u_x * u_x + u_y * u_y + u_z * u_z)) * (1.0 / 3.0)
    rate = 0.5 * density / (density + knudsen[0])
    code = codes[...]
    flowing, wall = code == 1, code == 2
    closed = flowing | wall
    u_x = jnp.where(flowing, inflow[1], jnp.where(wall, 0.0, u_x))
    u_y = jnp.where(closed, 0.0, u_y)
    u_z = jnp.where(closed, 0.0, u_z)
    heat = jnp.where(flowing, inflow[2], jnp.where(wall, inflow[3], heat))
    amount = jnp.where(flowing, inflow[0], jnp.where(wall, density, rate * density))
    keep = jnp.where(closed, 0.0, 1.0 - rate)
    g = (-0.5 * LOG2E) / heat

    def line(u, n, unit):
        s = None
        for i in range(n):
            gap = (i + 0.5 - n / 2) * unit - u
            e = jnp.exp2(g * (gap * gap))
            s = e if s is None else s + e
        return s

    norm = line(u_x, VGX, 6.0 / VGX) * line(u_y, VGY, 6.0 / VGY)
    norm = norm * line(u_z, VGZ, 6.0 / VGZ) * (1.0 / total)
    alpha = (jnp.log(amount) - jnp.log(norm)) * LOG2E
    alpha = alpha + g * (u_x * u_x + u_y * u_y + u_z * u_z)
    lean = (-2.0 * UNIT) * g
    params = (alpha, lean * u_x, lean * u_y, lean * u_z, g * (UNIT * UNIT), keep)
    rows = code.shape[0]
    for k, value in enumerate(params):
        out[k] = value
        out_low[k] = value[:2]
        out_high[k] = value[rows - 2 :]


def load_kernel(flags, state, cross, middle, inside, sems):
    rows = state.shape[0]
    copies = []
    for r in range(rows):
        place = jnp.where(flags[0] > 0, rows - 1 - r, r)
        if r < 2:
            target = cross.at[r]
        elif r < rows - 2:
            target = middle.at[r - 2]
        else:
            target = inside.at[r - rows + 2]
        copies.append(pltpu.make_async_copy(state.at[place], target, sems.at[r]))
    for copy in copies:
        copy.start()
    for copy in copies:
        copy.wait()


def inner_kernel(relax, rows, *refs):
    if relax:
        (m_cross, m_mid, m_in, params, table, factor, coef_ref, weights,
         cross, middle, inside, out, e_cross, e_in, sums, wide, tall, kept, ring, face_ring) = refs
        spread_features([params[k] for k in range(6)], wide, tall, rows)
        relax_rows(m_cross, cross, tall, 0, 2, table, factor, kept)
        relax_rows(m_mid, middle, tall, 2, rows - 4, table, factor, kept)
        relax_rows(m_in, inside, tall, rows - 2, 2, table, factor, kept)
    else:
        (cross, middle, inside, coef_ref, weights, out, e_cross, e_in, sums, ring, face_ring) = refs
    chunks = middle.shape[-1] // LANES
    inner = rows - 4

    def along_x(i, carry):
        chunk, y = i // 16, i % 16
        lanes = lanes_of(chunk)
        coef = coefs_of(coef_ref, lanes)
        for t in range(2):
            cells = {}
            for n in range(rows):
                if n < 2:
                    cells[n] = cross[n, y, t, :, lanes]
                elif n < rows - 2:
                    cells[n] = middle[n - 2, y, t, :, lanes]
                else:
                    cells[n] = inside[n - rows + 2, y, t, :, lanes]

            def store(n, v, t=t):
                out[n - 2, y, t, :, lanes] = v

            x_row(cells, list(range(2, rows - 2)), store, coef)
        return carry

    lax.fori_loop(0, chunks * 16, along_x, 0, unroll=2)
    yz_rows(middle, out, False, inner, coef_ref, ring, face_ring)
    yz_rows(cross, e_cross, True, 2, coef_ref, ring, face_ring)
    yz_rows(inside, e_in, True, 2, coef_ref, ring, face_ring)
    row_moments(out, inner, weights, sums, 0)


def edge_kernel(relax, rows, *refs):
    if relax:
        (flags, h_cross, h_in, p_cross, p_in, table, factor, cross, middle, inside, e_cross,
         e_in, coef_ref, weights, inner_sums, out_cross, out_in, sums,
         wide, tall, kept, low, high) = refs
        spread_features([p_cross[k] for k in range(6)], wide, tall, 2)
        relax_rows(h_cross, low, tall, 0, 2, table, factor, kept)
        spread_features([p_in[k] for k in range(6)], wide, tall, 2)
        relax_rows(h_in, high, tall, 0, 2, table, factor, kept)
    else:
        (flags, low, high, cross, middle, inside, e_cross, e_in, coef_ref, weights,
         inner_sums, out_cross, out_in, sums) = refs
    chunks = middle.shape[-1] // LANES
    present = jnp.where(flags[1] > 0, 1.0, 0.0)

    def along_x(i, carry):
        chunk, y = i // 16, i % 16
        lanes = lanes_of(chunk)
        coef = coefs_of(coef_ref, lanes)
        for t in range(2):
            cells = {}
            for n in range(2):
                cells[-1 - n] = low[n, y, t, :, lanes] * present
                cells[n] = cross[n, y, t, :, lanes]
                cells[2 + n] = middle[n, y, t, :, lanes]

            def store(n, v, t=t):
                out_cross[n, y, t, :, lanes] = e_cross[n, y, t, :, lanes] - v

            x_row(cells, [0, 1], store, coef, True)
            cells = {}
            for n in range(2):
                cells[rows - 4 + n] = middle[rows - 6 + n, y, t, :, lanes]
                cells[rows - 2 + n] = inside[n, y, t, :, lanes]
                cells[rows + n] = high[1 - n, y, t, :, lanes]

            def store_in(n, v, t=t):
                r = n - rows + 2
                out_in[r, y, t, :, lanes] = e_in[r, y, t, :, lanes] - v

            x_row(cells, [rows - 2, rows - 1], store_in, coef, True)
        return carry

    lax.fori_loop(0, chunks * 16, along_x, 0, unroll=2)
    for m in range(5):
        sums[m, 2 : rows - 2, :] = inner_sums[m]
    row_moments(out_cross, 2, weights, sums, 0)
    row_moments(out_in, 2, weights, sums, rows - 2)


def final_kernel(rows, flags, m_cross, m_mid, m_in, params, table, factor, out,
                 wide, tall, kept, cross, middle, inside, sems):
    spread_features([params[k] for k in range(6)], wide, tall, rows)
    copies = []
    for source, target, first, count in (
        (m_cross, cross, 0, 2), (m_mid, middle, 2, rows - 4), (m_in, inside, rows - 2, 2)
    ):
        relax_rows(source, target, tall, first, count, table, factor, kept)
        for n in range(count):
            r = first + n
            place = jnp.where(flags[0] > 0, rows - 1 - r, r)
            copy = pltpu.make_async_copy(target.at[n], out.at[place], sems.at[r])
            copy.start()
            copies.append(copy)
    for copy in copies:
        copy.wait()


def body(distribution, velocity_order, cell_codes, knudsen, inflow):
    rows, count_y, count_z, width = distribution.shape
    peers = lax.axis_size("vert")
    line = lax.axis_size("gx")
    total = width * peers
    cells = count_y * count_z
    state = distribution.reshape(rows, count_y, 2, SUB, width)

    place = lax.axis_index("gx")
    mirrored = place % 2
    present = jnp.where((place == 0) | (place == line - 1), 0, 1)
    flags = jnp.stack([mirrored, present]).astype(jnp.int32)
    codes = cell_codes.reshape(rows, cells)
    codes = jnp.where(mirrored > 0, codes[::-1], codes)

    plane = VGY * VGZ
    n_x = 2 * (velocity_order // plane) - (VGX - 1)
    n_y = 2 * (velocity_order // VGZ % VGY) - (VGY - 1)
    n_z = 2 * (2 * (velocity_order % VGZ) - (VGZ - 1))
    square = n_x * n_x + n_y * n_y + n_z * n_z
    ones = jnp.ones_like(n_x)
    low_part = square % 8
    whole = jnp.stack([ones, n_x, n_y, n_z, square - low_part, low_part]).astype(F32)
    weights = jnp.pad(whole, ((0, 10), (0, 0))).astype(BF16)
    weights = jnp.concatenate([weights, weights], axis=1)
    table = jnp.repeat(whole, 3, axis=0)
    table = jnp.pad(table, ((0, FEATURES - 18), (0, 0))).astype(BF16)
    slot = lax.broadcasted_iota(jnp.int32, (FEATURES, LANES), 0)
    factor = jnp.where((slot >= 18) & (slot < 21), 1.0, 0.0).astype(BF16)
    coef = []
    for n, scale in ((jnp.where(mirrored > 0, -n_x, n_x), 0.1), (n_y, 1.0 / 30.0), (n_z, 1.0 / 30.0)):
        reach = jnp.abs(n.astype(F32) * UNIT * scale)
        sign = jnp.where(n > 0, 1.0, -1.0)
        coef.extend([reach, 0.5 * sign * (1.0 - reach), sign])
    coef = jnp.broadcast_to(jnp.stack(coef)[:, None, :], (9, SUB, width))

    vmem = pl.BlockSpec(memory_space=pltpu.VMEM)
    smem = pl.BlockSpec(memory_space=pltpu.SMEM)
    hbm = pl.BlockSpec(memory_space=pltpu.HBM)

    def slab(n):
        return jax.ShapeDtypeStruct((n, count_y, 2, SUB, width), F32)

    def slab_scratch(n):
        return pltpu.VMEM((n, count_y, 2, SUB, width), F32)

    def feature_scratch(n):
        return [
            pltpu.VMEM((n, FEATURES, cells), F32),
            pltpu.VMEM((n, cells, FEATURES), BF16),
            pltpu.VMEM((2, count_y, 2, SUB, LANES), F32),
        ]

    ring_scratch = [pltpu.VMEM((count_y, 32, LANES), F32)] * 2

    def limits(mib):
        return pltpu.CompilerParams(vmem_limit_bytes=mib * 1024 * 1024)

    def load():
        return pl.pallas_call(
            load_kernel,
            in_specs=[smem, hbm],
            out_specs=[vmem] * 3,
            out_shape=[slab(2), slab(rows - 4), slab(2)],
            scratch_shapes=[pltpu.SemaphoreType.DMA((rows,))],
            compiler_params=limits(6),
            name="load_rows",
        )(flags, pltpu.with_memory_space_constraint(state, pltpu.HBM))

    def inner(relax, state, params):
        sums = jax.ShapeDtypeStruct((5, rows - 4, cells), F32)
        out_shape = [slab(rows - 4), slab(2), slab(2), sums]
        scratch = ring_scratch
        if relax:
            out_shape = [slab(2), slab(rows - 4), slab(2)] + out_shape
            scratch = feature_scratch(rows) + scratch
            args = (*state, params, table, factor, coef, weights)
        else:
            args = (*state, coef, weights)
        return pl.pallas_call(
            functools.partial(inner_kernel, relax, rows),
            in_specs=[vmem] * len(args),
            out_specs=[vmem] * len(out_shape),
            out_shape=out_shape,
            scratch_shapes=scratch,
            compiler_params=limits(LIMIT_MIB),
            name="inner_relax" if relax else "inner_first",
        )(*args)

    def edge(relax, halos, params, state, edges, sums):
        scratch = []
        args = (*state, *edges, coef, weights, sums)
        if relax:
            scratch = feature_scratch(2) + [slab_scratch(2)] * 2
            args = (*params, table, factor, *args)
        args = (*halos, *args)
        return pl.pallas_call(
            functools.partial(edge_kernel, relax, rows),
            in_specs=[smem] + [vmem] * len(args),
            out_specs=[vmem] * 3,
            out_shape=[slab(2), slab(2), jax.ShapeDtypeStruct((5, rows, cells), F32)],
            scratch_shapes=scratch,
            compiler_params=limits(LIMIT_MIB),
            name="edge_relax" if relax else "edge_first",
        )(flags, *args)

    def cell_params(parts):
        return pl.pallas_call(
            functools.partial(param_kernel, total, len(parts)),
            in_specs=[vmem] * (len(parts) + 1) + [smem, smem],
            out_specs=[vmem] * 3,
            out_shape=[jax.ShapeDtypeStruct((6, n, cells), F32) for n in (rows, 2, 2)],
            compiler_params=limits(4),
            name="cell_params",
        )(*parts, codes, knudsen, inflow)

    def final(moved, params):
        return pl.pallas_call(
            functools.partial(final_kernel, rows),
            in_specs=[smem] + [vmem] * 6,
            out_specs=hbm,
            out_shape=slab(rows),
            scratch_shapes=feature_scratch(rows)
            + [slab_scratch(2), slab_scratch(rows - 4), slab_scratch(2)]
            + [pltpu.SemaphoreType.DMA((rows,))],
            compiler_params=limits(LIMIT_MIB),
            name="final_relax",
        )(flags, *moved, params, table, factor)

    parts = lax.axis_size("groups")
    across = []
    for p in range(parts):
        for i in (0, line - 1):
            other = p ^ 1 if (p ^ 1) < parts else p
            across.append((p * line + i, other * line + i))
        for i in range(1, line - 1, 2):
            across += [(p * line + i, p * line + i + 1), (p * line + i + 1, p * line + i)]
    within = []
    for i in range(0, line, 2):
        within += [(i, i + 1), (i + 1, i)]

    def exchange(cross, inside):
        return (
            lax.ppermute(cross, ("groups", "gx"), across),
            lax.ppermute(inside, "gx", within),
        )

    def gather(part):
        parts = [part]
        for shift in range(1, peers):
            pairs = [(i, (i + shift) % peers) for i in range(peers)]
            parts.append(lax.ppermute(part, "vert", pairs))
        return parts

    flags, codes, weights, table, factor, coef = lax.optimization_barrier(
        (flags, codes, weights, table, factor, coef)
    )
    cross, middle, inside = load()
    halos = exchange(cross, inside)
    m_mid, e_cross, e_in, sums = inner(False, (cross, middle, inside), None)
    m_cross, m_in, sums = edge(
        False, halos, None, (cross, middle, inside), (e_cross, e_in), sums
    )
    for _ in range(1, STEPS):
        halos = exchange(m_cross, m_in)
        params, p_cross, p_in = cell_params(gather(sums))
        p_halos = exchange(p_cross, p_in)
        moved = (m_cross, m_mid, m_in)
        *state, m_mid, e_cross, e_in, sums = inner(True, moved, params)
        m_cross, m_in, sums = edge(True, halos, p_halos, state, (e_cross, e_in), sums)
    params, _, _ = cell_params(gather(sums))
    result = final((m_cross, m_mid, m_in), params)
    return result.reshape(rows, count_y, count_z, width)


def solution(mesh):
    placed = (
        P(("groups", "gx"), None, None, "vert"),
        P("vert"),
        P(("groups", "gx"), None, None),
        P("groups"),
        P("groups"),
    )
    return jax.shard_map(
        body,
        mesh=mesh,
        in_specs=placed,
        out_specs=P(("groups", "gx"), None, None, "vert"),
        check_vma=False,
    )
```

```python
import functools

import jax
import jax.numpy as jnp
from jax import lax
from jax.experimental import pallas as pl
from jax.experimental.pallas import tpu as pltpu
from jax.sharding import PartitionSpec as P

VGX = 16
VGY = 16
VGZ = 8
STEPS = 3
LANES = 128
SUB = 8
FEATURES = 32
PAIR = 2 * LANES
UNIT = 3.0 / 16.0
LOG2E = 1.4426950408889634
LIMIT_MIB = 10
F32 = jnp.float32
BF16 = jnp.bfloat16


def minmod(lower, upper):
    return jnp.maximum(
        jnp.minimum(lower, upper), jnp.minimum(jnp.maximum(lower, upper), 0.0)
    )


def lanes_of(chunk):
    return pl.ds(pl.multiple_of(chunk * LANES, LANES), LANES)


def coefs_of(coef_ref, lanes):
    return [coef_ref[k, :, lanes] for k in range(9)]


def x_row(cells, rows, store, coef, change=False):
    reach, lean, ahead = coef[0], coef[1], coef[2] > 0.0
    first, last = rows[0], rows[-1]
    steps = {n: cells[n + 1] - cells[n] for n in range(first - 2, last + 2)}
    faces = {
        n: cells[n] + lean * minmod(steps[n - 1], steps[n])
        for n in range(first - 1, last + 2)
    }
    for n in rows:
        source = jnp.where(ahead, faces[n - 1], faces[n + 1])
        v = reach * (faces[n] - source)
        store(n, v if change else cells[n] - v)


def yz_row(source, out, fresh, row, lanes, coef, ring, face_ring):
    reach_y, lean_y, ahead_y = coef[3], coef[4], coef[5] > 0.0
    reach_z, lean_z, ahead_z = coef[6], coef[7], coef[8] > 0.0
    count = 16
    cells, steps, faces, z_faces = {}, {}, {}, {}

    def cell(y, t):
        y %= count
        if (y, t) not in cells:
            cells[y, t] = source[row, y, t, :, lanes]
        return cells[y, t]

    def step(y, t):
        y %= count
        if (y, t) not in steps:
            steps[y, t] = cell(y + 1, t) - cell(y, t)
        return steps[y, t]

    def face(y, t):
        y %= count
        if (y, t) not in faces:
            faces[y, t] = cell(y, t) + lean_y * minmod(step(y - 1, t), step(y, t))
        return faces[y, t]

    def lay(y):
        for t in range(2):
            ring[y, 8 + 8 * t : 16 + 8 * t, :] = cell(y, t)
        ring[y, 7:8, :] = source[row, y, 1, 7:8, lanes]
        ring[y, 24:25, :] = source[row, y, 0, 0:1, lanes]

    def lay_faces(y):
        for t in range(2):
            below = ring[y, 7 + 8 * t : 15 + 8 * t, :]
            above = ring[y, 9 + 8 * t : 17 + 8 * t, :]
            here = cell(y, t)
            z_faces[y, t] = here + lean_z * minmod(here - below, above - here)
            face_ring[y, 8 + 8 * t : 16 + 8 * t, :] = z_faces[y, t]
        face_ring[y, 7:8, :] = face_ring[y, 23:24, :]
        face_ring[y, 24:25, :] = face_ring[y, 8:9, :]

    def finish(y):
        for t in range(2):
            below = face_ring[y, 7 + 8 * t : 15 + 8 * t, :]
            above = face_ring[y, 9 + 8 * t : 17 + 8 * t, :]
            v = cell(y, t) if fresh else out[row, y, t, :, lanes]
            v -= reach_z * (z_faces[y, t] - jnp.where(ahead_z, below, above))
            upwind = jnp.where(ahead_y, face(y - 1, t), face(y + 1, t))
            v -= reach_y * (face(y, t) - upwind)
            out[row, y, t, :, lanes] = v

    for y in range(count + 2):
        if y < count:
            lay(y)
        if 0 <= y - 1 < count:
            lay_faces(y - 1)
        if 0 <= y - 2 < count:
            finish(y - 2)


def row_moments(out, count, weights, sums, first):
    width = out.shape[-1]
    for r in range(count):
        flat = out[r].reshape(256, width)
        high = flat.astype(BF16)
        rest = (flat - high.astype(F32)).astype(BF16)
        both = jnp.concatenate([high, rest], axis=1)
        contract = (((1,), (1,)), ((), ()))
        part = lax.dot_general(weights[...], both, contract, preferred_element_type=F32)
        place = first + r
        for m in range(4):
            sums[m, place : place + 1, :] = part[m : m + 1]
        sums[4, place : place + 1, :] = part[4:5] + part[5:6]


def yz_rows(source, out, fresh, rows, coef_ref, ring, face_ring):
    chunks = source.shape[-1] // LANES

    def one(i, carry):
        chunk, row = i // rows, i % rows
        lanes = lanes_of(chunk)
        coef = coefs_of(coef_ref, lanes)
        yz_row(source, out, fresh, row, lanes, coef, ring, face_ring)
        return carry

    lax.fori_loop(0, chunks * rows, one, 0)


def three_parts(value):
    high = value.astype(BF16).astype(F32)
    rest = value - high
    middle = rest.astype(BF16).astype(F32)
    low = (rest - middle).astype(BF16).astype(F32)
    return high, middle, low


def spread_features(params, wide, tall, rows):
    alpha, beta_x, beta_y, beta_z, gamma, keep = params
    alpha = jnp.where(gamma == 0.0, -10000.0, alpha)
    zero = jnp.zeros_like(alpha)
    columns = []
    for value in (alpha, beta_x, beta_y, beta_z, gamma, gamma, keep):
        columns.extend(three_parts(value))
    columns.extend([zero] * (FEATURES - len(columns)))
    for k, value in enumerate(columns):
        for r in range(rows):
            wide[r, k : k + 1, :] = value[r : r + 1]
    for r in range(rows):
        tall[r] = wide[r].T.astype(BF16)


def relax_rows(source, out, tall, first, rows, table, factor, kept):
    width = source.shape[-1]

    def two(i, carry):
        for u in range(2):
            keep = jnp.dot(tall[first + 2 * i + u], factor[...], preferred_element_type=F32)
            kept[u] = keep.reshape(16, 2, SUB, LANES)
        for u in range(2):
            row = 2 * i + u
            for pair in range(width // PAIR):
                columns = table[:, pair * PAIR : (pair + 1) * PAIR]
                power = jnp.dot(tall[first + row], columns, preferred_element_type=F32)
                for half in range(2):
                    lanes = pl.ds(pair * PAIR + half * LANES, LANES)
                    shape = jnp.exp2(power[:, half * LANES : (half + 1) * LANES])
                    shape = shape.reshape(16, 2, SUB, LANES)
                    out[row, :, :, :, lanes] = kept[u] * source[row, :, :, :, lanes] + shape
        return carry

    lax.fori_loop(0, rows // 2, two, 0)


def param_kernel(total, count, *refs):
    parts = refs[:count]
    codes, knudsen, inflow, out, *edges = refs[count:]
    sums = [parts[0][m] for m in range(5)]
    for part in parts[1:]:
        sums = [s + part[m] for m, s in enumerate(sums)]
    density = sums[0] * (1.0 / total)
    scale = UNIT / sums[0]
    u_x, u_y, u_z = (sums[m] * scale for m in (1, 2, 3))
    heat = (UNIT * sums[4] * scale - (u_x * u_x + u_y * u_y + u_z * u_z)) * (1.0 / 3.0)
    rate = 0.5 * density / (density + knudsen[0])
    code = codes[...]
    flowing, wall = code == 1, code == 2
    closed = flowing | wall
    u_x = jnp.where(flowing, inflow[1], jnp.where(wall, 0.0, u_x))
    u_y = jnp.where(closed, 0.0, u_y)
    u_z = jnp.where(closed, 0.0, u_z)
    heat = jnp.where(flowing, inflow[2], jnp.where(wall, inflow[3], heat))
    amount = jnp.where(flowing, inflow[0], jnp.where(wall, density, rate * density))
    keep = jnp.where(closed, 0.0, 1.0 - rate)
    g = (-0.5 * LOG2E) / heat

    def line(u, n, unit):
        s = None
        for i in range(n):
            gap = (i + 0.5 - n / 2) * unit - u
            e = jnp.exp2(g * (gap * gap))
            s = e if s is None else s + e
        return s

    norm = line(u_x, VGX, 6.0 / VGX) * line(u_y, VGY, 6.0 / VGY)
    norm = norm * line(u_z, VGZ, 6.0 / VGZ) * (1.0 / total)
    alpha = (jnp.log(amount) - jnp.log(norm)) * LOG2E
    alpha = alpha + g * (u_x * u_x + u_y * u_y + u_z * u_z)
    lean = (-2.0 * UNIT) * g
    params = (alpha, lean * u_x, lean * u_y, lean * u_z, g * (UNIT * UNIT), keep)
    rows = code.shape[0]
    for k, value in enumerate(params):
        out[k] = value
        if edges:
            edges[0][k] = value[:2]
            edges[1][k] = value[rows - 2 :]


def row_copies(mirrored, state, target, first, sems):
    rows = state.shape[0]
    copies = []
    for n in range(target.shape[0]):
        place = jnp.where(mirrored > 0, rows - 1 - first - n, first + n)
        copies.append(pltpu.make_async_copy(state.at[place], target.at[n], sems.at[n]))
    return copies


def load_kernel(order_in, codes_in, state, cross, inside, codes, table, factor, weights, coef,
                order, raw, flat, cross_sems, inside_sems, more_sems):
    rows, width = state.shape[0], order.shape[-1]
    mirrored = lax.axis_index("gx") % 2
    more = [
        pltpu.make_async_copy(order_in, order, more_sems.at[0]),
        pltpu.make_async_copy(codes_in, raw, more_sems.at[1]),
    ]
    copies = row_copies(mirrored, state, cross, 0, cross_sems)
    copies += row_copies(mirrored, state, inside, rows - 2, inside_sems)
    for copy in more + copies:
        copy.start()
    for copy in more:
        copy.wait()

    slots = jnp.broadcast_to(order[...], (SUB, width))
    n_x = 2 * (slots // (VGY * VGZ)) - (VGX - 1)
    n_y = 2 * (slots // VGZ % VGY) - (VGY - 1)
    n_z = 2 * (2 * (slots % VGZ) - (VGZ - 1))
    square = n_x * n_x + n_y * n_y + n_z * n_z
    low_part = square % 8
    whole = [n.astype(F32) for n in (n_x, n_y, n_z, square - low_part, low_part)]
    whole = [jnp.ones_like(whole[0])] + whole

    def pick(values, index):
        out = jnp.zeros_like(values[0])
        for k, value in enumerate(values):
            out = jnp.where(index == k, value, out)
        return out

    line = lax.broadcasted_iota(jnp.int32, (SUB, width), 0)
    moments = jnp.concatenate([pick(whole, line), jnp.zeros((SUB, width), F32)], axis=0)
    moments = moments.astype(BF16)
    weights[:, :width] = moments
    weights[:, width:] = moments
    table[...] = jnp.concatenate(
        [pick(whole, (line + SUB * g) // 3) for g in range(FEATURES // SUB)], axis=0
    ).astype(BF16)
    slot = lax.broadcasted_iota(jnp.int32, (FEATURES, LANES), 0)
    factor[...] = jnp.where((slot >= 18) & (slot < 21), 1.0, 0.0).astype(BF16)
    turn = jnp.where(mirrored > 0, -1.0, 1.0)
    for k, (n, scale) in enumerate(
        ((whole[1] * turn, 0.1), (whole[2], 1.0 / 30.0), (whole[3], 1.0 / 30.0))
    ):
        reach = jnp.abs(n * UNIT * scale)
        sign = jnp.where(n > 0.0, 1.0, -1.0)
        coef[3 * k] = reach
        coef[3 * k + 1] = 0.5 * sign * (1.0 - reach)
        coef[3 * k + 2] = sign

    for y in range(raw.shape[1]):
        flat[:, y * raw.shape[2] : (y + 1) * raw.shape[2]] = raw[:, y, :]
    for r in range(rows):
        place = jnp.where(mirrored > 0, rows - 1 - r, r)
        codes[r : r + 1, :] = flat[pl.ds(place, 1), :]
    for copy in copies:
        copy.wait()


def inner_kernel(relax, rows, *refs):
    if relax:
        (m_cross, m_mid, m_in, params, table, factor, coef_ref, weights,
         cross, middle, inside, out, e_cross, e_in, sums, wide, tall, kept, ring, face_ring) = refs
        spread_features([params[k] for k in range(6)], wide, tall, rows)
        relax_rows(m_cross, cross, tall, 0, 2, table, factor, kept)
        relax_rows(m_mid, middle, tall, 2, rows - 4, table, factor, kept)
        relax_rows(m_in, inside, tall, rows - 2, 2, table, factor, kept)
    else:
        (cross, inside, state, coef_ref, weights, middle, out, e_cross, e_in, sums,
         ring, face_ring, sems) = refs
        mirrored = lax.axis_index("gx") % 2
        copies = row_copies(mirrored, state, middle, 2, sems)
        for copy in copies:
            copy.start()
    yz_rows(cross, e_cross, True, 2, coef_ref, ring, face_ring)
    yz_rows(inside, e_in, True, 2, coef_ref, ring, face_ring)
    if not relax:
        for copy in copies:
            copy.wait()
    chunks = middle.shape[-1] // LANES
    inner = rows - 4

    def along_x(i, carry):
        chunk, y = i // 16, i % 16
        lanes = lanes_of(chunk)
        coef = coefs_of(coef_ref, lanes)
        for t in range(2):
            cells = {}
            for n in range(rows):
                if n < 2:
                    cells[n] = cross[n, y, t, :, lanes]
                elif n < rows - 2:
                    cells[n] = middle[n - 2, y, t, :, lanes]
                else:
                    cells[n] = inside[n - rows + 2, y, t, :, lanes]

            def store(n, v, t=t):
                out[n - 2, y, t, :, lanes] = v

            x_row(cells, list(range(2, rows - 2)), store, coef)
        return carry

    lax.fori_loop(0, chunks * 16, along_x, 0, unroll=2)
    yz_rows(middle, out, False, inner, coef_ref, ring, face_ring)
    row_moments(out, inner, weights, sums, 0)


def edge_kernel(relax, rows, line, *refs):
    if relax:
        (h_cross, h_in, p_cross, p_in, table, factor, cross, middle, inside, e_cross,
         e_in, coef_ref, weights, inner_sums, out_cross, out_in, sums,
         wide, tall, kept, low, high) = refs
        spread_features([p_cross[k] for k in range(6)], wide, tall, 2)
        relax_rows(h_cross, low, tall, 0, 2, table, factor, kept)
        spread_features([p_in[k] for k in range(6)], wide, tall, 2)
        relax_rows(h_in, high, tall, 0, 2, table, factor, kept)
    else:
        (low, high, cross, middle, inside, e_cross, e_in, coef_ref, weights,
         inner_sums, out_cross, out_in, sums) = refs
    chunks = middle.shape[-1] // LANES
    place = lax.axis_index("gx")
    present = jnp.where((place == 0) | (place == line - 1), 0.0, 1.0)

    def along_x(i, carry):
        chunk, y = i // 16, i % 16
        lanes = lanes_of(chunk)
        coef = coefs_of(coef_ref, lanes)
        for t in range(2):
            cells = {}
            for n in range(2):
                cells[-1 - n] = low[n, y, t, :, lanes] * present
                cells[n] = cross[n, y, t, :, lanes]
                cells[2 + n] = middle[n, y, t, :, lanes]

            def store(n, v, t=t):
                out_cross[n, y, t, :, lanes] = e_cross[n, y, t, :, lanes] - v

            x_row(cells, [0, 1], store, coef, True)
            cells = {}
            for n in range(2):
                cells[rows - 4 + n] = middle[rows - 6 + n, y, t, :, lanes]
                cells[rows - 2 + n] = inside[n, y, t, :, lanes]
                cells[rows + n] = high[1 - n, y, t, :, lanes]

            def store_in(n, v, t=t):
                r = n - rows + 2
                out_in[r, y, t, :, lanes] = e_in[r, y, t, :, lanes] - v

            x_row(cells, [rows - 2, rows - 1], store_in, coef, True)
        return carry

    lax.fori_loop(0, chunks * 16, along_x, 0, unroll=2)
    for m in range(5):
        sums[m, 2 : rows - 2, :] = inner_sums[m]
    row_moments(out_cross, 2, weights, sums, 0)
    row_moments(out_in, 2, weights, sums, rows - 2)


def final_kernel(rows, m_cross, m_mid, m_in, params, table, factor, out,
                 wide, tall, kept, cross, middle, inside, sems):
    mirrored = lax.axis_index("gx") % 2
    spread_features([params[k] for k in range(6)], wide, tall, rows)
    copies = []
    for source, target, first, count in (
        (m_cross, cross, 0, 2), (m_mid, middle, 2, rows - 4), (m_in, inside, rows - 2, 2)
    ):
        relax_rows(source, target, tall, first, count, table, factor, kept)
        for n in range(count):
            r = first + n
            place = jnp.where(mirrored > 0, rows - 1 - r, r)
            copy = pltpu.make_async_copy(target.at[n], out.at[place], sems.at[r])
            copy.start()
            copies.append(copy)
    for copy in copies:
        copy.wait()


def body(distribution, velocity_order, cell_codes, knudsen, inflow):
    rows, count_y, count_z, width = distribution.shape
    peers = lax.axis_size("vert")
    line = lax.axis_size("gx")
    total = width * peers
    cells = count_y * count_z
    state = distribution.reshape(rows, count_y, 2, SUB, width)

    vmem = pl.BlockSpec(memory_space=pltpu.VMEM)
    smem = pl.BlockSpec(memory_space=pltpu.SMEM)
    hbm = pl.BlockSpec(memory_space=pltpu.HBM)

    def slab(n):
        return jax.ShapeDtypeStruct((n, count_y, 2, SUB, width), F32)

    def slab_scratch(n):
        return pltpu.VMEM((n, count_y, 2, SUB, width), F32)

    def feature_scratch(n):
        return [
            pltpu.VMEM((n, FEATURES, cells), F32),
            pltpu.VMEM((n, cells, FEATURES), BF16),
            pltpu.VMEM((2, count_y, 2, SUB, LANES), F32),
        ]

    ring_scratch = [pltpu.VMEM((count_y, 32, LANES), F32)] * 2

    def limits(mib):
        return pltpu.CompilerParams(vmem_limit_bytes=mib * 1024 * 1024)

    def in_hbm(array):
        return pltpu.with_memory_space_constraint(array, pltpu.HBM)

    def load():
        return pl.pallas_call(
            load_kernel,
            in_specs=[hbm] * 3,
            out_specs=[vmem] * 7,
            out_shape=[
                slab(2),
                slab(2),
                jax.ShapeDtypeStruct((rows, cells), jnp.int32),
                jax.ShapeDtypeStruct((FEATURES, width), BF16),
                jax.ShapeDtypeStruct((FEATURES, LANES), BF16),
                jax.ShapeDtypeStruct((16, 2 * width), BF16),
                jax.ShapeDtypeStruct((9, SUB, width), F32),
            ],
            scratch_shapes=[
                pltpu.VMEM((1, width), jnp.int32),
                pltpu.VMEM((rows, count_y, count_z), jnp.int32),
                pltpu.VMEM((rows, cells), jnp.int32),
                pltpu.SemaphoreType.DMA((2,)),
                pltpu.SemaphoreType.DMA((2,)),
                pltpu.SemaphoreType.DMA((2,)),
            ],
            compiler_params=limits(6),
            name="load_edges",
        )(in_hbm(velocity_order.reshape(1, width)), in_hbm(cell_codes), in_hbm(state))

    def inner(relax, state, params):
        sums = jax.ShapeDtypeStruct((5, rows - 4, cells), F32)
        out_shape = [slab(rows - 4), slab(2), slab(2), sums]
        scratch = ring_scratch
        if relax:
            out_shape = [slab(2), slab(rows - 4), slab(2)] + out_shape
            scratch = feature_scratch(rows) + scratch
            args = (*state, params, table, factor, coef, weights)
        else:
            out_shape = [slab(rows - 4)] + out_shape
            scratch = scratch + [pltpu.SemaphoreType.DMA((rows - 4,))]
            args = (*state, coef, weights)
        return pl.pallas_call(
            functools.partial(inner_kernel, relax, rows),
            in_specs=[vmem if relax or n != 2 else hbm for n in range(len(args))],
            out_specs=[vmem] * len(out_shape),
            out_shape=out_shape,
            scratch_shapes=scratch,
            compiler_params=limits(LIMIT_MIB),
            name="inner_relax" if relax else "inner_first",
        )(*args)

    def edge(relax, halos, params, state, edges, sums):
        scratch = []
        args = (*state, *edges, coef, weights, sums)
        if relax:
            scratch = feature_scratch(2) + [slab_scratch(2)] * 2
            args = (*params, table, factor, *args)
        args = (*halos, *args)
        return pl.pallas_call(
            functools.partial(edge_kernel, relax, rows, line),
            in_specs=[vmem] * len(args),
            out_specs=[vmem] * 3,
            out_shape=[slab(2), slab(2), jax.ShapeDtypeStruct((5, rows, cells), F32)],
            scratch_shapes=scratch,
            compiler_params=limits(LIMIT_MIB),
            name="edge_relax" if relax else "edge_first",
        )(*args)

    def cell_params(parts, *sizes):
        return pl.pallas_call(
            functools.partial(param_kernel, total, len(parts)),
            in_specs=[vmem] * (len(parts) + 1) + [smem, smem],
            out_specs=[vmem] * len(sizes),
            out_shape=[jax.ShapeDtypeStruct((6, n, cells), F32) for n in sizes],
            compiler_params=limits(4),
            name="cell_params",
        )(*parts, codes, knudsen, inflow)

    def final(moved, params):
        return pl.pallas_call(
            functools.partial(final_kernel, rows),
            in_specs=[vmem] * 6,
            out_specs=hbm,
            out_shape=slab(rows),
            scratch_shapes=feature_scratch(rows)
            + [slab_scratch(2), slab_scratch(rows - 4), slab_scratch(2)]
            + [pltpu.SemaphoreType.DMA((rows,))],
            compiler_params=limits(LIMIT_MIB),
            name="final_relax",
        )(*moved, params, table, factor)

    parts = lax.axis_size("groups")
    across = []
    for p in range(parts):
        for i in (0, line - 1):
            other = p ^ 1 if (p ^ 1) < parts else p
            across.append((p * line + i, other * line + i))
        for i in range(1, line - 1, 2):
            across += [(p * line + i, p * line + i + 1), (p * line + i + 1, p * line + i)]
    within = []
    for i in range(0, line, 2):
        within += [(i, i + 1), (i + 1, i)]

    def exchange(cross, inside):
        return (
            lax.ppermute(cross, ("groups", "gx"), across),
            lax.ppermute(inside, "gx", within),
        )

    def gather(part):
        parts = [part]
        for shift in range(1, peers):
            pairs = [(i, (i + shift) % peers) for i in range(peers)]
            parts.append(lax.ppermute(part, "vert", pairs))
        return parts

    cross, inside, codes, table, factor, weights, coef = load()
    halos = exchange(cross, inside)
    middle, m_mid, e_cross, e_in, sums = inner(False, (cross, inside, in_hbm(state)), None)
    m_cross, m_in, sums = edge(
        False, halos, None, (cross, middle, inside), (e_cross, e_in), sums
    )
    for _ in range(1, STEPS):
        halos = exchange(m_cross, m_in)
        params, p_cross, p_in = cell_params(gather(sums), rows, 2, 2)
        p_halos = exchange(p_cross, p_in)
        moved = (m_cross, m_mid, m_in)
        *state, m_mid, e_cross, e_in, sums = inner(True, moved, params)
        m_cross, m_in, sums = edge(True, halos, p_halos, state, (e_cross, e_in), sums)
    (params,) = cell_params(gather(sums), rows)
    result = final((m_cross, m_mid, m_in), params)
    return result.reshape(rows, count_y, count_z, width)


def solution(mesh):
    placed = (
        P(("groups", "gx"), None, None, "vert"),
        P("vert"),
        P(("groups", "gx"), None, None),
        P("groups"),
        P("groups"),
    )
    return jax.shard_map(
        body,
        mesh=mesh,
        in_specs=placed,
        out_specs=P(("groups", "gx"), None, None, "vert"),
        check_vma=False,
    )
```

```python
import functools

import jax
import jax.numpy as jnp
from jax import lax
from jax.experimental import pallas as pl
from jax.experimental.pallas import tpu as pltpu
from jax.sharding import PartitionSpec as P

VGX = 16
VGY = 16
VGZ = 8
STEPS = 3
LANES = 128
SUB = 8
FEATURES = 32
PAIR = 2 * LANES
UNIT = 3.0 / 16.0
LOG2E = 1.4426950408889634
LIMIT_MIB = 10
F32 = jnp.float32
BF16 = jnp.bfloat16


def minmod(lower, upper):
    return jnp.maximum(
        jnp.minimum(lower, upper), jnp.minimum(jnp.maximum(lower, upper), 0.0)
    )


def lanes_of(chunk):
    return pl.ds(pl.multiple_of(chunk * LANES, LANES), LANES)


def coefs_of(coef_ref, lanes):
    return [coef_ref[k, :, lanes] for k in range(9)]


def x_row(cells, rows, store, coef, change=False):
    reach, lean, ahead = coef[0], coef[1], coef[2] > 0.0
    first, last = rows[0], rows[-1]
    steps = {n: cells[n + 1] - cells[n] for n in range(first - 2, last + 2)}
    faces = {
        n: cells[n] + lean * minmod(steps[n - 1], steps[n])
        for n in range(first - 1, last + 2)
    }
    for n in rows:
        source = jnp.where(ahead, faces[n - 1], faces[n + 1])
        v = reach * (faces[n] - source)
        store(n, v if change else cells[n] - v)


def yz_row(source, out, fresh, row, lanes, coef):
    reach_y, lean_y, ahead_y = coef[3], coef[4], coef[5] > 0.0
    reach_z, lean_z, ahead_z = coef[6], coef[7], coef[8] > 0.0
    count = 16
    cells, steps, faces = {}, {}, {}

    def cell(y, t):
        y %= count
        if (y, t) not in cells:
            cells[y, t] = source[row, y, t, :, lanes]
        return cells[y, t]

    def step(y, t):
        y %= count
        if (y, t) not in steps:
            steps[y, t] = cell(y + 1, t) - cell(y, t)
        return steps[y, t]

    def face(y, t):
        y %= count
        if (y, t) not in faces:
            faces[y, t] = cell(y, t) + lean_y * minmod(step(y - 1, t), step(y, t))
        return faces[y, t]

    def up(v):
        return pltpu.roll(v, SUB - 1, 0)

    def down(v):
        return pltpu.roll(v, 1, 0)

    for y in range(count):
        even, odd = cell(y, 0), cell(y, 1)
        step_even = odd - even
        step_odd = up(even) - odd
        face_even = even + lean_z * minmod(down(step_odd), step_even)
        face_odd = odd + lean_z * minmod(step_even, step_odd)
        winds = (
            jnp.where(ahead_z, down(face_odd), face_odd),
            jnp.where(ahead_z, face_even, up(face_even)),
        )
        for t, z_face in enumerate((face_even, face_odd)):
            v = cell(y, t) if fresh else out[row, y, t, :, lanes]
            v -= reach_z * (z_face - winds[t])
            upwind = jnp.where(ahead_y, face(y - 1, t), face(y + 1, t))
            v -= reach_y * (face(y, t) - upwind)
            out[row, y, t, :, lanes] = v


def yz_rows(source, out, fresh, rows, coef_ref):
    chunks = source.shape[-1] // LANES

    def one(i, carry):
        chunk, row = i // rows, i % rows
        lanes = lanes_of(chunk)
        yz_row(source, out, fresh, row, lanes, coefs_of(coef_ref, lanes))
        return carry

    lax.fori_loop(0, chunks * rows, one, 0, unroll=2)


def row_moments(out, count, weights, sums, first):
    width = out.shape[-1]
    for r in range(count):
        flat = out[r].reshape(256, width)
        high = flat.astype(BF16)
        rest = (flat - high.astype(F32)).astype(BF16)
        both = jnp.concatenate([high, rest], axis=1)
        contract = (((1,), (1,)), ((), ()))
        part = lax.dot_general(weights[...], both, contract, preferred_element_type=F32)
        place = first + r
        for m in range(4):
            sums[m, place : place + 1, :] = part[m : m + 1]
        sums[4, place : place + 1, :] = part[4:5] + part[5:6]


def three_parts(value):
    high = value.astype(BF16).astype(F32)
    rest = value - high
    middle = rest.astype(BF16).astype(F32)
    low = (rest - middle).astype(BF16).astype(F32)
    return high, middle, low


def spread_features(params, wide, tall, rows):
    alpha, beta_x, beta_y, beta_z, gamma, keep = params
    alpha = jnp.where(gamma == 0.0, -10000.0, alpha)
    zero = jnp.zeros_like(alpha)
    columns = []
    for value in (alpha, beta_x, beta_y, beta_z, gamma, gamma, keep):
        columns.extend(three_parts(value))
    columns.extend([zero] * (FEATURES - len(columns)))
    for k, value in enumerate(columns):
        for r in range(rows):
            wide[r, k : k + 1, :] = value[r : r + 1]
    for r in range(rows):
        tall[r] = wide[r].T.astype(BF16)


def relax_rows(source, out, tall, first, rows, table, factor, kept):
    width = source.shape[-1]

    def two(i, carry):
        for u in range(2):
            keep = jnp.dot(tall[first + 2 * i + u], factor[...], preferred_element_type=F32)
            kept[u] = keep.reshape(16, 2, SUB, LANES)
        for u in range(2):
            row = 2 * i + u
            for pair in range(width // PAIR):
                columns = table[:, pair * PAIR : (pair + 1) * PAIR]
                power = jnp.dot(tall[first + row], columns, preferred_element_type=F32)
                for half in range(2):
                    lanes = pl.ds(pair * PAIR + half * LANES, LANES)
                    shape = jnp.exp2(power[:, half * LANES : (half + 1) * LANES])
                    shape = shape.reshape(16, 2, SUB, LANES)
                    value = kept[u] * source[row, :, :, :, lanes] + shape
                    if callable(out):
                        out(row, 2 * pair + half, value)
                    else:
                        out[row, :, :, :, lanes] = value
        return carry

    lax.fori_loop(0, rows // 2, two, 0)


def param_kernel(total, count, *refs):
    parts = refs[:count]
    codes, knudsen, inflow, out, *edges = refs[count:]
    sums = [parts[0][m] for m in range(5)]
    for part in parts[1:]:
        sums = [s + part[m] for m, s in enumerate(sums)]
    density = sums[0] * (1.0 / total)
    scale = UNIT / sums[0]
    u_x, u_y, u_z = (sums[m] * scale for m in (1, 2, 3))
    heat = (UNIT * sums[4] * scale - (u_x * u_x + u_y * u_y + u_z * u_z)) * (1.0 / 3.0)
    rate = 0.5 * density / (density + knudsen[0])
    code = codes[...]
    flowing, wall = code == 1, code == 2
    closed = flowing | wall
    u_x = jnp.where(flowing, inflow[1], jnp.where(wall, 0.0, u_x))
    u_y = jnp.where(closed, 0.0, u_y)
    u_z = jnp.where(closed, 0.0, u_z)
    heat = jnp.where(flowing, inflow[2], jnp.where(wall, inflow[3], heat))
    amount = jnp.where(flowing, inflow[0], jnp.where(wall, density, rate * density))
    keep = jnp.where(closed, 0.0, 1.0 - rate)
    g = (-0.5 * LOG2E) / heat

    def line(u, n, unit):
        s = None
        for i in range(n):
            gap = (i + 0.5 - n / 2) * unit - u
            e = jnp.exp2(g * (gap * gap))
            s = e if s is None else s + e
        return s

    norm = line(u_x, VGX, 6.0 / VGX) * line(u_y, VGY, 6.0 / VGY)
    norm = norm * line(u_z, VGZ, 6.0 / VGZ) * (1.0 / total)
    alpha = (jnp.log(amount) - jnp.log(norm)) * LOG2E
    alpha = alpha + g * (u_x * u_x + u_y * u_y + u_z * u_z)
    lean = (-2.0 * UNIT) * g
    params = (alpha, lean * u_x, lean * u_y, lean * u_z, g * (UNIT * UNIT), keep)
    rows = code.shape[0]
    for k, value in enumerate(params):
        out[k] = value
        if edges:
            edges[0][k] = value[:2]
            edges[1][k] = value[rows - 2 :]


def row_copies(mirrored, whole, staged, first, sems, out=False):
    rows = whole.shape[0]
    copies = []
    for n in range(staged.shape[0]):
        place = jnp.where(mirrored > 0, rows - 1 - first - n, first + n)
        for c in range(staged.shape[2]):
            far = whole.at[place, :, :, pl.ds(c * LANES, LANES)]
            near = staged.at[n, :, c]
            pair = (near, far) if out else (far, near)
            copies.append(pltpu.make_async_copy(*pair, sems.at[n, c]))
    return copies


def unstage(staged, out):
    count = staged.shape[1]

    def one(i, carry):
        n, y = i // count, i % count
        for c in range(staged.shape[2]):
            for t in range(2):
                v = staged[n, y, c, pl.ds(t, SUB, stride=2), :]
                out[n, y, t, :, pl.ds(c * LANES, LANES)] = v
        return carry

    lax.fori_loop(0, staged.shape[0] * count, one, 0, unroll=4)


def load_kernel(order_in, codes_in, state, cross, inside, codes, table, factor, weights, coef,
                order, raw, flat, near_cross, near_inside, cross_sems, inside_sems, more_sems):
    rows, width = state.shape[0], order.shape[-1]
    mirrored = lax.axis_index("gx") % 2
    more = [
        pltpu.make_async_copy(order_in, order, more_sems.at[0]),
        pltpu.make_async_copy(codes_in, raw, more_sems.at[1]),
    ]
    copies = row_copies(mirrored, state, near_cross, 0, cross_sems)
    copies += row_copies(mirrored, state, near_inside, rows - 2, inside_sems)
    for copy in more + copies:
        copy.start()
    for copy in more:
        copy.wait()

    slots = jnp.broadcast_to(order[...], (SUB, width))
    n_x = 2 * (slots // (VGY * VGZ)) - (VGX - 1)
    n_y = 2 * (slots // VGZ % VGY) - (VGY - 1)
    n_z = 2 * (2 * (slots % VGZ) - (VGZ - 1))
    square = n_x * n_x + n_y * n_y + n_z * n_z
    low_part = square % 8
    whole = [n.astype(F32) for n in (n_x, n_y, n_z, square - low_part, low_part)]
    whole = [jnp.ones_like(whole[0])] + whole

    def pick(values, index):
        out = jnp.zeros_like(values[0])
        for k, value in enumerate(values):
            out = jnp.where(index == k, value, out)
        return out

    line = lax.broadcasted_iota(jnp.int32, (SUB, width), 0)
    moments = jnp.concatenate([pick(whole, line), jnp.zeros((SUB, width), F32)], axis=0)
    moments = moments.astype(BF16)
    weights[:, :width] = moments
    weights[:, width:] = moments
    table[...] = jnp.concatenate(
        [pick(whole, (line + SUB * g) // 3) for g in range(FEATURES // SUB)], axis=0
    ).astype(BF16)
    slot = lax.broadcasted_iota(jnp.int32, (FEATURES, LANES), 0)
    factor[...] = jnp.where((slot >= 18) & (slot < 21), 1.0, 0.0).astype(BF16)
    turn = jnp.where(mirrored > 0, -1.0, 1.0)
    for k, (n, scale) in enumerate(
        ((whole[1] * turn, 0.1), (whole[2], 1.0 / 30.0), (whole[3], 1.0 / 30.0))
    ):
        reach = jnp.abs(n * UNIT * scale)
        sign = jnp.where(n > 0.0, 1.0, -1.0)
        coef[3 * k] = reach
        coef[3 * k + 1] = 0.5 * sign * (1.0 - reach)
        coef[3 * k + 2] = sign

    span = raw.shape[2]
    z = lax.broadcasted_iota(jnp.int32, (span, span), 0)
    goes = lax.broadcasted_iota(jnp.int32, (span, span), 1)
    shuffle = jnp.where(goes == z % 2 * SUB + z // 2, 1.0, 0.0).astype(BF16)
    lined = raw[...].reshape(rows * raw.shape[1], span).astype(F32).astype(BF16)
    lined = jnp.dot(lined, shuffle, preferred_element_type=F32).astype(jnp.int32)
    raw[...] = lined.reshape(rows, raw.shape[1], span)
    for y in range(raw.shape[1]):
        flat[:, y * span : (y + 1) * span] = raw[:, y, :]
    for r in range(rows):
        place = jnp.where(mirrored > 0, rows - 1 - r, r)
        codes[r : r + 1, :] = flat[pl.ds(place, 1), :]
    for copy in copies:
        copy.wait()
    unstage(near_cross, cross)
    unstage(near_inside, inside)


def inner_kernel(relax, rows, *refs):
    if relax:
        (m_cross, m_mid, m_in, params, table, factor, coef_ref, weights,
         cross, middle, inside, out, e_cross, e_in, sums, wide, tall, kept) = refs
        spread_features([params[k] for k in range(6)], wide, tall, rows)
        relax_rows(m_cross, cross, tall, 0, 2, table, factor, kept)
        relax_rows(m_mid, middle, tall, 2, rows - 4, table, factor, kept)
        relax_rows(m_in, inside, tall, rows - 2, 2, table, factor, kept)
    else:
        (cross, inside, state, coef_ref, weights, middle, out, e_cross, e_in, sums,
         near, sems) = refs
        mirrored = lax.axis_index("gx") % 2
        copies = row_copies(mirrored, state, near, 2, sems)
        for copy in copies:
            copy.start()
    yz_rows(cross, e_cross, True, 2, coef_ref)
    yz_rows(inside, e_in, True, 2, coef_ref)
    if not relax:
        for copy in copies:
            copy.wait()
        unstage(near, middle)
    chunks = middle.shape[-1] // LANES
    inner = rows - 4

    def along_x(i, carry):
        chunk, y = i // 16, i % 16
        lanes = lanes_of(chunk)
        coef = coefs_of(coef_ref, lanes)
        for t in range(2):
            cells = {}
            for n in range(rows):
                if n < 2:
                    cells[n] = cross[n, y, t, :, lanes]
                elif n < rows - 2:
                    cells[n] = middle[n - 2, y, t, :, lanes]
                else:
                    cells[n] = inside[n - rows + 2, y, t, :, lanes]

            def store(n, v, t=t):
                out[n - 2, y, t, :, lanes] = v

            x_row(cells, list(range(2, rows - 2)), store, coef)
        return carry

    lax.fori_loop(0, chunks * 16, along_x, 0, unroll=2)
    yz_rows(middle, out, False, inner, coef_ref)
    row_moments(out, inner, weights, sums, 0)


def edge_kernel(relax, rows, line, *refs):
    if relax:
        (h_cross, h_in, p_cross, p_in, table, factor, cross, middle, inside, e_cross,
         e_in, coef_ref, weights, inner_sums, out_cross, out_in, sums,
         wide, tall, kept, low, high) = refs
        spread_features([p_cross[k] for k in range(6)], wide, tall, 2)
        relax_rows(h_cross, low, tall, 0, 2, table, factor, kept)
        spread_features([p_in[k] for k in range(6)], wide, tall, 2)
        relax_rows(h_in, high, tall, 0, 2, table, factor, kept)
    else:
        (low, high, cross, middle, inside, e_cross, e_in, coef_ref, weights,
         inner_sums, out_cross, out_in, sums) = refs
    chunks = middle.shape[-1] // LANES
    place = lax.axis_index("gx")
    present = jnp.where((place == 0) | (place == line - 1), 0.0, 1.0)

    def along_x(i, carry):
        chunk, y = i // 16, i % 16
        lanes = lanes_of(chunk)
        coef = coefs_of(coef_ref, lanes)
        for t in range(2):
            cells = {}
            for n in range(2):
                cells[-1 - n] = low[n, y, t, :, lanes] * present
                cells[n] = cross[n, y, t, :, lanes]
                cells[2 + n] = middle[n, y, t, :, lanes]

            def store(n, v, t=t):
                out_cross[n, y, t, :, lanes] = e_cross[n, y, t, :, lanes] - v

            x_row(cells, [0, 1], store, coef, True)
            cells = {}
            for n in range(2):
                cells[rows - 4 + n] = middle[rows - 6 + n, y, t, :, lanes]
                cells[rows - 2 + n] = inside[n, y, t, :, lanes]
                cells[rows + n] = high[1 - n, y, t, :, lanes]

            def store_in(n, v, t=t):
                r = n - rows + 2
                out_in[r, y, t, :, lanes] = e_in[r, y, t, :, lanes] - v

            x_row(cells, [rows - 2, rows - 1], store_in, coef, True)
        return carry

    lax.fori_loop(0, chunks * 16, along_x, 0, unroll=2)
    for m in range(5):
        sums[m, 2 : rows - 2, :] = inner_sums[m]
    row_moments(out_cross, 2, weights, sums, 0)
    row_moments(out_in, 2, weights, sums, rows - 2)


def final_kernel(rows, m_cross, m_mid, m_in, params, table, factor, out,
                 wide, tall, kept, staged, sems):
    mirrored = lax.axis_index("gx") % 2
    spread_features([params[k] for k in range(6)], wide, tall, rows)
    copies = []
    for source, first, count in ((m_cross, 0, 2), (m_mid, 2, rows - 4), (m_in, rows - 2, 2)):
        near = staged.at[pl.ds(first, count)]

        def store(row, chunk, value, near=near):
            for y in range(16):
                for t in range(2):
                    near[row, y, chunk, pl.ds(t, SUB, stride=2), :] = value[y, t]

        relax_rows(source, store, tall, first, count, table, factor, kept)
        more = row_copies(mirrored, out, near, first, sems.at[pl.ds(first, count)], True)
        for copy in more:
            copy.start()
        copies += more
    for copy in copies:
        copy.wait()


def body(distribution, velocity_order, cell_codes, knudsen, inflow):
    rows, count_y, count_z, width = distribution.shape
    peers = lax.axis_size("vert")
    line = lax.axis_size("gx")
    total = width * peers
    cells = count_y * count_z
    chunks = width // LANES

    vmem = pl.BlockSpec(memory_space=pltpu.VMEM)
    smem = pl.BlockSpec(memory_space=pltpu.SMEM)
    hbm = pl.BlockSpec(memory_space=pltpu.HBM)

    def slab(n):
        return jax.ShapeDtypeStruct((n, count_y, 2, SUB, width), F32)

    def slab_scratch(n):
        return pltpu.VMEM((n, count_y, 2, SUB, width), F32)

    def feature_scratch(n):
        return [
            pltpu.VMEM((n, FEATURES, cells), F32),
            pltpu.VMEM((n, cells, FEATURES), BF16),
            pltpu.VMEM((2, count_y, 2, SUB, LANES), F32),
        ]

    def staging(n):
        return [
            pltpu.VMEM((n, count_y, chunks, count_z, LANES), F32),
            pltpu.SemaphoreType.DMA((n, chunks)),
        ]

    def limits(mib):
        return pltpu.CompilerParams(vmem_limit_bytes=mib * 1024 * 1024)

    def in_hbm(array):
        return pltpu.with_memory_space_constraint(array, pltpu.HBM)

    def load():
        return pl.pallas_call(
            load_kernel,
            in_specs=[hbm] * 3,
            out_specs=[vmem] * 7,
            out_shape=[
                slab(2),
                slab(2),
                jax.ShapeDtypeStruct((rows, cells), jnp.int32),
                jax.ShapeDtypeStruct((FEATURES, width), BF16),
                jax.ShapeDtypeStruct((FEATURES, LANES), BF16),
                jax.ShapeDtypeStruct((16, 2 * width), BF16),
                jax.ShapeDtypeStruct((9, SUB, width), F32),
            ],
            scratch_shapes=[
                pltpu.VMEM((1, width), jnp.int32),
                pltpu.VMEM((rows, count_y, count_z), jnp.int32),
                pltpu.VMEM((rows, cells), jnp.int32),
                staging(2)[0],
                staging(2)[0],
                staging(2)[1],
                staging(2)[1],
                pltpu.SemaphoreType.DMA((2,)),
            ],
            compiler_params=limits(6),
            name="load_edges",
        )(in_hbm(velocity_order.reshape(1, width)), in_hbm(cell_codes), in_hbm(distribution))

    def inner(relax, state, params):
        sums = jax.ShapeDtypeStruct((5, rows - 4, cells), F32)
        out_shape = [slab(rows - 4), slab(2), slab(2), sums]
        scratch = []
        if relax:
            out_shape = [slab(2), slab(rows - 4), slab(2)] + out_shape
            scratch = feature_scratch(rows)
            args = (*state, params, table, factor, coef, weights)
        else:
            out_shape = [slab(rows - 4)] + out_shape
            scratch = staging(rows - 4)
            args = (*state, coef, weights)
        return pl.pallas_call(
            functools.partial(inner_kernel, relax, rows),
            in_specs=[vmem if relax or n != 2 else hbm for n in range(len(args))],
            out_specs=[vmem] * len(out_shape),
            out_shape=out_shape,
            scratch_shapes=scratch,
            compiler_params=limits(LIMIT_MIB),
            name="inner_relax" if relax else "inner_first",
        )(*args)

    def edge(relax, halos, params, state, edges, sums):
        scratch = []
        args = (*state, *edges, coef, weights, sums)
        if relax:
            scratch = feature_scratch(2) + [slab_scratch(2)] * 2
            args = (*params, table, factor, *args)
        args = (*halos, *args)
        return pl.pallas_call(
            functools.partial(edge_kernel, relax, rows, line),
            in_specs=[vmem] * len(args),
            out_specs=[vmem] * 3,
            out_shape=[slab(2), slab(2), jax.ShapeDtypeStruct((5, rows, cells), F32)],
            scratch_shapes=scratch,
            compiler_params=limits(LIMIT_MIB),
            name="edge_relax" if relax else "edge_first",
        )(*args)

    def cell_params(parts, *sizes):
        return pl.pallas_call(
            functools.partial(param_kernel, total, len(parts)),
            in_specs=[vmem] * (len(parts) + 1) + [smem, smem],
            out_specs=[vmem] * len(sizes),
            out_shape=[jax.ShapeDtypeStruct((6, n, cells), F32) for n in sizes],
            compiler_params=limits(4),
            name="cell_params",
        )(*parts, codes, knudsen, inflow)

    def final(moved, params):
        return pl.pallas_call(
            functools.partial(final_kernel, rows),
            in_specs=[vmem] * 6,
            out_specs=hbm,
            out_shape=jax.ShapeDtypeStruct(distribution.shape, F32),
            scratch_shapes=feature_scratch(rows) + staging(rows),
            compiler_params=limits(LIMIT_MIB),
            name="final_relax",
        )(*moved, params, table, factor)

    parts = lax.axis_size("groups")
    across = []
    for p in range(parts):
        for i in (0, line - 1):
            other = p ^ 1 if (p ^ 1) < parts else p
            across.append((p * line + i, other * line + i))
        for i in range(1, line - 1, 2):
            across += [(p * line + i, p * line + i + 1), (p * line + i + 1, p * line + i)]
    within = []
    for i in range(0, line, 2):
        within += [(i, i + 1), (i + 1, i)]

    def exchange(cross, inside):
        return (
            lax.ppermute(cross, ("groups", "gx"), across),
            lax.ppermute(inside, "gx", within),
        )

    def gather(part):
        parts = [part]
        for shift in range(1, peers):
            pairs = [(i, (i + shift) % peers) for i in range(peers)]
            parts.append(lax.ppermute(part, "vert", pairs))
        return parts

    cross, inside, codes, table, factor, weights, coef = load()
    halos = exchange(cross, inside)
    middle, m_mid, e_cross, e_in, sums = inner(False, (cross, inside, in_hbm(distribution)), None)
    m_cross, m_in, sums = edge(
        False, halos, None, (cross, middle, inside), (e_cross, e_in), sums
    )
    for _ in range(1, STEPS):
        halos = exchange(m_cross, m_in)
        params, p_cross, p_in = cell_params(gather(sums), rows, 2, 2)
        p_halos = exchange(p_cross, p_in)
        moved = (m_cross, m_mid, m_in)
        *state, m_mid, e_cross, e_in, sums = inner(True, moved, params)
        m_cross, m_in, sums = edge(True, halos, p_halos, state, (e_cross, e_in), sums)
    (params,) = cell_params(gather(sums), rows)
    return final((m_cross, m_mid, m_in), params)


def solution(mesh):
    placed = (
        P(("groups", "gx"), None, None, "vert"),
        P("vert"),
        P(("groups", "gx"), None, None),
        P("groups"),
        P("groups"),
    )
    return jax.shard_map(
        body,
        mesh=mesh,
        in_specs=placed,
        out_specs=P(("groups", "gx"), None, None, "vert"),
        check_vma=False,
    )
```

```python
import functools

import jax
import jax.numpy as jnp
from jax import lax
from jax.experimental import pallas as pl
from jax.experimental.pallas import tpu as pltpu
from jax.sharding import PartitionSpec as P

VGX = 16
VGY = 16
VGZ = 8
STEPS = 3
LANES = 128
SUB = 8
FEATURES = 32
PAIR = 2 * LANES
UNIT = 3.0 / 16.0
LOG2E = 1.4426950408889634
LIMIT_MIB = 10
F32 = jnp.float32
BF16 = jnp.bfloat16


def minmod(lower, upper):
    return jnp.maximum(
        jnp.minimum(lower, upper), jnp.minimum(jnp.maximum(lower, upper), 0.0)
    )


def lanes_of(chunk):
    return pl.ds(pl.multiple_of(chunk * LANES, LANES), LANES)


def coefs_of(coef_ref, lanes):
    return [coef_ref[k, :, lanes] for k in range(9)]


def x_row(cells, rows, store, coef, change=False):
    reach, lean, ahead = coef[0], coef[1], coef[2] > 0.0
    first, last = rows[0], rows[-1]
    steps = {n: cells[n + 1] - cells[n] for n in range(first - 2, last + 2)}
    faces = {
        n: cells[n] + lean * minmod(steps[n - 1], steps[n])
        for n in range(first - 1, last + 2)
    }
    for n in rows:
        source = jnp.where(ahead, faces[n - 1], faces[n + 1])
        v = reach * (faces[n] - source)
        store(n, v if change else cells[n] - v)


def yz_row(source, out, fresh, row, lanes, coef):
    reach_y, lean_y, ahead_y = coef[3], coef[4], coef[5] > 0.0
    reach_z, lean_z, ahead_z = coef[6], coef[7], coef[8] > 0.0
    count = 16
    cells, steps, faces = {}, {}, {}

    def cell(y, t):
        y %= count
        if (y, t) not in cells:
            cells[y, t] = source[row, y, t, :, lanes]
        return cells[y, t]

    def step(y, t):
        y %= count
        if (y, t) not in steps:
            steps[y, t] = cell(y + 1, t) - cell(y, t)
        return steps[y, t]

    def face(y, t):
        y %= count
        if (y, t) not in faces:
            faces[y, t] = cell(y, t) + lean_y * minmod(step(y - 1, t), step(y, t))
        return faces[y, t]

    def up(v):
        return pltpu.roll(v, SUB - 1, 0)

    def down(v):
        return pltpu.roll(v, 1, 0)

    for y in range(count):
        even, odd = cell(y, 0), cell(y, 1)
        step_even = odd - even
        step_odd = up(even) - odd
        face_even = even + lean_z * minmod(down(step_odd), step_even)
        face_odd = odd + lean_z * minmod(step_even, step_odd)
        winds = (
            jnp.where(ahead_z, down(face_odd), face_odd),
            jnp.where(ahead_z, face_even, up(face_even)),
        )
        for t, z_face in enumerate((face_even, face_odd)):
            v = cell(y, t) if fresh else out[row, y, t, :, lanes]
            v -= reach_z * (z_face - winds[t])
            upwind = jnp.where(ahead_y, face(y - 1, t), face(y + 1, t))
            v -= reach_y * (face(y, t) - upwind)
            out[row, y, t, :, lanes] = v


def yz_rows(source, out, fresh, rows, coef_ref):
    chunks = source.shape[-1] // LANES

    def one(i, carry):
        chunk, row = i // rows, i % rows
        lanes = lanes_of(chunk)
        yz_row(source, out, fresh, row, lanes, coefs_of(coef_ref, lanes))
        return carry

    lax.fori_loop(0, chunks * rows, one, 0, unroll=2)


def row_moments(rows, weights, sums):
    for row, place in rows:
        flat = row[...].reshape(256, row.shape[-1])
        high = flat.astype(BF16)
        rest = (flat - high.astype(F32)).astype(BF16)
        both = jnp.concatenate([high, rest], axis=1)
        contract = (((1,), (1,)), ((), ()))
        part = lax.dot_general(weights[...], both, contract, preferred_element_type=F32)
        for m in range(4):
            sums[m, place : place + 1, :] = part[m : m + 1]
        sums[4, place : place + 1, :] = part[4:5] + part[5:6]


def three_parts(value):
    high = value.astype(BF16).astype(F32)
    rest = value - high
    middle = rest.astype(BF16).astype(F32)
    low = (rest - middle).astype(BF16).astype(F32)
    return high, middle, low


def spread_features(params, wide, tall, rows):
    alpha, beta_x, beta_y, beta_z, gamma, keep = params
    alpha = jnp.where(gamma == 0.0, -10000.0, alpha)
    zero = jnp.zeros_like(alpha)
    columns = []
    for value in (alpha, beta_x, beta_y, beta_z, gamma, gamma, keep):
        columns.extend(three_parts(value))
    columns.extend([zero] * (FEATURES - len(columns)))
    for k, value in enumerate(columns):
        for r in range(rows):
            wide[r, k : k + 1, :] = value[r : r + 1]
    for r in range(rows):
        tall[r] = wide[r].T.astype(BF16)


def relax_group(group, tall, table, factor, kept):
    for u, (place, _, _) in enumerate(group):
        keep = jnp.dot(tall[place], factor[...], preferred_element_type=F32)
        kept[u] = keep.reshape(16, 2, SUB, LANES)
    for u, (place, moved, store) in enumerate(group):
        for pair in range(moved.shape[-1] // PAIR):
            columns = table[:, pair * PAIR : (pair + 1) * PAIR]
            power = jnp.dot(tall[place], columns, preferred_element_type=F32)
            for half in range(2):
                chunk = 2 * pair + half
                shape = jnp.exp2(power[:, half * LANES : (half + 1) * LANES])
                shape = shape.reshape(16, 2, SUB, LANES)
                lanes = pl.ds(chunk * LANES, LANES)
                store(chunk, kept[u] * moved[:, :, :, lanes] + shape)


def into(row):
    def store(chunk, v):
        row[:, :, :, pl.ds(chunk * LANES, LANES)] = v

    return store


def param_kernel(total, count, *refs):
    parts = refs[:count]
    codes, knudsen, inflow, out, *edges = refs[count:]
    sums = [parts[0][m] for m in range(5)]
    for part in parts[1:]:
        sums = [s + part[m] for m, s in enumerate(sums)]
    density = sums[0] * (1.0 / total)
    scale = UNIT / sums[0]
    u_x, u_y, u_z = (sums[m] * scale for m in (1, 2, 3))
    heat = (UNIT * sums[4] * scale - (u_x * u_x + u_y * u_y + u_z * u_z)) * (1.0 / 3.0)
    rate = 0.5 * density / (density + knudsen[0])
    code = codes[...]
    flowing, wall = code == 1, code == 2
    closed = flowing | wall
    u_x = jnp.where(flowing, inflow[1], jnp.where(wall, 0.0, u_x))
    u_y = jnp.where(closed, 0.0, u_y)
    u_z = jnp.where(closed, 0.0, u_z)
    heat = jnp.where(flowing, inflow[2], jnp.where(wall, inflow[3], heat))
    amount = jnp.where(flowing, inflow[0], jnp.where(wall, density, rate * density))
    keep = jnp.where(closed, 0.0, 1.0 - rate)
    g = (-0.5 * LOG2E) / heat

    def line(u, n, unit):
        s = None
        for i in range(n):
            gap = (i + 0.5 - n / 2) * unit - u
            e = jnp.exp2(g * (gap * gap))
            s = e if s is None else s + e
        return s

    norm = line(u_x, VGX, 6.0 / VGX) * line(u_y, VGY, 6.0 / VGY)
    norm = norm * line(u_z, VGZ, 6.0 / VGZ) * (1.0 / total)
    alpha = (jnp.log(amount) - jnp.log(norm)) * LOG2E
    alpha = alpha + g * (u_x * u_x + u_y * u_y + u_z * u_z)
    lean = (-2.0 * UNIT) * g
    params = (alpha, lean * u_x, lean * u_y, lean * u_z, g * (UNIT * UNIT), keep)
    rows = code.shape[0]
    for k, value in enumerate(params):
        out[k] = value
        if edges:
            edges[0][k] = value[:2]
            edges[1][k] = value[rows - 2 :]


def row_copies(mirrored, whole, staged, first, sems, out=False):
    rows = whole.shape[0]
    copies = []
    for n in range(staged.shape[0]):
        place = jnp.where(mirrored > 0, rows - 1 - first - n, first + n)
        for c in range(staged.shape[2]):
            far = whole.at[place, :, :, pl.ds(c * LANES, LANES)]
            near = staged.at[n, :, c]
            pair = (near, far) if out else (far, near)
            copies.append(pltpu.make_async_copy(*pair, sems.at[n, c]))
    return copies


def unstage(staged, out):
    count = staged.shape[1]

    def one(i, carry):
        n, y = i // count, i % count
        for c in range(staged.shape[2]):
            for t in range(2):
                v = staged[n, y, c, pl.ds(t, SUB, stride=2), :]
                out[n, y, t, :, pl.ds(c * LANES, LANES)] = v
        return carry

    lax.fori_loop(0, staged.shape[0] * count, one, 0, unroll=4)


def load_kernel(order_in, codes_in, state, cross, inside, codes, table, factor, weights, coef,
                order, raw, flat, near_cross, near_inside, cross_sems, inside_sems, more_sems):
    rows, width = state.shape[0], order.shape[-1]
    mirrored = lax.axis_index("gx") % 2
    more = [
        pltpu.make_async_copy(order_in, order, more_sems.at[0]),
        pltpu.make_async_copy(codes_in, raw, more_sems.at[1]),
    ]
    copies = row_copies(mirrored, state, near_cross, 0, cross_sems)
    copies += row_copies(mirrored, state, near_inside, rows - 2, inside_sems)
    for copy in more + copies:
        copy.start()
    for copy in more:
        copy.wait()

    slots = jnp.broadcast_to(order[...], (SUB, width))
    n_x = 2 * (slots // (VGY * VGZ)) - (VGX - 1)
    n_y = 2 * (slots // VGZ % VGY) - (VGY - 1)
    n_z = 2 * (2 * (slots % VGZ) - (VGZ - 1))
    square = n_x * n_x + n_y * n_y + n_z * n_z
    low_part = square % 8
    whole = [n.astype(F32) for n in (n_x, n_y, n_z, square - low_part, low_part)]
    whole = [jnp.ones_like(whole[0])] + whole

    def pick(values, index):
        out = jnp.zeros_like(values[0])
        for k, value in enumerate(values):
            out = jnp.where(index == k, value, out)
        return out

    line = lax.broadcasted_iota(jnp.int32, (SUB, width), 0)
    moments = jnp.concatenate([pick(whole, line), jnp.zeros((SUB, width), F32)], axis=0)
    moments = moments.astype(BF16)
    weights[:, :width] = moments
    weights[:, width:] = moments
    table[...] = jnp.concatenate(
        [pick(whole, (line + SUB * g) // 3) for g in range(FEATURES // SUB)], axis=0
    ).astype(BF16)
    slot = lax.broadcasted_iota(jnp.int32, (FEATURES, LANES), 0)
    factor[...] = jnp.where((slot >= 18) & (slot < 21), 1.0, 0.0).astype(BF16)
    turn = jnp.where(mirrored > 0, -1.0, 1.0)
    for k, (n, scale) in enumerate(
        ((whole[1] * turn, 0.1), (whole[2], 1.0 / 30.0), (whole[3], 1.0 / 30.0))
    ):
        reach = jnp.abs(n * UNIT * scale)
        sign = jnp.where(n > 0.0, 1.0, -1.0)
        coef[3 * k] = reach
        coef[3 * k + 1] = 0.5 * sign * (1.0 - reach)
        coef[3 * k + 2] = sign

    span = raw.shape[2]
    z = lax.broadcasted_iota(jnp.int32, (span, span), 0)
    goes = lax.broadcasted_iota(jnp.int32, (span, span), 1)
    shuffle = jnp.where(goes == z % 2 * SUB + z // 2, 1.0, 0.0).astype(BF16)
    lined = raw[...].reshape(rows * raw.shape[1], span).astype(F32).astype(BF16)
    lined = jnp.dot(lined, shuffle, preferred_element_type=F32).astype(jnp.int32)
    raw[...] = lined.reshape(rows, raw.shape[1], span)
    for y in range(raw.shape[1]):
        flat[:, y * span : (y + 1) * span] = raw[:, y, :]
    for r in range(rows):
        place = jnp.where(mirrored > 0, rows - 1 - r, r)
        codes[r : r + 1, :] = flat[pl.ds(place, 1), :]
    half = len(copies) // 2
    for copy in copies[:half]:
        copy.wait()
    unstage(near_cross, cross)
    for copy in copies[half:]:
        copy.wait()
    unstage(near_inside, inside)


def inner_kernel(relax, rows, *refs):
    if relax:
        (m_cross, m_mid, m_in, params, table, factor, coef_ref, weights,
         cross, middle, inside, out, e_cross, e_in, sums, wide, tall, kept) = refs
        spread_features([params[k] for k in range(6)], wide, tall, rows)
        group = [(r, m_cross.at[r], into(cross.at[r])) for r in range(2)]
        group += [(rows - 2 + r, m_in.at[r], into(inside.at[r])) for r in range(2)]
        relax_group(group, tall, table, factor, kept)
        for first in range(0, rows - 4, 4):
            group = [
                (2 + r, m_mid.at[r], into(middle.at[r]))
                for r in range(first, min(first + 4, rows - 4))
            ]
            relax_group(group, tall, table, factor, kept)
    else:
        (cross, inside, state, coef_ref, weights, middle, out, e_cross, e_in, sums,
         near, sems) = refs
        mirrored = lax.axis_index("gx") % 2
        copies = row_copies(mirrored, state, near, 2, sems)
        for copy in copies:
            copy.start()
    yz_rows(cross, e_cross, True, 2, coef_ref)
    yz_rows(inside, e_in, True, 2, coef_ref)
    if not relax:
        for copy in copies:
            copy.wait()
        unstage(near, middle)
    chunks = middle.shape[-1] // LANES
    inner = rows - 4

    def along_x(i, carry):
        chunk, y = i // 16, i % 16
        lanes = lanes_of(chunk)
        coef = coefs_of(coef_ref, lanes)
        for t in range(2):
            cells = {}
            for n in range(rows):
                if n < 2:
                    cells[n] = cross[n, y, t, :, lanes]
                elif n < rows - 2:
                    cells[n] = middle[n - 2, y, t, :, lanes]
                else:
                    cells[n] = inside[n - rows + 2, y, t, :, lanes]

            def store(n, v, t=t):
                out[n - 2, y, t, :, lanes] = v

            x_row(cells, list(range(2, rows - 2)), store, coef)
        return carry

    lax.fori_loop(0, chunks * 16, along_x, 0, unroll=4)
    yz_rows(middle, out, False, inner, coef_ref)
    row_moments([(out.at[r], r) for r in range(inner)], weights, sums)


def edge_kernel(relax, rows, line, *refs):
    if relax:
        (h_cross, h_in, p_cross, p_in, table, factor, cross, middle, inside, e_cross,
         e_in, coef_ref, weights, inner_sums, out_cross, out_in, sums,
         wide, tall, kept, low, high) = refs
        params = [jnp.concatenate([p_cross[k], p_in[k]], axis=0) for k in range(6)]
        spread_features(params, wide, tall, 4)
        group = [(r, h_cross.at[r], into(low.at[r])) for r in range(2)]
        group += [(2 + r, h_in.at[r], into(high.at[r])) for r in range(2)]
        relax_group(group, tall, table, factor, kept)
    else:
        (low, high, cross, middle, inside, e_cross, e_in, coef_ref, weights,
         inner_sums, out_cross, out_in, sums) = refs
    chunks = middle.shape[-1] // LANES
    place = lax.axis_index("gx")
    present = jnp.where((place == 0) | (place == line - 1), 0.0, 1.0)

    def along_x(i, carry):
        chunk, y = i // 16, i % 16
        lanes = lanes_of(chunk)
        coef = coefs_of(coef_ref, lanes)
        for t in range(2):
            cells = {}
            for n in range(2):
                cells[-1 - n] = low[n, y, t, :, lanes] * present
                cells[n] = cross[n, y, t, :, lanes]
                cells[2 + n] = middle[n, y, t, :, lanes]

            def store(n, v, t=t):
                out_cross[n, y, t, :, lanes] = e_cross[n, y, t, :, lanes] - v

            x_row(cells, [0, 1], store, coef, True)
            cells = {}
            for n in range(2):
                cells[rows - 4 + n] = middle[rows - 6 + n, y, t, :, lanes]
                cells[rows - 2 + n] = inside[n, y, t, :, lanes]
                cells[rows + n] = high[1 - n, y, t, :, lanes]

            def store_in(n, v, t=t):
                r = n - rows + 2
                out_in[r, y, t, :, lanes] = e_in[r, y, t, :, lanes] - v

            x_row(cells, [rows - 2, rows - 1], store_in, coef, True)
        return carry

    lax.fori_loop(0, chunks * 16, along_x, 0, unroll=4)
    for m in range(5):
        sums[m, 2 : rows - 2, :] = inner_sums[m]
    edges = [(out_cross.at[r], r) for r in range(2)]
    edges += [(out_in.at[r], rows - 2 + r) for r in range(2)]
    row_moments(edges, weights, sums)


def final_kernel(rows, m_cross, m_mid, m_in, params, table, factor, out,
                 wide, tall, kept, staged, sems):
    mirrored = lax.axis_index("gx") % 2
    spread_features([params[k] for k in range(6)], wide, tall, rows)
    moved = [m_cross.at[r] for r in range(2)] + [m_mid.at[r] for r in range(rows - 4)]
    moved += [m_in.at[r] for r in range(2)]
    copies = []
    for first in range(0, rows, 2):
        near = staged.at[pl.ds(first, 2)]
        group = []
        for r in range(2):

            def store(chunk, v, row=near.at[r]):
                for y in range(16):
                    for t in range(2):
                        row[y, chunk, pl.ds(t, SUB, stride=2), :] = v[y, t]

            group.append((first + r, moved[first + r], store))
        relax_group(group, tall, table, factor, kept)
        more = row_copies(mirrored, out, near, first, sems.at[pl.ds(first, 2)], True)
        for copy in more:
            copy.start()
        copies += more
    for copy in copies:
        copy.wait()


def body(distribution, velocity_order, cell_codes, knudsen, inflow):
    rows, count_y, count_z, width = distribution.shape
    peers = lax.axis_size("vert")
    line = lax.axis_size("gx")
    total = width * peers
    cells = count_y * count_z
    chunks = width // LANES

    vmem = pl.BlockSpec(memory_space=pltpu.VMEM)
    smem = pl.BlockSpec(memory_space=pltpu.SMEM)
    hbm = pl.BlockSpec(memory_space=pltpu.HBM)

    def slab(n):
        return jax.ShapeDtypeStruct((n, count_y, 2, SUB, width), F32)

    def slab_scratch(n):
        return pltpu.VMEM((n, count_y, 2, SUB, width), F32)

    def feature_scratch(n):
        return [
            pltpu.VMEM((n, FEATURES, cells), F32),
            pltpu.VMEM((n, cells, FEATURES), BF16),
            pltpu.VMEM((4, count_y, 2, SUB, LANES), F32),
        ]

    def staging(n):
        return [
            pltpu.VMEM((n, count_y, chunks, count_z, LANES), F32),
            pltpu.SemaphoreType.DMA((n, chunks)),
        ]

    def limits(mib):
        return pltpu.CompilerParams(vmem_limit_bytes=mib * 1024 * 1024)

    def in_hbm(array):
        return pltpu.with_memory_space_constraint(array, pltpu.HBM)

    def load():
        return pl.pallas_call(
            load_kernel,
            in_specs=[hbm] * 3,
            out_specs=[vmem] * 7,
            out_shape=[
                slab(2),
                slab(2),
                jax.ShapeDtypeStruct((rows, cells), jnp.int32),
                jax.ShapeDtypeStruct((FEATURES, width), BF16),
                jax.ShapeDtypeStruct((FEATURES, LANES), BF16),
                jax.ShapeDtypeStruct((16, 2 * width), BF16),
                jax.ShapeDtypeStruct((9, SUB, width), F32),
            ],
            scratch_shapes=[
                pltpu.VMEM((1, width), jnp.int32),
                pltpu.VMEM((rows, count_y, count_z), jnp.int32),
                pltpu.VMEM((rows, cells), jnp.int32),
                staging(2)[0],
                staging(2)[0],
                staging(2)[1],
                staging(2)[1],
                pltpu.SemaphoreType.DMA((2,)),
            ],
            compiler_params=limits(6),
            name="load_edges",
        )(in_hbm(velocity_order.reshape(1, width)), in_hbm(cell_codes), in_hbm(distribution))

    def inner(relax, state, params):
        sums = jax.ShapeDtypeStruct((5, rows - 4, cells), F32)
        out_shape = [slab(rows - 4), slab(2), slab(2), sums]
        scratch = []
        if relax:
            out_shape = [slab(2), slab(rows - 4), slab(2)] + out_shape
            scratch = feature_scratch(rows)
            args = (*state, params, table, factor, coef, weights)
        else:
            out_shape = [slab(rows - 4)] + out_shape
            scratch = staging(rows - 4)
            args = (*state, coef, weights)
        return pl.pallas_call(
            functools.partial(inner_kernel, relax, rows),
            in_specs=[vmem if relax or n != 2 else hbm for n in range(len(args))],
            out_specs=[vmem] * len(out_shape),
            out_shape=out_shape,
            scratch_shapes=scratch,
            compiler_params=limits(LIMIT_MIB),
            name="inner_relax" if relax else "inner_first",
        )(*args)

    def edge(relax, halos, params, state, edges, sums):
        scratch = []
        args = (*state, *edges, coef, weights, sums)
        if relax:
            scratch = feature_scratch(4) + [slab_scratch(2)] * 2
            args = (*params, table, factor, *args)
        args = (*halos, *args)
        return pl.pallas_call(
            functools.partial(edge_kernel, relax, rows, line),
            in_specs=[vmem] * len(args),
            out_specs=[vmem] * 3,
            out_shape=[slab(2), slab(2), jax.ShapeDtypeStruct((5, rows, cells), F32)],
            scratch_shapes=scratch,
            compiler_params=limits(LIMIT_MIB),
            name="edge_relax" if relax else "edge_first",
        )(*args)

    def cell_params(parts, *sizes):
        return pl.pallas_call(
            functools.partial(param_kernel, total, len(parts)),
            in_specs=[vmem] * (len(parts) + 1) + [smem, smem],
            out_specs=[vmem] * len(sizes),
            out_shape=[jax.ShapeDtypeStruct((6, n, cells), F32) for n in sizes],
            compiler_params=limits(4),
            name="cell_params",
        )(*parts, codes, knudsen, inflow)

    def final(moved, params):
        return pl.pallas_call(
            functools.partial(final_kernel, rows),
            in_specs=[vmem] * 6,
            out_specs=hbm,
            out_shape=jax.ShapeDtypeStruct(distribution.shape, F32),
            scratch_shapes=feature_scratch(rows) + staging(rows),
            compiler_params=limits(LIMIT_MIB),
            name="final_relax",
        )(*moved, params, table, factor)

    parts = lax.axis_size("groups")
    across = []
    for p in range(parts):
        for i in (0, line - 1):
            other = p ^ 1 if (p ^ 1) < parts else p
            across.append((p * line + i, other * line + i))
        for i in range(1, line - 1, 2):
            across += [(p * line + i, p * line + i + 1), (p * line + i + 1, p * line + i)]
    within = []
    for i in range(0, line, 2):
        within += [(i, i + 1), (i + 1, i)]

    def exchange(cross, inside):
        return (
            lax.ppermute(cross, ("groups", "gx"), across),
            lax.ppermute(inside, "gx", within),
        )

    def gather(part):
        parts = [part]
        for shift in range(1, peers):
            pairs = [(i, (i + shift) % peers) for i in range(peers)]
            parts.append(lax.ppermute(part, "vert", pairs))
        return parts

    cross, inside, codes, table, factor, weights, coef = load()
    halos = exchange(cross, inside)
    middle, m_mid, e_cross, e_in, sums = inner(False, (cross, inside, in_hbm(distribution)), None)
    m_cross, m_in, sums = edge(
        False, halos, None, (cross, middle, inside), (e_cross, e_in), sums
    )
    for _ in range(1, STEPS):
        halos = exchange(m_cross, m_in)
        params, p_cross, p_in = cell_params(gather(sums), rows, 2, 2)
        p_halos = exchange(p_cross, p_in)
        moved = (m_cross, m_mid, m_in)
        *state, m_mid, e_cross, e_in, sums = inner(True, moved, params)
        m_cross, m_in, sums = edge(True, halos, p_halos, state, (e_cross, e_in), sums)
    (params,) = cell_params(gather(sums), rows)
    return final((m_cross, m_mid, m_in), params)


def solution(mesh):
    placed = (
        P(("groups", "gx"), None, None, "vert"),
        P("vert"),
        P(("groups", "gx"), None, None),
        P("groups"),
        P("groups"),
    )
    return jax.shard_map(
        body,
        mesh=mesh,
        in_specs=placed,
        out_specs=P(("groups", "gx"), None, None, "vert"),
        check_vma=False,
    )
```

```python
import functools

import jax
import jax.numpy as jnp
from jax import lax
from jax.experimental import pallas as pl
from jax.experimental.pallas import tpu as pltpu
from jax.sharding import PartitionSpec as P

VGX = 16
VGY = 16
VGZ = 8
STEPS = 3
LANES = 128
SUB = 8
FEATURES = 32
PAIR = 2 * LANES
UNIT = 3.0 / 16.0
LOG2E = 1.4426950408889634
LIMIT_MIB = 10
F32 = jnp.float32
BF16 = jnp.bfloat16


def minmod(lower, upper):
    return jnp.maximum(
        jnp.minimum(lower, upper), jnp.minimum(jnp.maximum(lower, upper), 0.0)
    )


def lanes_of(chunk):
    return pl.ds(pl.multiple_of(chunk * LANES, LANES), LANES)


def coefs_of(coef_ref, lanes):
    return [coef_ref[k, :, lanes] for k in range(9)]


def x_row(cells, rows, store, coef, change=False):
    reach, lean, ahead = coef[0], coef[1], coef[2] > 0.0
    first, last = rows[0], rows[-1]
    steps = {n: cells[n + 1] - cells[n] for n in range(first - 2, last + 2)}
    faces = {
        n: cells[n] + lean * minmod(steps[n - 1], steps[n])
        for n in range(first - 1, last + 2)
    }
    for n in rows:
        source = jnp.where(ahead, faces[n - 1], faces[n + 1])
        v = reach * (faces[n] - source)
        store(n, v if change else cells[n] - v)


def yz_row(source, out, fresh, row, lanes, coef):
    reach_y, lean_y, ahead_y = coef[3], coef[4], coef[5] > 0.0
    reach_z, lean_z, ahead_z = coef[6], coef[7], coef[8] > 0.0
    count = 16
    cells, steps, faces = {}, {}, {}

    def cell(y, t):
        y %= count
        if (y, t) not in cells:
            cells[y, t] = source[row, y, t, :, lanes]
        return cells[y, t]

    def step(y, t):
        y %= count
        if (y, t) not in steps:
            steps[y, t] = cell(y + 1, t) - cell(y, t)
        return steps[y, t]

    def face(y, t):
        y %= count
        if (y, t) not in faces:
            faces[y, t] = cell(y, t) + lean_y * minmod(step(y - 1, t), step(y, t))
        return faces[y, t]

    def up(v):
        return pltpu.roll(v, SUB - 1, 0)

    def down(v):
        return pltpu.roll(v, 1, 0)

    for y in range(count):
        even, odd = cell(y, 0), cell(y, 1)
        step_even = odd - even
        step_odd = up(even) - odd
        face_even = even + lean_z * minmod(down(step_odd), step_even)
        face_odd = odd + lean_z * minmod(step_even, step_odd)
        winds = (
            jnp.where(ahead_z, down(face_odd), face_odd),
            jnp.where(ahead_z, face_even, up(face_even)),
        )
        for t, z_face in enumerate((face_even, face_odd)):
            v = cell(y, t) if fresh else out[row, y, t, :, lanes]
            v -= reach_z * (z_face - winds[t])
            upwind = jnp.where(ahead_y, face(y - 1, t), face(y + 1, t))
            v -= reach_y * (face(y, t) - upwind)
            out[row, y, t, :, lanes] = v


def yz_rows(source, out, fresh, rows, coef_ref):
    chunks = source.shape[-1] // LANES

    def one(i, carry):
        chunk, row = i // rows, i % rows
        lanes = lanes_of(chunk)
        yz_row(source, out, fresh, row, lanes, coefs_of(coef_ref, lanes))
        return carry

    lax.fori_loop(0, chunks * rows, one, 0, unroll=2)


def row_moments(rows, weights, sums):
    for row, place in rows:
        flat = row[...].reshape(256, row.shape[-1])
        high = flat.astype(BF16)
        rest = (flat - high.astype(F32)).astype(BF16)
        both = jnp.concatenate([high, rest], axis=1)
        contract = (((1,), (1,)), ((), ()))
        part = lax.dot_general(weights[...], both, contract, preferred_element_type=F32)
        for m in range(4):
            sums[m, place : place + 1, :] = part[m : m + 1]
        sums[4, place : place + 1, :] = part[4:5] + part[5:6]


def three_parts(value):
    high = value.astype(BF16).astype(F32)
    rest = value - high
    middle = rest.astype(BF16).astype(F32)
    low = (rest - middle).astype(BF16).astype(F32)
    return high, middle, low


def spread_features(params, wide, tall, rows):
    alpha, beta_x, beta_y, beta_z, gamma, keep = params
    alpha = jnp.where(gamma == 0.0, -10000.0, alpha)
    zero = jnp.zeros_like(alpha)
    columns = []
    for value in (alpha, beta_x, beta_y, beta_z, gamma, gamma, keep):
        columns.extend(three_parts(value))
    columns.extend([zero] * (FEATURES - len(columns)))
    for k, value in enumerate(columns):
        for r in range(rows):
            wide[r, k : k + 1, :] = value[r : r + 1]
    for r in range(rows):
        tall[r] = wide[r].T.astype(BF16)


def relax_group(group, tall, table, factor, kept):
    for u, (place, _, _) in enumerate(group):
        keep = jnp.dot(tall[place], factor[...], preferred_element_type=F32)
        kept[u] = keep.reshape(16, 2, SUB, LANES)
    for u, (place, moved, store) in enumerate(group):
        for pair in range(moved.shape[-1] // PAIR):
            columns = table[:, pair * PAIR : (pair + 1) * PAIR]
            power = jnp.dot(tall[place], columns, preferred_element_type=F32)
            for half in range(2):
                chunk = 2 * pair + half
                shape = jnp.exp2(power[:, half * LANES : (half + 1) * LANES])
                shape = shape.reshape(16, 2, SUB, LANES)
                lanes = pl.ds(chunk * LANES, LANES)
                store(chunk, kept[u] * moved[:, :, :, lanes] + shape)


def into(row):
    def store(chunk, v):
        row[:, :, :, pl.ds(chunk * LANES, LANES)] = v

    return store


def param_kernel(total, count, *refs):
    parts = refs[:count]
    if len(refs) == count + 4:
        codes, knudsen, inflow, out = refs[count:]
    else:
        (codes, knudsen, inflow, m_in, table, factor, out, p_cross, inside,
         wide, tall, kept) = refs[count:]
    sums = [parts[0][m] for m in range(5)]
    for part in parts[1:]:
        sums = [s + part[m] for m, s in enumerate(sums)]
    density = sums[0] * (1.0 / total)
    scale = UNIT / sums[0]
    u_x, u_y, u_z = (sums[m] * scale for m in (1, 2, 3))
    heat = (UNIT * sums[4] * scale - (u_x * u_x + u_y * u_y + u_z * u_z)) * (1.0 / 3.0)
    rate = 0.5 * density / (density + knudsen[0])
    code = codes[...]
    flowing, wall = code == 1, code == 2
    closed = flowing | wall
    u_x = jnp.where(flowing, inflow[1], jnp.where(wall, 0.0, u_x))
    u_y = jnp.where(closed, 0.0, u_y)
    u_z = jnp.where(closed, 0.0, u_z)
    heat = jnp.where(flowing, inflow[2], jnp.where(wall, inflow[3], heat))
    amount = jnp.where(flowing, inflow[0], jnp.where(wall, density, rate * density))
    keep = jnp.where(closed, 0.0, 1.0 - rate)
    g = (-0.5 * LOG2E) / heat

    def line(u, n, unit):
        s = None
        for i in range(n):
            gap = (i + 0.5 - n / 2) * unit - u
            e = jnp.exp2(g * (gap * gap))
            s = e if s is None else s + e
        return s

    norm = line(u_x, VGX, 6.0 / VGX) * line(u_y, VGY, 6.0 / VGY)
    norm = norm * line(u_z, VGZ, 6.0 / VGZ) * (1.0 / total)
    alpha = (jnp.log(amount) - jnp.log(norm)) * LOG2E
    alpha = alpha + g * (u_x * u_x + u_y * u_y + u_z * u_z)
    lean = (-2.0 * UNIT) * g
    params = (alpha, lean * u_x, lean * u_y, lean * u_z, g * (UNIT * UNIT), keep)
    rows = code.shape[0]
    for k, value in enumerate(params):
        out[k] = value
    if len(refs) > count + 4:
        for k, value in enumerate(params):
            p_cross[k] = value[:2]
        spread_features([value[rows - 2 :] for value in params], wide, tall, 2)
        group = [(r, m_in.at[r], into(inside.at[r])) for r in range(2)]
        relax_group(group, tall, table, factor, kept)


def row_copies(mirrored, whole, staged, first, sems, out=False):
    rows = whole.shape[0]
    copies = []
    for n in range(staged.shape[0]):
        place = jnp.where(mirrored > 0, rows - 1 - first - n, first + n)
        for c in range(staged.shape[2]):
            far = whole.at[place, :, :, pl.ds(c * LANES, LANES)]
            near = staged.at[n, :, c]
            pair = (near, far) if out else (far, near)
            copies.append(pltpu.make_async_copy(*pair, sems.at[n, c]))
    return copies


def unstage(staged, out):
    count = staged.shape[1]

    def one(i, carry):
        n, y = i // count, i % count
        for c in range(staged.shape[2]):
            for t in range(2):
                v = staged[n, y, c, pl.ds(t, SUB, stride=2), :]
                out[n, y, t, :, pl.ds(c * LANES, LANES)] = v
        return carry

    lax.fori_loop(0, staged.shape[0] * count, one, 0, unroll=4)


def load_kernel(order_in, codes_in, state, cross, inside, codes, table, factor, weights, coef,
                order, raw, flat, near_cross, near_inside, cross_sems, inside_sems, more_sems):
    rows, width = state.shape[0], order.shape[-1]
    mirrored = lax.axis_index("gx") % 2
    more = [
        pltpu.make_async_copy(order_in, order, more_sems.at[0]),
        pltpu.make_async_copy(codes_in, raw, more_sems.at[1]),
    ]
    copies = row_copies(mirrored, state, near_cross, 0, cross_sems)
    copies += row_copies(mirrored, state, near_inside, rows - 2, inside_sems)
    for copy in more + copies:
        copy.start()
    for copy in more:
        copy.wait()

    slots = jnp.broadcast_to(order[...], (SUB, width))
    n_x = 2 * (slots // (VGY * VGZ)) - (VGX - 1)
    n_y = 2 * (slots // VGZ % VGY) - (VGY - 1)
    n_z = 2 * (2 * (slots % VGZ) - (VGZ - 1))
    square = n_x * n_x + n_y * n_y + n_z * n_z
    low_part = square % 8
    whole = [n.astype(F32) for n in (n_x, n_y, n_z, square - low_part, low_part)]
    whole = [jnp.ones_like(whole[0])] + whole

    def pick(values, index):
        out = jnp.zeros_like(values[0])
        for k, value in enumerate(values):
            out = jnp.where(index == k, value, out)
        return out

    line = lax.broadcasted_iota(jnp.int32, (SUB, width), 0)
    moments = jnp.concatenate([pick(whole, line), jnp.zeros((SUB, width), F32)], axis=0)
    moments = moments.astype(BF16)
    weights[:, :width] = moments
    weights[:, width:] = moments
    table[...] = jnp.concatenate(
        [pick(whole, (line + SUB * g) // 3) for g in range(FEATURES // SUB)], axis=0
    ).astype(BF16)
    slot = lax.broadcasted_iota(jnp.int32, (FEATURES, LANES), 0)
    factor[...] = jnp.where((slot >= 18) & (slot < 21), 1.0, 0.0).astype(BF16)
    turn = jnp.where(mirrored > 0, -1.0, 1.0)
    for k, (n, scale) in enumerate(
        ((whole[1] * turn, 0.1), (whole[2], 1.0 / 30.0), (whole[3], 1.0 / 30.0))
    ):
        reach = jnp.abs(n * UNIT * scale)
        sign = jnp.where(n > 0.0, 1.0, -1.0)
        coef[3 * k] = reach
        coef[3 * k + 1] = 0.5 * sign * (1.0 - reach)
        coef[3 * k + 2] = sign

    span = raw.shape[2]
    z = lax.broadcasted_iota(jnp.int32, (span, span), 0)
    goes = lax.broadcasted_iota(jnp.int32, (span, span), 1)
    shuffle = jnp.where(goes == z % 2 * SUB + z // 2, 1.0, 0.0).astype(BF16)
    lined = raw[...].reshape(rows * raw.shape[1], span).astype(F32).astype(BF16)
    lined = jnp.dot(lined, shuffle, preferred_element_type=F32).astype(jnp.int32)
    raw[...] = lined.reshape(rows, raw.shape[1], span)
    for y in range(raw.shape[1]):
        flat[:, y * span : (y + 1) * span] = raw[:, y, :]
    for r in range(rows):
        place = jnp.where(mirrored > 0, rows - 1 - r, r)
        codes[r : r + 1, :] = flat[pl.ds(place, 1), :]
    half = len(copies) // 2
    for copy in copies[:half]:
        copy.wait()
    unstage(near_cross, cross)
    for copy in copies[half:]:
        copy.wait()
    unstage(near_inside, inside)


def inner_kernel(relax, rows, *refs):
    if relax:
        (m_cross, m_mid, inside, params, table, factor, coef_ref, weights,
         cross, middle, out, e_cross, e_in, sums, wide, tall, kept) = refs
        spread_features([params[k] for k in range(6)], wide, tall, rows - 2)
        group = [(r, m_cross.at[r], into(cross.at[r])) for r in range(2)]
        group += [(2 + r, m_mid.at[r], into(middle.at[r])) for r in range(rows - 4)]
        for first in range(0, rows - 2, 3):
            relax_group(group[first : first + 3], tall, table, factor, kept)
    else:
        (cross, inside, state, coef_ref, weights, middle, out, e_cross, e_in, sums,
         near, sems) = refs
        mirrored = lax.axis_index("gx") % 2
        copies = row_copies(mirrored, state, near, 2, sems)
        for copy in copies:
            copy.start()
    yz_rows(cross, e_cross, True, 2, coef_ref)
    yz_rows(inside, e_in, True, 2, coef_ref)
    if not relax:
        for copy in copies:
            copy.wait()
        unstage(near, middle)
    chunks = middle.shape[-1] // LANES
    inner = rows - 4

    def along_x(i, carry):
        chunk, y = i // 16, i % 16
        lanes = lanes_of(chunk)
        coef = coefs_of(coef_ref, lanes)
        for t in range(2):
            cells = {}
            for n in range(rows):
                if n < 2:
                    cells[n] = cross[n, y, t, :, lanes]
                elif n < rows - 2:
                    cells[n] = middle[n - 2, y, t, :, lanes]
                else:
                    cells[n] = inside[n - rows + 2, y, t, :, lanes]

            def store(n, v, t=t):
                out[n - 2, y, t, :, lanes] = v

            x_row(cells, list(range(2, rows - 2)), store, coef)
        return carry

    lax.fori_loop(0, chunks * 16, along_x, 0, unroll=4)
    yz_rows(middle, out, False, inner, coef_ref)
    row_moments([(out.at[r], r) for r in range(inner)], weights, sums)


def edge_kernel(sides, relax, rows, line, *refs):
    refs = list(refs)
    take = lambda n: [refs.pop(0) for _ in range(n)]
    if "cross" in sides:
        low, cross, e_cross, inner_sums = take(4)
        if relax:
            params, table, factor = take(3)
    if "in" in sides:
        high, inside, e_in = take(3)
    elif "cross" in sides:
        (in_sums,) = take(1)
    middle, coef_ref, weights, sums = take(4)
    edges = []
    if "cross" in sides:
        (out_cross,) = take(1)
        edges += [(out_cross.at[r], r) for r in range(2)]
    if "in" in sides:
        (out_in,) = take(1)
        first = rows - 2 if "cross" in sides else 0
        edges += [(out_in.at[r], first + r) for r in range(2)]
    if relax:
        wide, tall, kept, relaxed = take(4)
        spread_features([params[k] for k in range(6)], wide, tall, 2)
        group = [(r, low.at[r], into(relaxed.at[r])) for r in range(2)]
        relax_group(group, tall, table, factor, kept)
        low = relaxed
    chunks = middle.shape[-1] // LANES
    place = lax.axis_index("gx")
    present = jnp.where((place == 0) | (place == line - 1), 0.0, 1.0)

    def along_x(i, carry):
        chunk, y = i // 16, i % 16
        lanes = lanes_of(chunk)
        coef = coefs_of(coef_ref, lanes)
        for t in range(2):
            if "cross" in sides:
                cells = {}
                for n in range(2):
                    cells[-1 - n] = low[n, y, t, :, lanes] * present
                    cells[n] = cross[n, y, t, :, lanes]
                    cells[2 + n] = middle[n, y, t, :, lanes]

                def store(n, v, t=t):
                    out_cross[n, y, t, :, lanes] = e_cross[n, y, t, :, lanes] - v

                x_row(cells, [0, 1], store, coef, True)
            if "in" in sides:
                cells = {}
                for n in range(2):
                    cells[rows - 4 + n] = middle[rows - 6 + n, y, t, :, lanes]
                    cells[rows - 2 + n] = inside[n, y, t, :, lanes]
                    cells[rows + n] = high[1 - n, y, t, :, lanes]

                def store_in(n, v, t=t):
                    r = n - rows + 2
                    out_in[r, y, t, :, lanes] = e_in[r, y, t, :, lanes] - v

                x_row(cells, [rows - 2, rows - 1], store_in, coef, True)
        return carry

    lax.fori_loop(0, chunks * 16, along_x, 0, unroll=4)
    if "cross" in sides:
        for m in range(5):
            sums[m, 2 : rows - 2, :] = inner_sums[m]
            if "in" not in sides:
                sums[m, rows - 2 :, :] = in_sums[m]
    row_moments(edges, weights, sums)


def final_kernel(rows, m_cross, m_mid, m_in, params, table, factor, out,
                 wide, tall, kept, staged, sems):
    mirrored = lax.axis_index("gx") % 2
    spread_features([params[k] for k in range(6)], wide, tall, rows)
    moved = [m_cross.at[r] for r in range(2)] + [m_mid.at[r] for r in range(rows - 4)]
    moved += [m_in.at[r] for r in range(2)]
    copies = []
    for first in range(0, rows, 2):
        near = staged.at[pl.ds(first, 2)]
        group = []
        for r in range(2):

            def store(chunk, v, row=near.at[r]):
                for y in range(16):
                    for t in range(2):
                        row[y, chunk, pl.ds(t, SUB, stride=2), :] = v[y, t]

            group.append((first + r, moved[first + r], store))
        relax_group(group, tall, table, factor, kept)
        more = row_copies(mirrored, out, near, first, sems.at[pl.ds(first, 2)], True)
        for copy in more:
            copy.start()
        copies += more
    for copy in copies:
        copy.wait()


def body(distribution, velocity_order, cell_codes, knudsen, inflow):
    rows, count_y, count_z, width = distribution.shape
    peers = lax.axis_size("vert")
    line = lax.axis_size("gx")
    total = width * peers
    cells = count_y * count_z
    chunks = width // LANES

    vmem = pl.BlockSpec(memory_space=pltpu.VMEM)
    smem = pl.BlockSpec(memory_space=pltpu.SMEM)
    hbm = pl.BlockSpec(memory_space=pltpu.HBM)

    def slab(n):
        return jax.ShapeDtypeStruct((n, count_y, 2, SUB, width), F32)

    def slab_scratch(n):
        return pltpu.VMEM((n, count_y, 2, SUB, width), F32)

    def feature_scratch(n):
        return [
            pltpu.VMEM((n, FEATURES, cells), F32),
            pltpu.VMEM((n, cells, FEATURES), BF16),
            pltpu.VMEM((min(n, 4), count_y, 2, SUB, LANES), F32),
        ]

    def staging(n):
        return [
            pltpu.VMEM((n, count_y, chunks, count_z, LANES), F32),
            pltpu.SemaphoreType.DMA((n, chunks)),
        ]

    def limits(mib):
        return pltpu.CompilerParams(vmem_limit_bytes=mib * 1024 * 1024)

    def in_hbm(array):
        return pltpu.with_memory_space_constraint(array, pltpu.HBM)

    def load():
        return pl.pallas_call(
            load_kernel,
            in_specs=[hbm] * 3,
            out_specs=[vmem] * 7,
            out_shape=[
                slab(2),
                slab(2),
                jax.ShapeDtypeStruct((rows, cells), jnp.int32),
                jax.ShapeDtypeStruct((FEATURES, width), BF16),
                jax.ShapeDtypeStruct((FEATURES, LANES), BF16),
                jax.ShapeDtypeStruct((16, 2 * width), BF16),
                jax.ShapeDtypeStruct((9, SUB, width), F32),
            ],
            scratch_shapes=[
                pltpu.VMEM((1, width), jnp.int32),
                pltpu.VMEM((rows, count_y, count_z), jnp.int32),
                pltpu.VMEM((rows, cells), jnp.int32),
                staging(2)[0],
                staging(2)[0],
                staging(2)[1],
                staging(2)[1],
                pltpu.SemaphoreType.DMA((2,)),
            ],
            compiler_params=limits(6),
            name="load_edges",
        )(in_hbm(velocity_order.reshape(1, width)), in_hbm(cell_codes), in_hbm(distribution))

    def inner(relax, state, params):
        sums = jax.ShapeDtypeStruct((5, rows - 4, cells), F32)
        out_shape = [slab(rows - 4), slab(2), slab(2), sums]
        scratch = []
        if relax:
            out_shape = [slab(2), slab(rows - 4)] + out_shape
            scratch = feature_scratch(rows - 2)
            args = (*state, params, table, factor, coef, weights)
        else:
            out_shape = [slab(rows - 4)] + out_shape
            scratch = staging(rows - 4)
            args = (*state, coef, weights)
        return pl.pallas_call(
            functools.partial(inner_kernel, relax, rows),
            in_specs=[vmem if relax or n != 2 else hbm for n in range(len(args))],
            out_specs=[vmem] * len(out_shape),
            out_shape=out_shape,
            scratch_shapes=scratch,
            compiler_params=limits(LIMIT_MIB),
            name="inner_relax" if relax else "inner_first",
        )(*args)

    def edge(sides, relax, *args):
        scratch = feature_scratch(2) + [slab_scratch(2)] if relax else []
        return pl.pallas_call(
            functools.partial(edge_kernel, sides, relax, rows, line),
            in_specs=[vmem] * (len(args) + 2),
            out_specs=[vmem] * (1 + len(sides)),
            out_shape=[jax.ShapeDtypeStruct((5, rows if "cross" in sides else 2, cells), F32)]
            + [slab(2)] * len(sides),
            scratch_shapes=scratch,
            compiler_params=limits(LIMIT_MIB),
            name="edge_" + "_".join(sides),
        )(*args, coef, weights)

    def cell_params(parts, *edge_args):
        out_shape = [jax.ShapeDtypeStruct((6, rows, cells), F32)]
        if edge_args:
            out_shape += [jax.ShapeDtypeStruct((6, 2, cells), F32), slab(2)]
        return pl.pallas_call(
            functools.partial(param_kernel, total, len(parts)),
            in_specs=[vmem] * (len(parts) + 1) + [smem, smem] + [vmem] * len(edge_args),
            out_specs=[vmem] * len(out_shape),
            out_shape=out_shape,
            scratch_shapes=feature_scratch(2) if edge_args else [],
            compiler_params=limits(4),
            name="cell_params",
        )(*parts, codes, knudsen, inflow, *edge_args)

    def final(moved, params):
        return pl.pallas_call(
            functools.partial(final_kernel, rows),
            in_specs=[vmem] * 6,
            out_specs=hbm,
            out_shape=jax.ShapeDtypeStruct(distribution.shape, F32),
            scratch_shapes=feature_scratch(rows) + staging(rows),
            compiler_params=limits(LIMIT_MIB),
            name="final_relax",
        )(*moved, params, table, factor)

    parts = lax.axis_size("groups")
    across = []
    for p in range(parts):
        for i in (0, line - 1):
            other = p ^ 1 if (p ^ 1) < parts else p
            across.append((p * line + i, other * line + i))
        for i in range(1, line - 1, 2):
            across += [(p * line + i, p * line + i + 1), (p * line + i + 1, p * line + i)]
    within = []
    for i in range(0, line, 2):
        within += [(i, i + 1), (i + 1, i)]

    def swap_across(x):
        return lax.ppermute(x, ("groups", "gx"), across)

    def swap_within(x):
        return lax.ppermute(x, "gx", within)

    def gather(part):
        parts = [part]
        for shift in range(1, peers):
            pairs = [(i, (i + shift) % peers) for i in range(peers)]
            parts.append(lax.ppermute(part, "vert", pairs))
        return parts

    cross, inside, codes, table, factor, weights, coef = load()
    low, high = swap_across(cross), swap_within(inside)
    middle, m_mid, e_cross, e_in, sums = inner(False, (cross, inside, in_hbm(distribution)), None)
    in_sums, m_in = edge(("in",), False, high, inside, e_in, middle)
    sums, m_cross = edge(("cross",), False, low, cross, e_cross, sums, in_sums, middle)
    for _ in range(1, STEPS):
        low = swap_across(m_cross)
        params, p_cross, inside = cell_params(gather(sums), m_in, table, factor)
        p_low, high = swap_across(p_cross), swap_within(inside)
        cross, middle, m_mid, e_cross, e_in, sums = inner(
            True, (m_cross, m_mid, inside), params
        )
        far = (low, cross, e_cross, sums, p_low, table, factor)
        near = (high, inside, e_in)
        sums, m_cross, m_in = edge(("cross", "in"), True, *far, *near, middle)
    (params,) = cell_params(gather(sums))
    return final((m_cross, m_mid, m_in), params)


def solution(mesh):
    placed = (
        P(("groups", "gx"), None, None, "vert"),
        P("vert"),
        P(("groups", "gx"), None, None),
        P("groups"),
        P("groups"),
    )
    return jax.shard_map(
        body,
        mesh=mesh,
        in_specs=placed,
        out_specs=P(("groups", "gx"), None, None, "vert"),
        check_vma=False,
    )
```

```python
import functools

import jax
import jax.numpy as jnp
from jax import lax
from jax.experimental import pallas as pl
from jax.experimental.pallas import tpu as pltpu
from jax.sharding import PartitionSpec as P

VGX = 16
VGY = 16
VGZ = 8
STEPS = 3
LANES = 128
SUB = 8
FEATURES = 32
PAIR = 2 * LANES
UNIT = 3.0 / 16.0
LOG2E = 1.4426950408889634
LIMIT_MIB = 10
F32 = jnp.float32
BF16 = jnp.bfloat16


def minmod(lower, upper):
    return jnp.maximum(
        jnp.minimum(lower, upper), jnp.minimum(jnp.maximum(lower, upper), 0.0)
    )


def lanes_of(chunk):
    return pl.ds(pl.multiple_of(chunk * LANES, LANES), LANES)


def coefs_of(coef_ref, lanes):
    return [coef_ref[k, :, lanes] for k in range(9)]


def x_row(cells, rows, store, coef, change=False):
    reach, lean, ahead = coef[0], coef[1], coef[2] > 0.0
    first, last = rows[0], rows[-1]
    steps = {n: cells[n + 1] - cells[n] for n in range(first - 2, last + 2)}
    faces = {
        n: cells[n] + lean * minmod(steps[n - 1], steps[n])
        for n in range(first - 1, last + 2)
    }
    for n in rows:
        source = jnp.where(ahead, faces[n - 1], faces[n + 1])
        v = reach * (faces[n] - source)
        store(n, v if change else cells[n] - v)


def yz_row(source, out, fresh, row, lanes, coef):
    reach_y, lean_y, ahead_y = coef[3], coef[4], coef[5] > 0.0
    reach_z, lean_z, ahead_z = coef[6], coef[7], coef[8] > 0.0
    count = 16
    cells, steps, faces = {}, {}, {}

    def cell(y, t):
        y %= count
        if (y, t) not in cells:
            cells[y, t] = source[row, y, t, :, lanes]
        return cells[y, t]

    def step(y, t):
        y %= count
        if (y, t) not in steps:
            steps[y, t] = cell(y + 1, t) - cell(y, t)
        return steps[y, t]

    def face(y, t):
        y %= count
        if (y, t) not in faces:
            faces[y, t] = cell(y, t) + lean_y * minmod(step(y - 1, t), step(y, t))
        return faces[y, t]

    def up(v):
        return pltpu.roll(v, SUB - 1, 0)

    def down(v):
        return pltpu.roll(v, 1, 0)

    for y in range(count):
        even, odd = cell(y, 0), cell(y, 1)
        step_even = odd - even
        step_odd = up(even) - odd
        face_even = even + lean_z * minmod(down(step_odd), step_even)
        face_odd = odd + lean_z * minmod(step_even, step_odd)
        winds = (
            jnp.where(ahead_z, down(face_odd), face_odd),
            jnp.where(ahead_z, face_even, up(face_even)),
        )
        for t, z_face in enumerate((face_even, face_odd)):
            v = cell(y, t) if fresh else out[row, y, t, :, lanes]
            v -= reach_z * (z_face - winds[t])
            upwind = jnp.where(ahead_y, face(y - 1, t), face(y + 1, t))
            v -= reach_y * (face(y, t) - upwind)
            out[row, y, t, :, lanes] = v


def yz_rows(source, out, fresh, rows, coef_ref):
    chunks = source.shape[-1] // LANES

    def one(i, carry):
        chunk, row = i // rows, i % rows
        lanes = lanes_of(chunk)
        yz_row(source, out, fresh, row, lanes, coefs_of(coef_ref, lanes))
        return carry

    lax.fori_loop(0, chunks * rows, one, 0, unroll=2)


def row_moments(rows, weights, sums):
    for row, place in rows:
        flat = row[...].reshape(256, row.shape[-1])
        high = flat.astype(BF16)
        rest = (flat - high.astype(F32)).astype(BF16)
        both = jnp.concatenate([high, rest], axis=1)
        contract = (((1,), (1,)), ((), ()))
        part = lax.dot_general(weights[...], both, contract, preferred_element_type=F32)
        for m in range(4):
            sums[m, place : place + 1, :] = part[m : m + 1]
        sums[4, place : place + 1, :] = part[4:5] + part[5:6]


def three_parts(value):
    high = value.astype(BF16).astype(F32)
    rest = value - high
    middle = rest.astype(BF16).astype(F32)
    low = (rest - middle).astype(BF16).astype(F32)
    return high, middle, low


def spread_features(params, wide, tall, rows):
    alpha, beta_x, beta_y, beta_z, gamma, keep = params
    alpha = jnp.where(gamma == 0.0, -10000.0, alpha)
    zero = jnp.zeros_like(alpha)
    columns = []
    for value in (alpha, beta_x, beta_y, beta_z, gamma, gamma, keep):
        columns.extend(three_parts(value))
    columns.extend([zero] * (FEATURES - len(columns)))
    for k, value in enumerate(columns):
        for r in range(rows):
            wide[r, k : k + 1, :] = value[r : r + 1]
    for r in range(rows):
        tall[r] = wide[r].T.astype(BF16)


def relax_group(group, tall, table, factor, kept):
    for u, (place, _, _) in enumerate(group):
        keep = jnp.dot(tall[place], factor[...], preferred_element_type=F32)
        kept[u] = keep.reshape(16, 2, SUB, LANES)
    for u, (place, moved, store) in enumerate(group):
        for pair in range(moved.shape[-1] // PAIR):
            columns = table[:, pair * PAIR : (pair + 1) * PAIR]
            power = jnp.dot(tall[place], columns, preferred_element_type=F32)
            for half in range(2):
                chunk = 2 * pair + half
                shape = jnp.exp2(power[:, half * LANES : (half + 1) * LANES])
                shape = shape.reshape(16, 2, SUB, LANES)
                lanes = pl.ds(chunk * LANES, LANES)
                store(chunk, kept[u] * moved[:, :, :, lanes] + shape)


def into(row):
    def store(chunk, v):
        row[:, :, :, pl.ds(chunk * LANES, LANES)] = v

    return store


def param_kernel(total, count, *refs):
    parts = refs[:count]
    codes, knudsen, inflow, out, *edges = refs[count:]
    sums = [parts[0][m] for m in range(5)]
    for part in parts[1:]:
        sums = [s + part[m] for m, s in enumerate(sums)]
    density = sums[0] * (1.0 / total)
    scale = UNIT / sums[0]
    u_x, u_y, u_z = (sums[m] * scale for m in (1, 2, 3))
    heat = (UNIT * sums[4] * scale - (u_x * u_x + u_y * u_y + u_z * u_z)) * (1.0 / 3.0)
    rate = 0.5 * density / (density + knudsen[0])
    code = codes[...]
    flowing, wall = code == 1, code == 2
    closed = flowing | wall
    u_x = jnp.where(flowing, inflow[1], jnp.where(wall, 0.0, u_x))
    u_y = jnp.where(closed, 0.0, u_y)
    u_z = jnp.where(closed, 0.0, u_z)
    heat = jnp.where(flowing, inflow[2], jnp.where(wall, inflow[3], heat))
    amount = jnp.where(flowing, inflow[0], jnp.where(wall, density, rate * density))
    keep = jnp.where(closed, 0.0, 1.0 - rate)
    g = (-0.5 * LOG2E) / heat

    def line(u, n, unit):
        s = None
        for i in range(n):
            gap = (i + 0.5 - n / 2) * unit - u
            e = jnp.exp2(g * (gap * gap))
            s = e if s is None else s + e
        return s

    norm = line(u_x, VGX, 6.0 / VGX) * line(u_y, VGY, 6.0 / VGY)
    norm = norm * line(u_z, VGZ, 6.0 / VGZ) * (1.0 / total)
    alpha = (jnp.log(amount) - jnp.log(norm)) * LOG2E
    alpha = alpha + g * (u_x * u_x + u_y * u_y + u_z * u_z)
    lean = (-2.0 * UNIT) * g
    params = (alpha, lean * u_x, lean * u_y, lean * u_z, g * (UNIT * UNIT), keep)
    rows = code.shape[0]
    for k, value in enumerate(params):
        out[k] = value
        if edges:
            edges[0][k] = value[:2]
            edges[1][k] = value[rows - 2 :]


def row_copies(mirrored, whole, staged, first, sems, out=False):
    rows = whole.shape[0]
    copies = []
    for n in range(staged.shape[0]):
        place = jnp.where(mirrored > 0, rows - 1 - first - n, first + n)
        for c in range(staged.shape[2]):
            far = whole.at[place, :, :, pl.ds(c * LANES, LANES)]
            near = staged.at[n, :, c]
            pair = (near, far) if out else (far, near)
            copies.append(pltpu.make_async_copy(*pair, sems.at[n, c]))
    return copies


def unstage(staged, out):
    count = staged.shape[1]

    def one(i, carry):
        n, y = i // count, i % count
        for c in range(staged.shape[2]):
            for t in range(2):
                v = staged[n, y, c, pl.ds(t, SUB, stride=2), :]
                out[n, y, t, :, pl.ds(c * LANES, LANES)] = v
        return carry

    lax.fori_loop(0, staged.shape[0] * count, one, 0, unroll=4)


def load_kernel(order_in, codes_in, state, cross, inside, codes, table, factor, weights, coef,
                order, raw, flat, near_cross, near_inside, cross_sems, inside_sems, more_sems):
    rows, width = state.shape[0], order.shape[-1]
    mirrored = lax.axis_index("gx") % 2
    more = [
        pltpu.make_async_copy(order_in, order, more_sems.at[0]),
        pltpu.make_async_copy(codes_in, raw, more_sems.at[1]),
    ]
    copies = row_copies(mirrored, state, near_cross, 0, cross_sems)
    copies += row_copies(mirrored, state, near_inside, rows - 2, inside_sems)
    for copy in more + copies:
        copy.start()
    for copy in more:
        copy.wait()

    slots = jnp.broadcast_to(order[...], (SUB, width))
    n_x = 2 * (slots // (VGY * VGZ)) - (VGX - 1)
    n_y = 2 * (slots // VGZ % VGY) - (VGY - 1)
    n_z = 2 * (2 * (slots % VGZ) - (VGZ - 1))
    square = n_x * n_x + n_y * n_y + n_z * n_z
    low_part = square % 8
    whole = [n.astype(F32) for n in (n_x, n_y, n_z, square - low_part, low_part)]
    whole = [jnp.ones_like(whole[0])] + whole

    def pick(values, index):
        out = jnp.zeros_like(values[0])
        for k, value in enumerate(values):
            out = jnp.where(index == k, value, out)
        return out

    line = lax.broadcasted_iota(jnp.int32, (SUB, width), 0)
    moments = jnp.concatenate([pick(whole, line), jnp.zeros((SUB, width), F32)], axis=0)
    moments = moments.astype(BF16)
    weights[:, :width] = moments
    weights[:, width:] = moments
    table[...] = jnp.concatenate(
        [pick(whole, (line + SUB * g) // 3) for g in range(FEATURES // SUB)], axis=0
    ).astype(BF16)
    slot = lax.broadcasted_iota(jnp.int32, (FEATURES, LANES), 0)
    factor[...] = jnp.where((slot >= 18) & (slot < 21), 1.0, 0.0).astype(BF16)
    turn = jnp.where(mirrored > 0, -1.0, 1.0)
    for k, (n, scale) in enumerate(
        ((whole[1] * turn, 0.1), (whole[2], 1.0 / 30.0), (whole[3], 1.0 / 30.0))
    ):
        reach = jnp.abs(n * UNIT * scale)
        sign = jnp.where(n > 0.0, 1.0, -1.0)
        coef[3 * k] = reach
        coef[3 * k + 1] = 0.5 * sign * (1.0 - reach)
        coef[3 * k + 2] = sign

    span = raw.shape[2]
    z = lax.broadcasted_iota(jnp.int32, (span, span), 0)
    goes = lax.broadcasted_iota(jnp.int32, (span, span), 1)
    shuffle = jnp.where(goes == z % 2 * SUB + z // 2, 1.0, 0.0).astype(BF16)
    lined = raw[...].reshape(rows * raw.shape[1], span).astype(F32).astype(BF16)
    lined = jnp.dot(lined, shuffle, preferred_element_type=F32).astype(jnp.int32)
    raw[...] = lined.reshape(rows, raw.shape[1], span)
    for y in range(raw.shape[1]):
        flat[:, y * span : (y + 1) * span] = raw[:, y, :]
    for r in range(rows):
        place = jnp.where(mirrored > 0, rows - 1 - r, r)
        codes[r : r + 1, :] = flat[pl.ds(place, 1), :]
    half = len(copies) // 2
    for copy in copies[:half]:
        copy.wait()
    unstage(near_cross, cross)
    for copy in copies[half:]:
        copy.wait()
    unstage(near_inside, inside)


def inner_kernel(relax, rows, *refs):
    if relax:
        (m_cross, m_mid, m_in, params, table, factor, coef_ref, weights,
         cross, middle, inside, out, e_cross, e_in, sums, wide, tall, kept) = refs
        spread_features([params[k] for k in range(6)], wide, tall, rows)
        group = [(r, m_cross.at[r], into(cross.at[r])) for r in range(2)]
        group += [(rows - 2 + r, m_in.at[r], into(inside.at[r])) for r in range(2)]
        relax_group(group, tall, table, factor, kept)
        for first in range(0, rows - 4, 4):
            group = [
                (2 + r, m_mid.at[r], into(middle.at[r]))
                for r in range(first, min(first + 4, rows - 4))
            ]
            relax_group(group, tall, table, factor, kept)
    else:
        (cross, inside, state, coef_ref, weights, middle, out, e_cross, e_in, sums,
         near, sems) = refs
        mirrored = lax.axis_index("gx") % 2
        copies = row_copies(mirrored, state, near, 2, sems)
        for copy in copies:
            copy.start()
    yz_rows(cross, e_cross, True, 2, coef_ref)
    yz_rows(inside, e_in, True, 2, coef_ref)
    if not relax:
        for copy in copies:
            copy.wait()
        unstage(near, middle)
    chunks = middle.shape[-1] // LANES
    inner = rows - 4

    def along_x(i, carry):
        chunk, y = i // 16, i % 16
        lanes = lanes_of(chunk)
        coef = coefs_of(coef_ref, lanes)
        for t in range(2):
            cells = {}
            for n in range(rows):
                if n < 2:
                    cells[n] = cross[n, y, t, :, lanes]
                elif n < rows - 2:
                    cells[n] = middle[n - 2, y, t, :, lanes]
                else:
                    cells[n] = inside[n - rows + 2, y, t, :, lanes]

            def store(n, v, t=t):
                out[n - 2, y, t, :, lanes] = v

            x_row(cells, list(range(2, rows - 2)), store, coef)
        return carry

    lax.fori_loop(0, chunks * 16, along_x, 0, unroll=4)
    yz_rows(middle, out, False, inner, coef_ref)
    row_moments([(out.at[r], r) for r in range(inner)], weights, sums)


def presence(line):
    place = lax.axis_index("gx")
    return jnp.where((place == 0) | (place == line - 1), 0.0, 1.0)


def cross_x(low, cross, middle, before, out, y, t, lanes, coef, present):
    cells = {}
    for n in range(2):
        cells[-1 - n] = low[n, y, t, :, lanes] * present
        cells[n] = cross[n, y, t, :, lanes]
        cells[2 + n] = middle[n, y, t, :, lanes]

    def store(n, v):
        out[n, y, t, :, lanes] = before[n, y, t, :, lanes] - v

    x_row(cells, [0, 1], store, coef, True)


def in_x(high, inside, middle, before, out, y, t, lanes, coef):
    last = middle.shape[0]
    cells = {}
    for n in range(2):
        cells[n] = middle[last - 2 + n, y, t, :, lanes]
        cells[2 + n] = inside[n, y, t, :, lanes]
        cells[4 + n] = high[1 - n, y, t, :, lanes]

    def store(n, v):
        out[n - 2, y, t, :, lanes] = before[n - 2, y, t, :, lanes] - v

    x_row(cells, [2, 3], store, coef, True)


def each_place(middle, coef_ref, work):
    def one(i, carry):
        lanes = lanes_of(i // 16)
        coef = coefs_of(coef_ref, lanes)
        for t in range(2):
            work(i % 16, t, lanes, coef)
        return carry

    lax.fori_loop(0, middle.shape[-1] // LANES * 16, one, 0, unroll=4)


def first_in_kernel(high, inside, e_in, middle, coef_ref, weights, out, sums):
    each_place(middle, coef_ref, lambda *at: in_x(high, inside, middle, e_in, out, *at))
    row_moments([(out.at[r], r) for r in range(2)], weights, sums)


def first_cross_kernel(line, low, cross, e_cross, middle, coef_ref, weights, inner_sums, in_sums,
                       out, sums):
    present = presence(line)
    each_place(
        middle, coef_ref, lambda *at: cross_x(low, cross, middle, e_cross, out, *at, present)
    )
    rows = sums.shape[1]
    for m in range(5):
        sums[m, 2 : rows - 2, :] = inner_sums[m]
        sums[m, rows - 2 :, :] = in_sums[m]
    row_moments([(out.at[r], r) for r in range(2)], weights, sums)


def edge_kernel(rows, line, h_cross, h_in, p_cross, p_in, table, factor, cross, middle, inside,
                e_cross, e_in, coef_ref, weights, inner_sums, out_cross, out_in, sums,
                wide, tall, kept, low, high):
    params = [jnp.concatenate([p_cross[k], p_in[k]], axis=0) for k in range(6)]
    spread_features(params, wide, tall, 4)
    group = [(r, h_cross.at[r], into(low.at[r])) for r in range(2)]
    group += [(2 + r, h_in.at[r], into(high.at[r])) for r in range(2)]
    relax_group(group, tall, table, factor, kept)
    present = presence(line)

    def work(*at):
        cross_x(low, cross, middle, e_cross, out_cross, *at, present)
        in_x(high, inside, middle, e_in, out_in, *at)

    each_place(middle, coef_ref, work)
    for m in range(5):
        sums[m, 2 : rows - 2, :] = inner_sums[m]
    edges = [(out_cross.at[r], r) for r in range(2)]
    edges += [(out_in.at[r], rows - 2 + r) for r in range(2)]
    row_moments(edges, weights, sums)


def final_kernel(rows, m_cross, m_mid, m_in, params, table, factor, out,
                 wide, tall, kept, staged, sems):
    mirrored = lax.axis_index("gx") % 2
    spread_features([params[k] for k in range(6)], wide, tall, rows)
    moved = [m_cross.at[r] for r in range(2)] + [m_mid.at[r] for r in range(rows - 4)]
    moved += [m_in.at[r] for r in range(2)]
    copies = []
    for first in range(0, rows, 2):
        near = staged.at[pl.ds(first, 2)]
        group = []
        for r in range(2):

            def store(chunk, v, row=near.at[r]):
                for y in range(16):
                    for t in range(2):
                        row[y, chunk, pl.ds(t, SUB, stride=2), :] = v[y, t]

            group.append((first + r, moved[first + r], store))
        relax_group(group, tall, table, factor, kept)
        more = row_copies(mirrored, out, near, first, sems.at[pl.ds(first, 2)], True)
        for copy in more:
            copy.start()
        copies += more
    for copy in copies:
        copy.wait()


def body(distribution, velocity_order, cell_codes, knudsen, inflow):
    rows, count_y, count_z, width = distribution.shape
    peers = lax.axis_size("vert")
    line = lax.axis_size("gx")
    total = width * peers
    cells = count_y * count_z
    chunks = width // LANES

    vmem = pl.BlockSpec(memory_space=pltpu.VMEM)
    smem = pl.BlockSpec(memory_space=pltpu.SMEM)
    hbm = pl.BlockSpec(memory_space=pltpu.HBM)

    def slab(n):
        return jax.ShapeDtypeStruct((n, count_y, 2, SUB, width), F32)

    def slab_scratch(n):
        return pltpu.VMEM((n, count_y, 2, SUB, width), F32)

    def feature_scratch(n):
        return [
            pltpu.VMEM((n, FEATURES, cells), F32),
            pltpu.VMEM((n, cells, FEATURES), BF16),
            pltpu.VMEM((4, count_y, 2, SUB, LANES), F32),
        ]

    def staging(n):
        return [
            pltpu.VMEM((n, count_y, chunks, count_z, LANES), F32),
            pltpu.SemaphoreType.DMA((n, chunks)),
        ]

    def limits(mib):
        return pltpu.CompilerParams(vmem_limit_bytes=mib * 1024 * 1024)

    def in_hbm(array):
        return pltpu.with_memory_space_constraint(array, pltpu.HBM)

    def load():
        return pl.pallas_call(
            load_kernel,
            in_specs=[hbm] * 3,
            out_specs=[vmem] * 7,
            out_shape=[
                slab(2),
                slab(2),
                jax.ShapeDtypeStruct((rows, cells), jnp.int32),
                jax.ShapeDtypeStruct((FEATURES, width), BF16),
                jax.ShapeDtypeStruct((FEATURES, LANES), BF16),
                jax.ShapeDtypeStruct((16, 2 * width), BF16),
                jax.ShapeDtypeStruct((9, SUB, width), F32),
            ],
            scratch_shapes=[
                pltpu.VMEM((1, width), jnp.int32),
                pltpu.VMEM((rows, count_y, count_z), jnp.int32),
                pltpu.VMEM((rows, cells), jnp.int32),
                staging(2)[0],
                staging(2)[0],
                staging(2)[1],
                staging(2)[1],
                pltpu.SemaphoreType.DMA((2,)),
            ],
            compiler_params=limits(6),
            name="load_edges",
        )(in_hbm(velocity_order.reshape(1, width)), in_hbm(cell_codes), in_hbm(distribution))

    def inner(relax, state, params):
        sums = jax.ShapeDtypeStruct((5, rows - 4, cells), F32)
        out_shape = [slab(rows - 4), slab(2), slab(2), sums]
        scratch = []
        if relax:
            out_shape = [slab(2), slab(rows - 4), slab(2)] + out_shape
            scratch = feature_scratch(rows)
            args = (*state, params, table, factor, coef, weights)
        else:
            out_shape = [slab(rows - 4)] + out_shape
            scratch = staging(rows - 4)
            args = (*state, coef, weights)
        return pl.pallas_call(
            functools.partial(inner_kernel, relax, rows),
            in_specs=[vmem if relax or n != 2 else hbm for n in range(len(args))],
            out_specs=[vmem] * len(out_shape),
            out_shape=out_shape,
            scratch_shapes=scratch,
            compiler_params=limits(LIMIT_MIB),
            name="inner_relax" if relax else "inner_first",
        )(*args)

    whole_sums = jax.ShapeDtypeStruct((5, rows, cells), F32)
    edge_sums = jax.ShapeDtypeStruct((5, 2, cells), F32)

    def first_in(*args):
        return pl.pallas_call(
            first_in_kernel,
            in_specs=[vmem] * 6,
            out_specs=[vmem] * 2,
            out_shape=[slab(2), edge_sums],
            compiler_params=limits(LIMIT_MIB),
            name="first_in",
        )(*args, middle, coef, weights)

    def first_cross(*args):
        return pl.pallas_call(
            functools.partial(first_cross_kernel, line),
            in_specs=[vmem] * 8,
            out_specs=[vmem] * 2,
            out_shape=[slab(2), whole_sums],
            compiler_params=limits(LIMIT_MIB),
            name="first_cross",
        )(*args)

    def edge(halos, params, state, edges, sums):
        args = (*halos, *params, table, factor, *state, *edges, coef, weights, sums)
        return pl.pallas_call(
            functools.partial(edge_kernel, rows, line),
            in_specs=[vmem] * len(args),
            out_specs=[vmem] * 3,
            out_shape=[slab(2), slab(2), whole_sums],
            scratch_shapes=feature_scratch(4) + [slab_scratch(2)] * 2,
            compiler_params=limits(LIMIT_MIB),
            name="edge_relax",
        )(*args)

    def cell_params(parts, *sizes):
        return pl.pallas_call(
            functools.partial(param_kernel, total, len(parts)),
            in_specs=[vmem] * (len(parts) + 1) + [smem, smem],
            out_specs=[vmem] * len(sizes),
            out_shape=[jax.ShapeDtypeStruct((6, n, cells), F32) for n in sizes],
            compiler_params=limits(4),
            name="cell_params",
        )(*parts, codes, knudsen, inflow)

    def final(moved, params):
        return pl.pallas_call(
            functools.partial(final_kernel, rows),
            in_specs=[vmem] * 6,
            out_specs=hbm,
            out_shape=jax.ShapeDtypeStruct(distribution.shape, F32),
            scratch_shapes=feature_scratch(rows) + staging(rows),
            compiler_params=limits(LIMIT_MIB),
            name="final_relax",
        )(*moved, params, table, factor)

    parts = lax.axis_size("groups")
    across = []
    for p in range(parts):
        for i in (0, line - 1):
            other = p ^ 1 if (p ^ 1) < parts else p
            across.append((p * line + i, other * line + i))
        for i in range(1, line - 1, 2):
            across += [(p * line + i, p * line + i + 1), (p * line + i + 1, p * line + i)]
    within = []
    for i in range(0, line, 2):
        within += [(i, i + 1), (i + 1, i)]

    def exchange(cross, inside):
        return (
            lax.ppermute(cross, ("groups", "gx"), across),
            lax.ppermute(inside, "gx", within),
        )

    def gather(part):
        parts = [part]
        for shift in range(1, peers):
            pairs = [(i, (i + shift) % peers) for i in range(peers)]
            parts.append(lax.ppermute(part, "vert", pairs))
        return parts

    cross, inside, codes, table, factor, weights, coef = load()
    halos = exchange(cross, inside)
    middle, m_mid, e_cross, e_in, sums = inner(False, (cross, inside, in_hbm(distribution)), None)
    m_in, in_sums = first_in(halos[1], inside, e_in)
    m_cross, sums = first_cross(halos[0], cross, e_cross, middle, coef, weights, sums, in_sums)
    m_cross, m_in, sums = lax.optimization_barrier((m_cross, m_in, sums))
    for _ in range(1, STEPS):
        halos = exchange(m_cross, m_in)
        params, p_cross, p_in = cell_params(gather(sums), rows, 2, 2)
        p_halos = exchange(p_cross, p_in)
        moved = (m_cross, m_mid, m_in)
        *state, m_mid, e_cross, e_in, sums = inner(True, moved, params)
        m_cross, m_in, sums = edge(halos, p_halos, state, (e_cross, e_in), sums)
    (params,) = cell_params(gather(sums), rows)
    return final((m_cross, m_mid, m_in), params)


def solution(mesh):
    placed = (
        P(("groups", "gx"), None, None, "vert"),
        P("vert"),
        P(("groups", "gx"), None, None),
        P("groups"),
        P("groups"),
    )
    return jax.shard_map(
        body,
        mesh=mesh,
        in_specs=placed,
        out_specs=P(("groups", "gx"), None, None, "vert"),
        check_vma=False,
    )
```

```python
import functools

import jax
import jax.numpy as jnp
from jax import lax
from jax.experimental import pallas as pl
from jax.experimental.pallas import tpu as pltpu
from jax.sharding import PartitionSpec as P

VGX = 16
VGY = 16
VGZ = 8
STEPS = 3
LANES = 128
SUB = 8
FEATURES = 32
PAIR = 2 * LANES
UNIT = 3.0 / 16.0
LOG2E = 1.4426950408889634
LIMIT_MIB = 10
F32 = jnp.float32
BF16 = jnp.bfloat16


def minmod(lower, upper):
    return jnp.maximum(
        jnp.minimum(lower, upper), jnp.minimum(jnp.maximum(lower, upper), 0.0)
    )


def lanes_of(chunk):
    return pl.ds(pl.multiple_of(chunk * LANES, LANES), LANES)


def coefs_of(coef_ref, lanes):
    return [coef_ref[k, :, lanes] for k in range(9)]


def x_row(cells, rows, store, coef, change=False, known=None):
    reach, lean, ahead = coef[0], coef[1], coef[2] > 0.0
    steps = {n: cells[n + 1] - cells[n] for n in cells if n + 1 in cells}
    faces = dict(known or {})
    for n in range(rows[0] - 1, rows[-1] + 2):
        if n not in faces:
            faces[n] = cells[n] + lean * minmod(steps[n - 1], steps[n])
    for n in rows:
        source = jnp.where(ahead, faces[n - 1], faces[n + 1])
        v = reach * (faces[n] - source)
        store(n, v if change else cells[n] - v)
    return faces


def yz_row(source, out, fresh, row, lanes, coef):
    reach_y, lean_y, ahead_y = coef[3], coef[4], coef[5] > 0.0
    reach_z, lean_z, ahead_z = coef[6], coef[7], coef[8] > 0.0
    count = 16
    cells, steps, faces = {}, {}, {}

    def cell(y, t):
        y %= count
        if (y, t) not in cells:
            cells[y, t] = source[row, y, t, :, lanes]
        return cells[y, t]

    def step(y, t):
        y %= count
        if (y, t) not in steps:
            steps[y, t] = cell(y + 1, t) - cell(y, t)
        return steps[y, t]

    def face(y, t):
        y %= count
        if (y, t) not in faces:
            faces[y, t] = cell(y, t) + lean_y * minmod(step(y - 1, t), step(y, t))
        return faces[y, t]

    def up(v):
        return pltpu.roll(v, SUB - 1, 0)

    def down(v):
        return pltpu.roll(v, 1, 0)

    for y in range(count):
        even, odd = cell(y, 0), cell(y, 1)
        step_even = odd - even
        step_odd = up(even) - odd
        face_even = even + lean_z * minmod(down(step_odd), step_even)
        face_odd = odd + lean_z * minmod(step_even, step_odd)
        winds = (
            jnp.where(ahead_z, down(face_odd), face_odd),
            jnp.where(ahead_z, face_even, up(face_even)),
        )
        for t, z_face in enumerate((face_even, face_odd)):
            v = cell(y, t) if fresh else out[row, y, t, :, lanes]
            v -= reach_z * (z_face - winds[t])
            upwind = jnp.where(ahead_y, face(y - 1, t), face(y + 1, t))
            v -= reach_y * (face(y, t) - upwind)
            out[row, y, t, :, lanes] = v


def yz_rows(source, out, fresh, rows, coef_ref):
    chunks = source.shape[-1] // LANES

    def one(i, carry):
        chunk, row = i // rows, i % rows
        lanes = lanes_of(chunk)
        yz_row(source, out, fresh, row, lanes, coefs_of(coef_ref, lanes))
        return carry

    lax.fori_loop(0, chunks * rows, one, 0, unroll=2)


def row_moments(rows, weights, sums):
    for row, place in rows:
        flat = row[...].reshape(256, row.shape[-1])
        high = flat.astype(BF16)
        rest = (flat - high.astype(F32)).astype(BF16)
        both = jnp.concatenate([high, rest], axis=1)
        contract = (((1,), (1,)), ((), ()))
        part = lax.dot_general(weights[...], both, contract, preferred_element_type=F32)
        for m in range(4):
            sums[m, place : place + 1, :] = part[m : m + 1]
        sums[4, place : place + 1, :] = part[4:5] + part[5:6]


def three_parts(value):
    high = value.astype(BF16).astype(F32)
    rest = value - high
    middle = rest.astype(BF16).astype(F32)
    low = (rest - middle).astype(BF16).astype(F32)
    return high, middle, low


def spread_features(params, wide, tall, rows):
    alpha, beta_x, beta_y, beta_z, gamma, keep = params
    alpha = jnp.where(gamma == 0.0, -10000.0, alpha)
    zero = jnp.zeros_like(alpha)
    columns = []
    for value in (alpha, beta_x, beta_y, beta_z, gamma, gamma, keep):
        columns.extend(three_parts(value))
    columns.extend([zero] * (FEATURES - len(columns)))
    for k, value in enumerate(columns):
        for r in range(rows):
            wide[r, k : k + 1, :] = value[r : r + 1]
    for r in range(rows):
        tall[r] = wide[r].T.astype(BF16)


def relax_group(group, tall, table, factor, kept):
    for u, (place, _, _) in enumerate(group):
        keep = jnp.dot(tall[place], factor[...], preferred_element_type=F32)
        kept[u] = keep.reshape(16, 2, SUB, LANES)
    for u, (place, moved, store) in enumerate(group):
        for pair in range(moved.shape[-1] // PAIR):
            columns = table[:, pair * PAIR : (pair + 1) * PAIR]
            power = jnp.dot(tall[place], columns, preferred_element_type=F32)
            for half in range(2):
                chunk = 2 * pair + half
                shape = jnp.exp2(power[:, half * LANES : (half + 1) * LANES])
                shape = shape.reshape(16, 2, SUB, LANES)
                lanes = pl.ds(chunk * LANES, LANES)
                store(chunk, kept[u] * moved[:, :, :, lanes] + shape)


def into(row):
    def store(chunk, v):
        row[:, :, :, pl.ds(chunk * LANES, LANES)] = v

    return store


def param_kernel(total, count, *refs):
    parts = refs[:count]
    codes, knudsen, inflow, out, *edges = refs[count:]
    sums = [parts[0][m] for m in range(5)]
    for part in parts[1:]:
        sums = [s + part[m] for m, s in enumerate(sums)]
    density = sums[0] * (1.0 / total)
    scale = UNIT / sums[0]
    u_x, u_y, u_z = (sums[m] * scale for m in (1, 2, 3))
    heat = (UNIT * sums[4] * scale - (u_x * u_x + u_y * u_y + u_z * u_z)) * (1.0 / 3.0)
    rate = 0.5 * density / (density + knudsen[0])
    code = codes[...]
    flowing, wall = code == 1, code == 2
    closed = flowing | wall
    u_x = jnp.where(flowing, inflow[1], jnp.where(wall, 0.0, u_x))
    u_y = jnp.where(closed, 0.0, u_y)
    u_z = jnp.where(closed, 0.0, u_z)
    heat = jnp.where(flowing, inflow[2], jnp.where(wall, inflow[3], heat))
    amount = jnp.where(flowing, inflow[0], jnp.where(wall, density, rate * density))
    keep = jnp.where(closed, 0.0, 1.0 - rate)
    g = (-0.5 * LOG2E) / heat

    def line(u, n, unit):
        s = None
        for i in range(n):
            gap = (i + 0.5 - n / 2) * unit - u
            e = jnp.exp2(g * (gap * gap))
            s = e if s is None else s + e
        return s

    norm = line(u_x, VGX, 6.0 / VGX) * line(u_y, VGY, 6.0 / VGY)
    norm = norm * line(u_z, VGZ, 6.0 / VGZ) * (1.0 / total)
    alpha = (jnp.log(amount) - jnp.log(norm)) * LOG2E
    alpha = alpha + g * (u_x * u_x + u_y * u_y + u_z * u_z)
    lean = (-2.0 * UNIT) * g
    params = (alpha, lean * u_x, lean * u_y, lean * u_z, g * (UNIT * UNIT), keep)
    rows = code.shape[0]
    for k, value in enumerate(params):
        out[k] = value
        if edges:
            edges[0][k] = value[:2]
            edges[1][k] = value[rows - 2 :]


def row_copies(mirrored, whole, staged, first, sems, out=False):
    rows = whole.shape[0]
    copies = []
    for n in range(staged.shape[0]):
        place = jnp.where(mirrored > 0, rows - 1 - first - n, first + n)
        for c in range(staged.shape[2]):
            far = whole.at[place, :, :, pl.ds(c * LANES, LANES)]
            near = staged.at[n, :, c]
            pair = (near, far) if out else (far, near)
            copies.append(pltpu.make_async_copy(*pair, sems.at[n, c]))
    return copies


def unstage(staged, out):
    count = staged.shape[1]

    def one(i, carry):
        n, y = i // count, i % count
        for c in range(staged.shape[2]):
            for t in range(2):
                v = staged[n, y, c, pl.ds(t, SUB, stride=2), :]
                out[n, y, t, :, pl.ds(c * LANES, LANES)] = v
        return carry

    lax.fori_loop(0, staged.shape[0] * count, one, 0, unroll=4)


def load_kernel(order_in, codes_in, state, cross, near_inside, codes, table, factor, weights, coef,
                order, raw, flat, near_cross, cross_sems, inside_sems, more_sems):
    rows, width = state.shape[0], order.shape[-1]
    mirrored = lax.axis_index("gx") % 2
    more = [
        pltpu.make_async_copy(order_in, order, more_sems.at[0]),
        pltpu.make_async_copy(codes_in, raw, more_sems.at[1]),
    ]
    copies = row_copies(mirrored, state, near_cross, 0, cross_sems)
    copies += row_copies(mirrored, state, near_inside, rows - 2, inside_sems)
    for copy in more + copies:
        copy.start()
    for copy in more:
        copy.wait()

    slots = jnp.broadcast_to(order[...], (SUB, width))
    n_x = 2 * (slots // (VGY * VGZ)) - (VGX - 1)
    n_y = 2 * (slots // VGZ % VGY) - (VGY - 1)
    n_z = 2 * (2 * (slots % VGZ) - (VGZ - 1))
    square = n_x * n_x + n_y * n_y + n_z * n_z
    low_part = square % 8
    whole = [n.astype(F32) for n in (n_x, n_y, n_z, square - low_part, low_part)]
    whole = [jnp.ones_like(whole[0])] + whole

    def pick(values, index):
        out = jnp.zeros_like(values[0])
        for k, value in enumerate(values):
            out = jnp.where(index == k, value, out)
        return out

    line = lax.broadcasted_iota(jnp.int32, (SUB, width), 0)
    moments = jnp.concatenate([pick(whole, line), jnp.zeros((SUB, width), F32)], axis=0)
    moments = moments.astype(BF16)
    weights[:, :width] = moments
    weights[:, width:] = moments
    table[...] = jnp.concatenate(
        [pick(whole, (line + SUB * g) // 3) for g in range(FEATURES // SUB)], axis=0
    ).astype(BF16)
    slot = lax.broadcasted_iota(jnp.int32, (FEATURES, LANES), 0)
    factor[...] = jnp.where((slot >= 18) & (slot < 21), 1.0, 0.0).astype(BF16)
    turn = jnp.where(mirrored > 0, -1.0, 1.0)
    for k, (n, scale) in enumerate(
        ((whole[1] * turn, 0.1), (whole[2], 1.0 / 30.0), (whole[3], 1.0 / 30.0))
    ):
        reach = jnp.abs(n * UNIT * scale)
        sign = jnp.where(n > 0.0, 1.0, -1.0)
        coef[3 * k] = reach
        coef[3 * k + 1] = 0.5 * sign * (1.0 - reach)
        coef[3 * k + 2] = sign

    span = raw.shape[2]
    z = lax.broadcasted_iota(jnp.int32, (span, span), 0)
    goes = lax.broadcasted_iota(jnp.int32, (span, span), 1)
    shuffle = jnp.where(goes == z % 2 * SUB + z // 2, 1.0, 0.0).astype(BF16)
    lined = raw[...].reshape(rows * raw.shape[1], span).astype(F32).astype(BF16)
    lined = jnp.dot(lined, shuffle, preferred_element_type=F32).astype(jnp.int32)
    raw[...] = lined.reshape(rows, raw.shape[1], span)
    for y in range(raw.shape[1]):
        flat[:, y * span : (y + 1) * span] = raw[:, y, :]
    for r in range(rows):
        place = jnp.where(mirrored > 0, rows - 1 - r, r)
        codes[r : r + 1, :] = flat[pl.ds(place, 1), :]
    half = len(copies) // 2
    for copy in copies[:half]:
        copy.wait()
    unstage(near_cross, cross)
    for copy in copies[half:]:
        copy.wait()


def inner_kernel(relax, rows, *refs):
    if relax:
        (m_cross, m_mid, m_in, params, table, factor, coef_ref, weights,
         cross, middle, inside, out, e_cross, e_in, f_cross, f_in, sums,
         wide, tall, kept) = refs
        spread_features([params[k] for k in range(6)], wide, tall, rows)
        group = [(r, m_cross.at[r], into(cross.at[r])) for r in range(2)]
        group += [(rows - 2 + r, m_in.at[r], into(inside.at[r])) for r in range(2)]
        relax_group(group, tall, table, factor, kept)
        for first in range(0, rows - 4, 4):
            group = [
                (2 + r, m_mid.at[r], into(middle.at[r]))
                for r in range(first, min(first + 4, rows - 4))
            ]
            relax_group(group, tall, table, factor, kept)
    else:
        (cross, near_inside, state, coef_ref, weights, middle, inside, out, e_cross, e_in,
         f_cross, f_in, sums, near, sems) = refs
        mirrored = lax.axis_index("gx") % 2
        copies = row_copies(mirrored, state, near, 2, sems)
        for copy in copies:
            copy.start()
    yz_rows(cross, e_cross, True, 2, coef_ref)
    if not relax:
        unstage(near_inside, inside)
    yz_rows(inside, e_in, True, 2, coef_ref)
    if not relax:
        for copy in copies:
            copy.wait()
        unstage(near, middle)
    chunks = middle.shape[-1] // LANES
    inner = rows - 4

    def along_x(i, carry):
        chunk, y = i // 16, i % 16
        lanes = lanes_of(chunk)
        coef = coefs_of(coef_ref, lanes)
        for t in range(2):
            cells = {}
            for n in range(rows):
                if n < 2:
                    cells[n] = cross[n, y, t, :, lanes]
                elif n < rows - 2:
                    cells[n] = middle[n - 2, y, t, :, lanes]
                else:
                    cells[n] = inside[n - rows + 2, y, t, :, lanes]

            def store(n, v, t=t):
                out[n - 2, y, t, :, lanes] = v

            faces = x_row(cells, list(range(2, rows - 2)), store, coef)
            for n in range(2):
                f_cross[n, y, t, :, lanes] = faces[1 + n]
                f_in[n, y, t, :, lanes] = faces[rows - 3 + n]
        return carry

    lax.fori_loop(0, chunks * 16, along_x, 0, unroll=4)
    yz_rows(middle, out, False, inner, coef_ref)
    row_moments([(out.at[r], r) for r in range(inner)], weights, sums)


def presence(line):
    place = lax.axis_index("gx")
    return jnp.where((place == 0) | (place == line - 1), 0.0, 1.0)


def cross_x(low, cross, known, before, out, y, t, lanes, coef, present):
    cells = {}
    for n in range(2):
        cells[-1 - n] = low[n, y, t, :, lanes] * present
        cells[n] = cross[n, y, t, :, lanes]

    def store(n, v):
        out[n, y, t, :, lanes] = before[n, y, t, :, lanes] - v

    x_row(cells, [0, 1], store, coef, True, {1 + n: known[n, y, t, :, lanes] for n in range(2)})


def in_x(high, inside, known, before, out, y, t, lanes, coef):
    cells = {}
    for n in range(2):
        cells[n] = inside[n, y, t, :, lanes]
        cells[2 + n] = high[1 - n, y, t, :, lanes]

    def store(n, v):
        out[n, y, t, :, lanes] = before[n, y, t, :, lanes] - v

    x_row(cells, [0, 1], store, coef, True, {n - 1: known[n, y, t, :, lanes] for n in range(2)})


def each_place(width, coef_ref, work):
    def one(i, carry):
        lanes = lanes_of(i // 16)
        coef = coefs_of(coef_ref, lanes)
        for t in range(2):
            work(i % 16, t, lanes, coef)
        return carry

    lax.fori_loop(0, width // LANES * 16, one, 0, unroll=4)


def first_in_kernel(near_high, inside, e_in, f_in, coef_ref, weights, out, sums, high):
    unstage(near_high, high)
    each_place(
        out.shape[-1], coef_ref, lambda *at: in_x(high, inside, f_in, e_in, out, *at)
    )
    row_moments([(out.at[r], r) for r in range(2)], weights, sums)


def first_cross_kernel(line, low, cross, e_cross, f_cross, coef_ref, weights, inner_sums, in_sums,
                       out, sums):
    present = presence(line)
    each_place(
        out.shape[-1],
        coef_ref,
        lambda *at: cross_x(low, cross, f_cross, e_cross, out, *at, present),
    )
    rows = sums.shape[1]
    for m in range(5):
        sums[m, 2 : rows - 2, :] = inner_sums[m]
        sums[m, rows - 2 :, :] = in_sums[m]
    row_moments([(out.at[r], r) for r in range(2)], weights, sums)


def edge_kernel(rows, line, h_cross, h_in, p_cross, p_in, table, factor, cross, inside,
                e_cross, e_in, f_cross, f_in, coef_ref, weights, inner_sums, out_cross, out_in, sums,
                wide, tall, kept, low, high):
    params = [jnp.concatenate([p_cross[k], p_in[k]], axis=0) for k in range(6)]
    spread_features(params, wide, tall, 4)
    group = [(r, h_cross.at[r], into(low.at[r])) for r in range(2)]
    group += [(2 + r, h_in.at[r], into(high.at[r])) for r in range(2)]
    relax_group(group, tall, table, factor, kept)
    present = presence(line)

    def work(*at):
        cross_x(low, cross, f_cross, e_cross, out_cross, *at, present)
        in_x(high, inside, f_in, e_in, out_in, *at)

    each_place(out_in.shape[-1], coef_ref, work)
    for m in range(5):
        sums[m, 2 : rows - 2, :] = inner_sums[m]
    edges = [(out_cross.at[r], r) for r in range(2)]
    edges += [(out_in.at[r], rows - 2 + r) for r in range(2)]
    row_moments(edges, weights, sums)


def final_kernel(rows, m_cross, m_mid, m_in, params, table, factor, out,
                 wide, tall, kept, staged, sems):
    mirrored = lax.axis_index("gx") % 2
    spread_features([params[k] for k in range(6)], wide, tall, rows)
    moved = [m_cross.at[r] for r in range(2)] + [m_mid.at[r] for r in range(rows - 4)]
    moved += [m_in.at[r] for r in range(2)]
    copies = []
    for first in range(0, rows, 2):
        near = staged.at[pl.ds(first, 2)]
        group = []
        for r in range(2):

            def store(chunk, v, row=near.at[r]):
                for y in range(16):
                    for t in range(2):
                        row[y, chunk, pl.ds(t, SUB, stride=2), :] = v[y, t]

            group.append((first + r, moved[first + r], store))
        relax_group(group, tall, table, factor, kept)
        more = row_copies(mirrored, out, near, first, sems.at[pl.ds(first, 2)], True)
        for copy in more:
            copy.start()
        copies += more
    for copy in copies:
        copy.wait()


def body(distribution, velocity_order, cell_codes, knudsen, inflow):
    rows, count_y, count_z, width = distribution.shape
    peers = lax.axis_size("vert")
    line = lax.axis_size("gx")
    total = width * peers
    cells = count_y * count_z
    chunks = width // LANES

    vmem = pl.BlockSpec(memory_space=pltpu.VMEM)
    smem = pl.BlockSpec(memory_space=pltpu.SMEM)
    hbm = pl.BlockSpec(memory_space=pltpu.HBM)

    def slab(n):
        return jax.ShapeDtypeStruct((n, count_y, 2, SUB, width), F32)

    def slab_scratch(n):
        return pltpu.VMEM((n, count_y, 2, SUB, width), F32)

    def feature_scratch(n):
        return [
            pltpu.VMEM((n, FEATURES, cells), F32),
            pltpu.VMEM((n, cells, FEATURES), BF16),
            pltpu.VMEM((4, count_y, 2, SUB, LANES), F32),
        ]

    def staging(n):
        return [
            pltpu.VMEM((n, count_y, chunks, count_z, LANES), F32),
            pltpu.SemaphoreType.DMA((n, chunks)),
        ]

    def limits(mib):
        return pltpu.CompilerParams(vmem_limit_bytes=mib * 1024 * 1024)

    def in_hbm(array):
        return pltpu.with_memory_space_constraint(array, pltpu.HBM)

    def load():
        return pl.pallas_call(
            load_kernel,
            in_specs=[hbm] * 3,
            out_specs=[vmem] * 7,
            out_shape=[
                slab(2),
                jax.ShapeDtypeStruct((2, count_y, chunks, count_z, LANES), F32),
                jax.ShapeDtypeStruct((rows, cells), jnp.int32),
                jax.ShapeDtypeStruct((FEATURES, width), BF16),
                jax.ShapeDtypeStruct((FEATURES, LANES), BF16),
                jax.ShapeDtypeStruct((16, 2 * width), BF16),
                jax.ShapeDtypeStruct((9, SUB, width), F32),
            ],
            scratch_shapes=[
                pltpu.VMEM((1, width), jnp.int32),
                pltpu.VMEM((rows, count_y, count_z), jnp.int32),
                pltpu.VMEM((rows, cells), jnp.int32),
                staging(2)[0],
                staging(2)[1],
                staging(2)[1],
                pltpu.SemaphoreType.DMA((2,)),
            ],
            compiler_params=limits(6),
            name="load_edges",
        )(in_hbm(velocity_order.reshape(1, width)), in_hbm(cell_codes), in_hbm(distribution))

    def inner(relax, state, params):
        sums = jax.ShapeDtypeStruct((5, rows - 4, cells), F32)
        out_shape = [slab(rows - 4)] + [slab(2)] * 4 + [sums]
        scratch = []
        if relax:
            out_shape = [slab(2), slab(rows - 4), slab(2)] + out_shape
            scratch = feature_scratch(rows)
            args = (*state, params, table, factor, coef, weights)
        else:
            out_shape = [slab(rows - 4), slab(2)] + out_shape
            scratch = staging(rows - 4)
            args = (*state, coef, weights)
        return pl.pallas_call(
            functools.partial(inner_kernel, relax, rows),
            in_specs=[vmem if relax or n != 2 else hbm for n in range(len(args))],
            out_specs=[vmem] * len(out_shape),
            out_shape=out_shape,
            scratch_shapes=scratch,
            compiler_params=limits(LIMIT_MIB),
            name="inner_relax" if relax else "inner_first",
        )(*args)

    whole_sums = jax.ShapeDtypeStruct((5, rows, cells), F32)
    edge_sums = jax.ShapeDtypeStruct((5, 2, cells), F32)

    def first_in(*args):
        return pl.pallas_call(
            first_in_kernel,
            in_specs=[vmem] * 6,
            out_specs=[vmem] * 2,
            out_shape=[slab(2), edge_sums],
            scratch_shapes=[slab_scratch(2)],
            compiler_params=limits(LIMIT_MIB),
            name="first_in",
        )(*args, coef, weights)

    def first_cross(*args):
        return pl.pallas_call(
            functools.partial(first_cross_kernel, line),
            in_specs=[vmem] * 8,
            out_specs=[vmem] * 2,
            out_shape=[slab(2), whole_sums],
            compiler_params=limits(LIMIT_MIB),
            name="first_cross",
        )(*args)

    def edge(halos, params, edges, sums):
        args = (*halos, *params, table, factor, *edges, coef, weights, sums)
        return pl.pallas_call(
            functools.partial(edge_kernel, rows, line),
            in_specs=[vmem] * len(args),
            out_specs=[vmem] * 3,
            out_shape=[slab(2), slab(2), whole_sums],
            scratch_shapes=feature_scratch(4) + [slab_scratch(2)] * 2,
            compiler_params=limits(LIMIT_MIB),
            name="edge_relax",
        )(*args)

    def cell_params(parts, *sizes):
        return pl.pallas_call(
            functools.partial(param_kernel, total, len(parts)),
            in_specs=[vmem] * (len(parts) + 1) + [smem, smem],
            out_specs=[vmem] * len(sizes),
            out_shape=[jax.ShapeDtypeStruct((6, n, cells), F32) for n in sizes],
            compiler_params=limits(4),
            name="cell_params",
        )(*parts, codes, knudsen, inflow)

    def final(moved, params):
        return pl.pallas_call(
            functools.partial(final_kernel, rows),
            in_specs=[vmem] * 6,
            out_specs=hbm,
            out_shape=jax.ShapeDtypeStruct(distribution.shape, F32),
            scratch_shapes=feature_scratch(rows) + staging(rows),
            compiler_params=limits(LIMIT_MIB),
            name="final_relax",
        )(*moved, params, table, factor)

    parts = lax.axis_size("groups")
    across = []
    for p in range(parts):
        for i in (0, line - 1):
            other = p ^ 1 if (p ^ 1) < parts else p
            across.append((p * line + i, other * line + i))
        for i in range(1, line - 1, 2):
            across += [(p * line + i, p * line + i + 1), (p * line + i + 1, p * line + i)]
    within = []
    for i in range(0, line, 2):
        within += [(i, i + 1), (i + 1, i)]

    def exchange(cross, inside):
        return (
            lax.ppermute(cross, ("groups", "gx"), across),
            lax.ppermute(inside, "gx", within),
        )

    def gather(part):
        parts = [part]
        for shift in range(1, peers):
            pairs = [(i, (i + shift) % peers) for i in range(peers)]
            parts.append(lax.ppermute(part, "vert", pairs))
        return parts

    cross, near_inside, codes, table, factor, weights, coef = load()
    low, near_high = exchange(cross, near_inside)
    _, inside, m_mid, e_cross, e_in, f_cross, f_in, sums = inner(
        False, (cross, near_inside, in_hbm(distribution)), None
    )
    m_in, in_sums = first_in(near_high, inside, e_in, f_in)
    m_cross, sums = first_cross(low, cross, e_cross, f_cross, coef, weights, sums, in_sums)
    m_cross, m_in, sums = lax.optimization_barrier((m_cross, m_in, sums))
    for _ in range(1, STEPS):
        halos = exchange(m_cross, m_in)
        params, p_cross, p_in = cell_params(gather(sums), rows, 2, 2)
        p_halos = exchange(p_cross, p_in)
        moved = (m_cross, m_mid, m_in)
        cross, _, inside, m_mid, e_cross, e_in, f_cross, f_in, sums = inner(True, moved, params)
        edges = (cross, inside, e_cross, e_in, f_cross, f_in)
        m_cross, m_in, sums = edge(halos, p_halos, edges, sums)
    (params,) = cell_params(gather(sums), rows)
    return final((m_cross, m_mid, m_in), params)


def solution(mesh):
    placed = (
        P(("groups", "gx"), None, None, "vert"),
        P("vert"),
        P(("groups", "gx"), None, None),
        P("groups"),
        P("groups"),
    )
    return jax.shard_map(
        body,
        mesh=mesh,
        in_specs=placed,
        out_specs=P(("groups", "gx"), None, None, "vert"),
        check_vma=False,
    )
```

```python
import functools

import jax
import jax.numpy as jnp
from jax import lax
from jax.experimental import pallas as pl
from jax.experimental.pallas import tpu as pltpu
from jax.sharding import PartitionSpec as P

VGX = 16
VGY = 16
VGZ = 8
STEPS = 3
LANES = 128
SUB = 8
FEATURES = 32
PAIR = 2 * LANES
UNIT = 3.0 / 16.0
LOG2E = 1.4426950408889634
LIMIT_MIB = 10
F32 = jnp.float32
BF16 = jnp.bfloat16


def minmod(lower, upper):
    return jnp.maximum(
        jnp.minimum(lower, upper), jnp.minimum(jnp.maximum(lower, upper), 0.0)
    )


def lanes_of(chunk):
    return pl.ds(pl.multiple_of(chunk * LANES, LANES), LANES)


def coefs_of(coef_ref, lanes):
    return [coef_ref[k, :, lanes] for k in range(9)]


def x_row(cells, rows, store, coef, change=False):
    reach, lean, ahead = coef[0], coef[1], coef[2] > 0.0
    first, last = rows[0], rows[-1]
    steps = {n: cells[n + 1] - cells[n] for n in range(first - 2, last + 2)}
    faces = {
        n: cells[n] + lean * minmod(steps[n - 1], steps[n])
        for n in range(first - 1, last + 2)
    }
    for n in rows:
        source = jnp.where(ahead, faces[n - 1], faces[n + 1])
        v = reach * (faces[n] - source)
        store(n, v if change else cells[n] - v)


def yz_row(source, out, fresh, row, lanes, coef):
    reach_y, lean_y, ahead_y = coef[3], coef[4], coef[5] > 0.0
    reach_z, lean_z, ahead_z = coef[6], coef[7], coef[8] > 0.0
    count = 16
    cells, steps, faces = {}, {}, {}

    def cell(y, t):
        y %= count
        if (y, t) not in cells:
            cells[y, t] = source[row, y, t, :, lanes]
        return cells[y, t]

    def step(y, t):
        y %= count
        if (y, t) not in steps:
            steps[y, t] = cell(y + 1, t) - cell(y, t)
        return steps[y, t]

    def face(y, t):
        y %= count
        if (y, t) not in faces:
            faces[y, t] = cell(y, t) + lean_y * minmod(step(y - 1, t), step(y, t))
        return faces[y, t]

    def up(v):
        return pltpu.roll(v, SUB - 1, 0)

    def down(v):
        return pltpu.roll(v, 1, 0)

    for y in range(count):
        even, odd = cell(y, 0), cell(y, 1)
        step_even = odd - even
        step_odd = up(even) - odd
        face_even = even + lean_z * minmod(down(step_odd), step_even)
        face_odd = odd + lean_z * minmod(step_even, step_odd)
        winds = (
            jnp.where(ahead_z, down(face_odd), face_odd),
            jnp.where(ahead_z, face_even, up(face_even)),
        )
        for t, z_face in enumerate((face_even, face_odd)):
            v = cell(y, t) if fresh else out[row, y, t, :, lanes]
            v -= reach_z * (z_face - winds[t])
            upwind = jnp.where(ahead_y, face(y - 1, t), face(y + 1, t))
            v -= reach_y * (face(y, t) - upwind)
            out[row, y, t, :, lanes] = v


def yz_rows(source, out, fresh, rows, coef_ref):
    chunks = source.shape[-1] // LANES

    def one(i, carry):
        chunk, row = i // rows, i % rows
        lanes = lanes_of(chunk)
        yz_row(source, out, fresh, row, lanes, coefs_of(coef_ref, lanes))
        return carry

    lax.fori_loop(0, chunks * rows, one, 0, unroll=2)


def row_moments(rows, weights, sums):
    for row, place in rows:
        flat = row[...].reshape(256, row.shape[-1])
        high = flat.astype(BF16)
        rest = (flat - high.astype(F32)).astype(BF16)
        both = jnp.concatenate([high, rest], axis=1)
        contract = (((1,), (1,)), ((), ()))
        part = lax.dot_general(weights[...], both, contract, preferred_element_type=F32)
        for m in range(4):
            sums[m, place : place + 1, :] = part[m : m + 1]
        sums[4, place : place + 1, :] = part[4:5] + part[5:6]


def three_parts(value):
    high = value.astype(BF16).astype(F32)
    rest = value - high
    middle = rest.astype(BF16).astype(F32)
    low = (rest - middle).astype(BF16).astype(F32)
    return high, middle, low


def spread_features(params, wide, tall, rows, first=0):
    alpha, beta_x, beta_y, beta_z, gamma, keep = params
    alpha = jnp.where(gamma == 0.0, -10000.0, alpha)
    zero = jnp.zeros_like(alpha)
    columns = []
    for value in (alpha, beta_x, beta_y, beta_z, gamma, gamma, keep):
        columns.extend(three_parts(value))
    columns.extend([zero] * (FEATURES - len(columns)))
    for k, value in enumerate(columns):
        for half in range(2):
            part = value[:, half * LANES : (half + 1) * LANES]
            wide[half, pl.ds(k, rows, stride=FEATURES), :] = part
    for r in range(rows):
        for half in range(2):
            block = wide[half, r * FEATURES : (r + 1) * FEATURES, :]
            tall[first + r, half * LANES : (half + 1) * LANES, :] = block.T.astype(BF16)


def relax_group(group, tall, table, factor, kept):
    for u, (place, _, _) in enumerate(group):
        keep = jnp.dot(tall[place], factor[...], preferred_element_type=F32)
        kept[u] = keep.reshape(16, 2, SUB, LANES)
    for u, (place, moved, store) in enumerate(group):
        for pair in range(moved.shape[-1] // PAIR):
            columns = table[:, pair * PAIR : (pair + 1) * PAIR]
            power = jnp.dot(tall[place], columns, preferred_element_type=F32)
            for half in range(2):
                chunk = 2 * pair + half
                shape = jnp.exp2(power[:, half * LANES : (half + 1) * LANES])
                shape = shape.reshape(16, 2, SUB, LANES)
                lanes = pl.ds(chunk * LANES, LANES)
                store(chunk, kept[u] * moved[:, :, :, lanes] + shape)


def into(row):
    def store(chunk, v):
        row[:, :, :, pl.ds(chunk * LANES, LANES)] = v

    return store


def param_kernel(total, count, *refs):
    parts = refs[:count]
    codes, knudsen, inflow, out, *edges = refs[count:]
    sums = [parts[0][m] for m in range(5)]
    for part in parts[1:]:
        sums = [s + part[m] for m, s in enumerate(sums)]
    density = sums[0] * (1.0 / total)
    scale = UNIT / sums[0]
    u_x, u_y, u_z = (sums[m] * scale for m in (1, 2, 3))
    heat = (UNIT * sums[4] * scale - (u_x * u_x + u_y * u_y + u_z * u_z)) * (1.0 / 3.0)
    rate = 0.5 * density / (density + knudsen[0])
    code = codes[...]
    flowing, wall = code == 1, code == 2
    closed = flowing | wall
    u_x = jnp.where(flowing, inflow[1], jnp.where(wall, 0.0, u_x))
    u_y = jnp.where(closed, 0.0, u_y)
    u_z = jnp.where(closed, 0.0, u_z)
    heat = jnp.where(flowing, inflow[2], jnp.where(wall, inflow[3], heat))
    amount = jnp.where(flowing, inflow[0], jnp.where(wall, density, rate * density))
    keep = jnp.where(closed, 0.0, 1.0 - rate)
    g = (-0.5 * LOG2E) / heat

    def line(u, n, unit):
        s = None
        for i in range(n):
            gap = (i + 0.5 - n / 2) * unit - u
            e = jnp.exp2(g * (gap * gap))
            s = e if s is None else s + e
        return s

    norm = line(u_x, VGX, 6.0 / VGX) * line(u_y, VGY, 6.0 / VGY)
    norm = norm * line(u_z, VGZ, 6.0 / VGZ) * (1.0 / total)
    alpha = (jnp.log(amount) - jnp.log(norm)) * LOG2E
    alpha = alpha + g * (u_x * u_x + u_y * u_y + u_z * u_z)
    lean = (-2.0 * UNIT) * g
    params = (alpha, lean * u_x, lean * u_y, lean * u_z, g * (UNIT * UNIT), keep)
    rows = code.shape[0]
    for k, value in enumerate(params):
        out[k] = value
        if edges:
            edges[0][k] = value[:2]
            edges[1][k] = value[rows - 2 :]


def row_copies(mirrored, whole, staged, first, sems, out=False):
    rows = whole.shape[0]
    copies = []
    for n in range(staged.shape[0]):
        place = jnp.where(mirrored > 0, rows - 1 - first - n, first + n)
        for c in range(staged.shape[2]):
            far = whole.at[place, :, :, pl.ds(c * LANES, LANES)]
            near = staged.at[n, :, c]
            pair = (near, far) if out else (far, near)
            copies.append(pltpu.make_async_copy(*pair, sems.at[n, c]))
    return copies


def unstage(staged, out):
    count = staged.shape[1]

    def one(i, carry):
        n, y = i // count, i % count
        for c in range(staged.shape[2]):
            for t in range(2):
                v = staged[n, y, c, pl.ds(t, SUB, stride=2), :]
                out[n, y, t, :, pl.ds(c * LANES, LANES)] = v
        return carry

    lax.fori_loop(0, staged.shape[0] * count, one, 0, unroll=4)


def load_kernel(order_in, codes_in, state, cross, near_inside, codes, table, factor, weights, coef,
                order, raw, flat, near_cross, cross_sems, inside_sems, more_sems):
    rows, width = state.shape[0], order.shape[-1]
    mirrored = lax.axis_index("gx") % 2
    more = [
        pltpu.make_async_copy(order_in, order, more_sems.at[0]),
        pltpu.make_async_copy(codes_in, raw, more_sems.at[1]),
    ]
    copies = row_copies(mirrored, state, near_cross, 0, cross_sems)
    copies += row_copies(mirrored, state, near_inside, rows - 2, inside_sems)
    for copy in more + copies:
        copy.start()
    for copy in more:
        copy.wait()

    slots = jnp.broadcast_to(order[...], (SUB, width))
    n_x = 2 * (slots // (VGY * VGZ)) - (VGX - 1)
    n_y = 2 * (slots // VGZ % VGY) - (VGY - 1)
    n_z = 2 * (2 * (slots % VGZ) - (VGZ - 1))
    square = n_x * n_x + n_y * n_y + n_z * n_z
    low_part = square % 8
    whole = [n.astype(F32) for n in (n_x, n_y, n_z, square - low_part, low_part)]
    whole = [jnp.ones_like(whole[0])] + whole

    def pick(values, index):
        out = jnp.zeros_like(values[0])
        for k, value in enumerate(values):
            out = jnp.where(index == k, value, out)
        return out

    line = lax.broadcasted_iota(jnp.int32, (SUB, width), 0)
    moments = jnp.concatenate([pick(whole, line), jnp.zeros((SUB, width), F32)], axis=0)
    moments = moments.astype(BF16)
    weights[:, :width] = moments
    weights[:, width:] = moments
    table[...] = jnp.concatenate(
        [pick(whole, (line + SUB * g) // 3) for g in range(FEATURES // SUB)], axis=0
    ).astype(BF16)
    slot = lax.broadcasted_iota(jnp.int32, (FEATURES, LANES), 0)
    factor[...] = jnp.where((slot >= 18) & (slot < 21), 1.0, 0.0).astype(BF16)
    turn = jnp.where(mirrored > 0, -1.0, 1.0)
    for k, (n, scale) in enumerate(
        ((whole[1] * turn, 0.1), (whole[2], 1.0 / 30.0), (whole[3], 1.0 / 30.0))
    ):
        reach = jnp.abs(n * UNIT * scale)
        sign = jnp.where(n > 0.0, 1.0, -1.0)
        coef[3 * k] = reach
        coef[3 * k + 1] = 0.5 * sign * (1.0 - reach)
        coef[3 * k + 2] = sign

    span = raw.shape[2]
    z = lax.broadcasted_iota(jnp.int32, (span, span), 0)
    goes = lax.broadcasted_iota(jnp.int32, (span, span), 1)
    shuffle = jnp.where(goes == z % 2 * SUB + z // 2, 1.0, 0.0).astype(BF16)
    lined = raw[...].reshape(rows * raw.shape[1], span).astype(F32).astype(BF16)
    lined = jnp.dot(lined, shuffle, preferred_element_type=F32).astype(jnp.int32)
    raw[...] = lined.reshape(rows, raw.shape[1], span)
    for y in range(raw.shape[1]):
        flat[:, y * span : (y + 1) * span] = raw[:, y, :]
    for r in range(rows):
        place = jnp.where(mirrored > 0, rows - 1 - r, r)
        codes[r : r + 1, :] = flat[pl.ds(place, 1), :]
    half = len(copies) // 2
    for copy in copies[:half]:
        copy.wait()
    unstage(near_cross, cross)
    for copy in copies[half:]:
        copy.wait()


def inner_kernel(relax, rows, *refs):
    if relax:
        (m_cross, m_mid, m_in, params, table, factor, coef_ref, weights,
         cross, middle, inside, out, e_cross, e_in, sums, wide, tall, kept) = refs
        spread_features([params[k] for k in range(6)], wide, tall, rows)
        group = [(r, m_cross.at[r], into(cross.at[r])) for r in range(2)]
        group += [(rows - 2 + r, m_in.at[r], into(inside.at[r])) for r in range(2)]
        relax_group(group, tall, table, factor, kept)
        for first in range(0, rows - 4, 4):
            group = [
                (2 + r, m_mid.at[r], into(middle.at[r]))
                for r in range(first, min(first + 4, rows - 4))
            ]
            relax_group(group, tall, table, factor, kept)
    else:
        (cross, near_inside, state, coef_ref, weights, middle, inside, out, e_cross, e_in, sums,
         near, sems) = refs
        mirrored = lax.axis_index("gx") % 2
        copies = row_copies(mirrored, state, near, 2, sems)
        for copy in copies:
            copy.start()
    yz_rows(cross, e_cross, True, 2, coef_ref)
    if not relax:
        unstage(near_inside, inside)
    yz_rows(inside, e_in, True, 2, coef_ref)
    if not relax:
        for copy in copies:
            copy.wait()
        unstage(near, middle)
    chunks = middle.shape[-1] // LANES
    inner = rows - 4

    def along_x(i, carry):
        chunk, y = i // 16, i % 16
        lanes = lanes_of(chunk)
        coef = coefs_of(coef_ref, lanes)
        for t in range(2):
            cells = {}
            for n in range(rows):
                if n < 2:
                    cells[n] = cross[n, y, t, :, lanes]
                elif n < rows - 2:
                    cells[n] = middle[n - 2, y, t, :, lanes]
                else:
                    cells[n] = inside[n - rows + 2, y, t, :, lanes]

            def store(n, v, t=t):
                out[n - 2, y, t, :, lanes] = v

            x_row(cells, list(range(2, rows - 2)), store, coef)
        return carry

    lax.fori_loop(0, chunks * 16, along_x, 0, unroll=4)
    yz_rows(middle, out, False, inner, coef_ref)
    row_moments([(out.at[r], r) for r in range(inner)], weights, sums)


def presence(line):
    place = lax.axis_index("gx")
    return jnp.where((place == 0) | (place == line - 1), 0.0, 1.0)


def cross_x(low, cross, middle, before, out, y, t, lanes, coef, present):
    cells = {}
    for n in range(2):
        cells[-1 - n] = low[n, y, t, :, lanes] * present
        cells[n] = cross[n, y, t, :, lanes]
        cells[2 + n] = middle[n, y, t, :, lanes]

    def store(n, v):
        out[n, y, t, :, lanes] = before[n, y, t, :, lanes] - v

    x_row(cells, [0, 1], store, coef, True)


def in_x(high, inside, middle, before, out, y, t, lanes, coef):
    last = middle.shape[0]
    cells = {}
    for n in range(2):
        cells[n] = middle[last - 2 + n, y, t, :, lanes]
        cells[2 + n] = inside[n, y, t, :, lanes]
        cells[4 + n] = high[1 - n, y, t, :, lanes]

    def store(n, v):
        out[n - 2, y, t, :, lanes] = before[n - 2, y, t, :, lanes] - v

    x_row(cells, [2, 3], store, coef, True)


def each_place(middle, coef_ref, work):
    def one(i, carry):
        lanes = lanes_of(i // 16)
        coef = coefs_of(coef_ref, lanes)
        for t in range(2):
            work(i % 16, t, lanes, coef)
        return carry

    lax.fori_loop(0, middle.shape[-1] // LANES * 16, one, 0, unroll=4)


def first_in_kernel(near_high, inside, e_in, middle, coef_ref, weights, out, sums, high):
    unstage(near_high, high)
    each_place(middle, coef_ref, lambda *at: in_x(high, inside, middle, e_in, out, *at))
    row_moments([(out.at[r], r) for r in range(2)], weights, sums)


def first_cross_kernel(line, low, cross, e_cross, middle, coef_ref, weights, inner_sums, in_sums,
                       out, sums):
    present = presence(line)
    each_place(
        middle, coef_ref, lambda *at: cross_x(low, cross, middle, e_cross, out, *at, present)
    )
    rows = sums.shape[1]
    for m in range(5):
        sums[m, 2 : rows - 2, :] = inner_sums[m]
        sums[m, rows - 2 :, :] = in_sums[m]
    row_moments([(out.at[r], r) for r in range(2)], weights, sums)


def edge_kernel(rows, line, h_cross, h_in, p_cross, p_in, table, factor, cross, middle, inside,
                e_cross, e_in, coef_ref, weights, inner_sums, out_cross, out_in, sums,
                wide, tall, kept, low, high):
    params = [jnp.concatenate([p_cross[k], p_in[k]], axis=0) for k in range(6)]
    spread_features(params, wide, tall, 4)
    group = [(r, h_cross.at[r], into(low.at[r])) for r in range(2)]
    group += [(2 + r, h_in.at[r], into(high.at[r])) for r in range(2)]
    relax_group(group, tall, table, factor, kept)
    present = presence(line)

    def work(*at):
        cross_x(low, cross, middle, e_cross, out_cross, *at, present)
        in_x(high, inside, middle, e_in, out_in, *at)

    each_place(middle, coef_ref, work)
    for m in range(5):
        sums[m, 2 : rows - 2, :] = inner_sums[m]
    edges = [(out_cross.at[r], r) for r in range(2)]
    edges += [(out_in.at[r], rows - 2 + r) for r in range(2)]
    row_moments(edges, weights, sums)


def final_kernel(rows, m_cross, m_mid, m_in, params, table, factor, out,
                 wide, tall, kept, staged, sems):
    mirrored = lax.axis_index("gx") % 2
    moved = [m_cross.at[r] for r in range(2)] + [m_mid.at[r] for r in range(rows - 4)]
    moved += [m_in.at[r] for r in range(2)]
    copies = []
    for first in range(0, rows, 2):
        near = staged.at[pl.ds(first, 2)]
        spread_features([params[k, first : first + 2] for k in range(6)], wide, tall, 2, first)
        group = []
        for r in range(2):

            def store(chunk, v, row=near.at[r]):
                for y in range(16):
                    for t in range(2):
                        row[y, chunk, pl.ds(t, SUB, stride=2), :] = v[y, t]

            group.append((first + r, moved[first + r], store))
        relax_group(group, tall, table, factor, kept)
        more = row_copies(mirrored, out, near, first, sems.at[pl.ds(first, 2)], True)
        for copy in more:
            copy.start()
        copies += more
    for copy in copies:
        copy.wait()


def body(distribution, velocity_order, cell_codes, knudsen, inflow):
    rows, count_y, count_z, width = distribution.shape
    peers = lax.axis_size("vert")
    line = lax.axis_size("gx")
    total = width * peers
    cells = count_y * count_z
    chunks = width // LANES

    vmem = pl.BlockSpec(memory_space=pltpu.VMEM)
    smem = pl.BlockSpec(memory_space=pltpu.SMEM)
    hbm = pl.BlockSpec(memory_space=pltpu.HBM)

    def slab(n):
        return jax.ShapeDtypeStruct((n, count_y, 2, SUB, width), F32)

    def slab_scratch(n):
        return pltpu.VMEM((n, count_y, 2, SUB, width), F32)

    def feature_scratch(n):
        return [
            pltpu.VMEM((2, n * FEATURES, LANES), F32),
            pltpu.VMEM((n, cells, FEATURES), BF16),
            pltpu.VMEM((4, count_y, 2, SUB, LANES), F32),
        ]

    def staging(n):
        return [
            pltpu.VMEM((n, count_y, chunks, count_z, LANES), F32),
            pltpu.SemaphoreType.DMA((n, chunks)),
        ]

    def limits(mib):
        return pltpu.CompilerParams(vmem_limit_bytes=mib * 1024 * 1024)

    def in_hbm(array):
        return pltpu.with_memory_space_constraint(array, pltpu.HBM)

    def load():
        return pl.pallas_call(
            load_kernel,
            in_specs=[hbm] * 3,
            out_specs=[vmem] * 7,
            out_shape=[
                slab(2),
                jax.ShapeDtypeStruct((2, count_y, chunks, count_z, LANES), F32),
                jax.ShapeDtypeStruct((rows, cells), jnp.int32),
                jax.ShapeDtypeStruct((FEATURES, width), BF16),
                jax.ShapeDtypeStruct((FEATURES, LANES), BF16),
                jax.ShapeDtypeStruct((16, 2 * width), BF16),
                jax.ShapeDtypeStruct((9, SUB, width), F32),
            ],
            scratch_shapes=[
                pltpu.VMEM((1, width), jnp.int32),
                pltpu.VMEM((rows, count_y, count_z), jnp.int32),
                pltpu.VMEM((rows, cells), jnp.int32),
                staging(2)[0],
                staging(2)[1],
                staging(2)[1],
                pltpu.SemaphoreType.DMA((2,)),
            ],
            compiler_params=limits(6),
            name="load_edges",
        )(in_hbm(velocity_order.reshape(1, width)), in_hbm(cell_codes), in_hbm(distribution))

    def inner(relax, state, params):
        sums = jax.ShapeDtypeStruct((5, rows - 4, cells), F32)
        out_shape = [slab(rows - 4), slab(2), slab(2), sums]
        scratch = []
        if relax:
            out_shape = [slab(2), slab(rows - 4), slab(2)] + out_shape
            scratch = feature_scratch(rows)
            args = (*state, params, table, factor, coef, weights)
        else:
            out_shape = [slab(rows - 4), slab(2)] + out_shape
            scratch = staging(rows - 4)
            args = (*state, coef, weights)
        return pl.pallas_call(
            functools.partial(inner_kernel, relax, rows),
            in_specs=[vmem if relax or n != 2 else hbm for n in range(len(args))],
            out_specs=[vmem] * len(out_shape),
            out_shape=out_shape,
            scratch_shapes=scratch,
            compiler_params=limits(LIMIT_MIB),
            name="inner_relax" if relax else "inner_first",
        )(*args)

    whole_sums = jax.ShapeDtypeStruct((5, rows, cells), F32)
    edge_sums = jax.ShapeDtypeStruct((5, 2, cells), F32)

    def first_in(*args):
        return pl.pallas_call(
            first_in_kernel,
            in_specs=[vmem] * 6,
            out_specs=[vmem] * 2,
            out_shape=[slab(2), edge_sums],
            scratch_shapes=[slab_scratch(2)],
            compiler_params=limits(LIMIT_MIB),
            name="first_in",
        )(*args, middle, coef, weights)

    def first_cross(*args):
        return pl.pallas_call(
            functools.partial(first_cross_kernel, line),
            in_specs=[vmem] * 8,
            out_specs=[vmem] * 2,
            out_shape=[slab(2), whole_sums],
            compiler_params=limits(LIMIT_MIB),
            name="first_cross",
        )(*args)

    def edge(halos, params, state, edges, sums):
        args = (*halos, *params, table, factor, *state, *edges, coef, weights, sums)
        return pl.pallas_call(
            functools.partial(edge_kernel, rows, line),
            in_specs=[vmem] * len(args),
            out_specs=[vmem] * 3,
            out_shape=[slab(2), slab(2), whole_sums],
            scratch_shapes=feature_scratch(4) + [slab_scratch(2)] * 2,
            compiler_params=limits(LIMIT_MIB),
            name="edge_relax",
        )(*args)

    def cell_params(parts, *sizes):
        return pl.pallas_call(
            functools.partial(param_kernel, total, len(parts)),
            in_specs=[vmem] * (len(parts) + 1) + [smem, smem],
            out_specs=[vmem] * len(sizes),
            out_shape=[jax.ShapeDtypeStruct((6, n, cells), F32) for n in sizes],
            compiler_params=limits(4),
            name="cell_params",
        )(*parts, codes, knudsen, inflow)

    def final(moved, params):
        return pl.pallas_call(
            functools.partial(final_kernel, rows),
            in_specs=[vmem] * 6,
            out_specs=hbm,
            out_shape=jax.ShapeDtypeStruct(distribution.shape, F32),
            scratch_shapes=feature_scratch(rows) + staging(rows),
            compiler_params=limits(LIMIT_MIB),
            name="final_relax",
        )(*moved, params, table, factor)

    parts = lax.axis_size("groups")
    across = []
    for p in range(parts):
        for i in (0, line - 1):
            other = p ^ 1 if (p ^ 1) < parts else p
            across.append((p * line + i, other * line + i))
        for i in range(1, line - 1, 2):
            across += [(p * line + i, p * line + i + 1), (p * line + i + 1, p * line + i)]
    within = []
    for i in range(0, line, 2):
        within += [(i, i + 1), (i + 1, i)]

    def exchange(cross, inside):
        return (
            lax.ppermute(cross, ("groups", "gx"), across),
            lax.ppermute(inside, "gx", within),
        )

    def gather(part):
        parts = [part]
        for shift in range(1, peers):
            pairs = [(i, (i + shift) % peers) for i in range(peers)]
            parts.append(lax.ppermute(part, "vert", pairs))
        return parts

    cross, near_inside, codes, table, factor, weights, coef = load()
    halos = exchange(cross, near_inside)
    middle, inside, m_mid, e_cross, e_in, sums = inner(
        False, (cross, near_inside, in_hbm(distribution)), None
    )
    m_in, in_sums = first_in(halos[1], inside, e_in)
    m_cross, sums = first_cross(halos[0], cross, e_cross, middle, coef, weights, sums, in_sums)
    m_cross, m_in, sums = lax.optimization_barrier((m_cross, m_in, sums))
    for _ in range(1, STEPS):
        halos = exchange(m_cross, m_in)
        params, p_cross, p_in = cell_params(gather(sums), rows, 2, 2)
        p_halos = exchange(p_cross, p_in)
        moved = (m_cross, m_mid, m_in)
        *state, m_mid, e_cross, e_in, sums = inner(True, moved, params)
        m_cross, m_in, sums = edge(halos, p_halos, state, (e_cross, e_in), sums)
    (params,) = cell_params(gather(sums), rows)
    return final((m_cross, m_mid, m_in), params)


def solution(mesh):
    placed = (
        P(("groups", "gx"), None, None, "vert"),
        P("vert"),
        P(("groups", "gx"), None, None),
        P("groups"),
        P("groups"),
    )
    return jax.shard_map(
        body,
        mesh=mesh,
        in_specs=placed,
        out_specs=P(("groups", "gx"), None, None, "vert"),
        check_vma=False,
    )
```

```python
import functools

import jax
import jax.numpy as jnp
from jax import lax
from jax.experimental import pallas as pl
from jax.experimental.pallas import tpu as pltpu
from jax.sharding import PartitionSpec as P

VGX = 16
VGY = 16
VGZ = 8
STEPS = 3
LANES = 128
SUB = 8
FEATURES = 32
PAIR = 2 * LANES
UNIT = 3.0 / 16.0
LOG2E = 1.4426950408889634
LIMIT_MIB = 10
F32 = jnp.float32
BF16 = jnp.bfloat16


def minmod(lower, upper):
    return jnp.maximum(
        jnp.minimum(lower, upper), jnp.minimum(jnp.maximum(lower, upper), 0.0)
    )


def lanes_of(chunk):
    return pl.ds(pl.multiple_of(chunk * LANES, LANES), LANES)


def coefs_of(coef_ref, lanes):
    return [coef_ref[k, :, lanes] for k in range(9)]


def x_row(cells, rows, store, coef, change=False):
    reach, lean, ahead = coef[0], coef[1], coef[2] > 0.0
    first, last = rows[0], rows[-1]
    steps = {n: cells[n + 1] - cells[n] for n in range(first - 2, last + 2)}
    faces = {
        n: cells[n] + lean * minmod(steps[n - 1], steps[n])
        for n in range(first - 1, last + 2)
    }
    for n in rows:
        source = jnp.where(ahead, faces[n - 1], faces[n + 1])
        v = reach * (faces[n] - source)
        store(n, v if change else cells[n] - v)


def yz_row(source, out, fresh, row, lanes, coef):
    reach_y, lean_y, ahead_y = coef[3], coef[4], coef[5] > 0.0
    reach_z, lean_z, ahead_z = coef[6], coef[7], coef[8] > 0.0
    count = 16
    cells, steps, faces = {}, {}, {}

    def cell(y, t):
        y %= count
        if (y, t) not in cells:
            cells[y, t] = source[row, y, t, :, lanes]
        return cells[y, t]

    def step(y, t):
        y %= count
        if (y, t) not in steps:
            steps[y, t] = cell(y + 1, t) - cell(y, t)
        return steps[y, t]

    def face(y, t):
        y %= count
        if (y, t) not in faces:
            faces[y, t] = cell(y, t) + lean_y * minmod(step(y - 1, t), step(y, t))
        return faces[y, t]

    def up(v):
        return pltpu.roll(v, SUB - 1, 0)

    def down(v):
        return pltpu.roll(v, 1, 0)

    for y in range(count):
        even, odd = cell(y, 0), cell(y, 1)
        step_even = odd - even
        step_odd = up(even) - odd
        face_even = even + lean_z * minmod(down(step_odd), step_even)
        face_odd = odd + lean_z * minmod(step_even, step_odd)
        winds = (
            jnp.where(ahead_z, down(face_odd), face_odd),
            jnp.where(ahead_z, face_even, up(face_even)),
        )
        for t, z_face in enumerate((face_even, face_odd)):
            v = cell(y, t) if fresh else out[row, y, t, :, lanes]
            v -= reach_z * (z_face - winds[t])
            upwind = jnp.where(ahead_y, face(y - 1, t), face(y + 1, t))
            v -= reach_y * (face(y, t) - upwind)
            out[row, y, t, :, lanes] = v


def yz_rows(source, out, fresh, rows, coef_ref):
    chunks = source.shape[-1] // LANES

    def one(i, carry):
        chunk, row = i // rows, i % rows
        lanes = lanes_of(chunk)
        yz_row(source, out, fresh, row, lanes, coefs_of(coef_ref, lanes))
        return carry

    lax.fori_loop(0, chunks * rows, one, 0, unroll=4)


def row_moments(rows, weights, sums):
    for row, place in rows:
        flat = row[...].reshape(256, row.shape[-1])
        high = flat.astype(BF16)
        rest = (flat - high.astype(F32)).astype(BF16)
        both = jnp.concatenate([high, rest], axis=1)
        contract = (((1,), (1,)), ((), ()))
        part = lax.dot_general(weights[...], both, contract, preferred_element_type=F32)
        for m in range(4):
            sums[m, place : place + 1, :] = part[m : m + 1]
        sums[4, place : place + 1, :] = part[4:5] + part[5:6]


def three_parts(value):
    high = value.astype(BF16).astype(F32)
    rest = value - high
    middle = rest.astype(BF16).astype(F32)
    low = (rest - middle).astype(BF16).astype(F32)
    return high, middle, low


def spread_features(params, wide, tall, rows):
    alpha, beta_x, beta_y, beta_z, gamma, keep = params
    alpha = jnp.where(gamma == 0.0, -10000.0, alpha)
    zero = jnp.zeros_like(alpha)
    columns = []
    for value in (alpha, beta_x, beta_y, beta_z, gamma, gamma, keep):
        columns.extend(three_parts(value))
    columns.extend([zero] * (FEATURES - len(columns)))
    for k, value in enumerate(columns):
        for r in range(rows):
            wide[r, k : k + 1, :] = value[r : r + 1]
    for r in range(rows):
        tall[r] = wide[r].T.astype(BF16)


def relax_group(group, tall, table, factor, kept):
    for u, (place, _, _) in enumerate(group):
        keep = jnp.dot(tall[place], factor[...], preferred_element_type=F32)
        kept[u] = keep.reshape(16, 2, SUB, LANES)
    for u, (place, moved, store) in enumerate(group):
        for pair in range(moved.shape[-1] // PAIR):
            columns = table[:, pair * PAIR : (pair + 1) * PAIR]
            power = jnp.dot(tall[place], columns, preferred_element_type=F32)
            for half in range(2):
                chunk = 2 * pair + half
                shape = jnp.exp2(power[:, half * LANES : (half + 1) * LANES])
                shape = shape.reshape(16, 2, SUB, LANES)
                lanes = pl.ds(chunk * LANES, LANES)
                store(chunk, kept[u] * moved[:, :, :, lanes] + shape)


def into(row):
    def store(chunk, v):
        row[:, :, :, pl.ds(chunk * LANES, LANES)] = v

    return store


def param_kernel(total, count, *refs):
    parts = refs[:count]
    codes, knudsen, inflow, out, *edges = refs[count:]
    sums = [parts[0][m] for m in range(5)]
    for part in parts[1:]:
        sums = [s + part[m] for m, s in enumerate(sums)]
    density = sums[0] * (1.0 / total)
    scale = UNIT / sums[0]
    u_x, u_y, u_z = (sums[m] * scale for m in (1, 2, 3))
    heat = (UNIT * sums[4] * scale - (u_x * u_x + u_y * u_y + u_z * u_z)) * (1.0 / 3.0)
    rate = 0.5 * density / (density + knudsen[0])
    code = codes[...]
    flowing, wall = code == 1, code == 2
    closed = flowing | wall
    u_x = jnp.where(flowing, inflow[1], jnp.where(wall, 0.0, u_x))
    u_y = jnp.where(closed, 0.0, u_y)
    u_z = jnp.where(closed, 0.0, u_z)
    heat = jnp.where(flowing, inflow[2], jnp.where(wall, inflow[3], heat))
    amount = jnp.where(flowing, inflow[0], jnp.where(wall, density, rate * density))
    keep = jnp.where(closed, 0.0, 1.0 - rate)
    g = (-0.5 * LOG2E) / heat

    def line(u, n, unit):
        s = None
        for i in range(n):
            gap = (i + 0.5 - n / 2) * unit - u
            e = jnp.exp2(g * (gap * gap))
            s = e if s is None else s + e
        return s

    norm = line(u_x, VGX, 6.0 / VGX) * line(u_y, VGY, 6.0 / VGY)
    norm = norm * line(u_z, VGZ, 6.0 / VGZ) * (1.0 / total)
    alpha = (jnp.log(amount) - jnp.log(norm)) * LOG2E
    alpha = alpha + g * (u_x * u_x + u_y * u_y + u_z * u_z)
    lean = (-2.0 * UNIT) * g
    params = (alpha, lean * u_x, lean * u_y, lean * u_z, g * (UNIT * UNIT), keep)
    rows = code.shape[0]
    for k, value in enumerate(params):
        out[k] = value
        if edges:
            edges[0][k] = value[:2]
            edges[1][k] = value[rows - 2 :]


def row_copies(mirrored, whole, staged, first, sems, out=False):
    rows = whole.shape[0]
    copies = []
    for n in range(staged.shape[0]):
        place = jnp.where(mirrored > 0, rows - 1 - first - n, first + n)
        for c in range(staged.shape[2]):
            far = whole.at[place, :, :, pl.ds(c * LANES, LANES)]
            near = staged.at[n, :, c]
            pair = (near, far) if out else (far, near)
            copies.append(pltpu.make_async_copy(*pair, sems.at[n, c]))
    return copies


def unstage(staged, out):
    count = staged.shape[1]

    def one(i, carry):
        n, y = i // count, i % count
        for c in range(staged.shape[2]):
            for t in range(2):
                v = staged[n, y, c, pl.ds(t, SUB, stride=2), :]
                out[n, y, t, :, pl.ds(c * LANES, LANES)] = v
        return carry

    lax.fori_loop(0, staged.shape[0] * count, one, 0, unroll=4)


def load_kernel(order_in, codes_in, state, cross, inside, codes, table, factor, weights, coef,
                order, raw, flat, near_cross, near_inside, cross_sems, inside_sems, more_sems):
    rows, width = state.shape[0], order.shape[-1]
    mirrored = lax.axis_index("gx") % 2
    more = [
        pltpu.make_async_copy(order_in, order, more_sems.at[0]),
        pltpu.make_async_copy(codes_in, raw, more_sems.at[1]),
    ]
    copies = row_copies(mirrored, state, near_cross, 0, cross_sems)
    copies += row_copies(mirrored, state, near_inside, rows - 2, inside_sems)
    for copy in more + copies:
        copy.start()
    for copy in more:
        copy.wait()

    slots = jnp.broadcast_to(order[...], (SUB, width))
    n_x = 2 * (slots // (VGY * VGZ)) - (VGX - 1)
    n_y = 2 * (slots // VGZ % VGY) - (VGY - 1)
    n_z = 2 * (2 * (slots % VGZ) - (VGZ - 1))
    square = n_x * n_x + n_y * n_y + n_z * n_z
    low_part = square % 8
    whole = [n.astype(F32) for n in (n_x, n_y, n_z, square - low_part, low_part)]
    whole = [jnp.ones_like(whole[0])] + whole

    def pick(values, index):
        out = jnp.zeros_like(values[0])
        for k, value in enumerate(values):
            out = jnp.where(index == k, value, out)
        return out

    line = lax.broadcasted_iota(jnp.int32, (SUB, width), 0)
    moments = jnp.concatenate([pick(whole, line), jnp.zeros((SUB, width), F32)], axis=0)
    moments = moments.astype(BF16)
    weights[:, :width] = moments
    weights[:, width:] = moments
    table[...] = jnp.concatenate(
        [pick(whole, (line + SUB * g) // 3) for g in range(FEATURES // SUB)], axis=0
    ).astype(BF16)
    slot = lax.broadcasted_iota(jnp.int32, (FEATURES, LANES), 0)
    factor[...] = jnp.where((slot >= 18) & (slot < 21), 1.0, 0.0).astype(BF16)
    turn = jnp.where(mirrored > 0, -1.0, 1.0)
    for k, (n, scale) in enumerate(
        ((whole[1] * turn, 0.1), (whole[2], 1.0 / 30.0), (whole[3], 1.0 / 30.0))
    ):
        reach = jnp.abs(n * UNIT * scale)
        sign = jnp.where(n > 0.0, 1.0, -1.0)
        coef[3 * k] = reach
        coef[3 * k + 1] = 0.5 * sign * (1.0 - reach)
        coef[3 * k + 2] = sign

    span = raw.shape[2]
    z = lax.broadcasted_iota(jnp.int32, (span, span), 0)
    goes = lax.broadcasted_iota(jnp.int32, (span, span), 1)
    shuffle = jnp.where(goes == z % 2 * SUB + z // 2, 1.0, 0.0).astype(BF16)
    lined = raw[...].reshape(rows * raw.shape[1], span).astype(F32).astype(BF16)
    lined = jnp.dot(lined, shuffle, preferred_element_type=F32).astype(jnp.int32)
    raw[...] = lined.reshape(rows, raw.shape[1], span)
    for y in range(raw.shape[1]):
        flat[:, y * span : (y + 1) * span] = raw[:, y, :]
    for r in range(rows):
        place = jnp.where(mirrored > 0, rows - 1 - r, r)
        codes[r : r + 1, :] = flat[pl.ds(place, 1), :]
    half = len(copies) // 2
    for copy in copies[:half]:
        copy.wait()
    unstage(near_cross, cross)
    for copy in copies[half:]:
        copy.wait()
    unstage(near_inside, inside)


def inner_kernel(relax, rows, *refs):
    if relax:
        (m_cross, m_mid, m_in, params, table, factor, coef_ref, weights,
         cross, middle, inside, out, e_cross, e_in, sums, wide, tall, kept) = refs
        spread_features([params[k] for k in range(6)], wide, tall, rows)
        group = [(r, m_cross.at[r], into(cross.at[r])) for r in range(2)]
        group += [(2 + r, m_mid.at[r], into(middle.at[r])) for r in range(rows - 4)]
        group += [(rows - 2 + r, m_in.at[r], into(inside.at[r])) for r in range(2)]
        relax_group(group, tall, table, factor, kept)
    else:
        (cross, inside, state, coef_ref, weights, middle, out, e_cross, e_in, sums,
         near, sems) = refs
        mirrored = lax.axis_index("gx") % 2
        copies = row_copies(mirrored, state, near, 2, sems)
        for copy in copies:
            copy.start()
    yz_rows(cross, e_cross, True, 2, coef_ref)
    yz_rows(inside, e_in, True, 2, coef_ref)
    if not relax:
        for copy in copies:
            copy.wait()
        unstage(near, middle)
    chunks = middle.shape[-1] // LANES
    inner = rows - 4

    def along_x(i, carry):
        chunk, y = i // 16, i % 16
        lanes = lanes_of(chunk)
        coef = coefs_of(coef_ref, lanes)
        for t in range(2):
            cells = {}
            for n in range(rows):
                if n < 2:
                    cells[n] = cross[n, y, t, :, lanes]
                elif n < rows - 2:
                    cells[n] = middle[n - 2, y, t, :, lanes]
                else:
                    cells[n] = inside[n - rows + 2, y, t, :, lanes]

            def store(n, v, t=t):
                out[n - 2, y, t, :, lanes] = v

            x_row(cells, list(range(2, rows - 2)), store, coef)
        return carry

    lax.fori_loop(0, chunks * 16, along_x, 0, unroll=8)
    yz_rows(middle, out, False, inner, coef_ref)
    row_moments([(out.at[r], r) for r in range(inner)], weights, sums)


def presence(line):
    place = lax.axis_index("gx")
    return jnp.where((place == 0) | (place == line - 1), 0.0, 1.0)


def cross_x(low, cross, middle, before, out, y, t, lanes, coef, present):
    cells = {}
    for n in range(2):
        cells[-1 - n] = low[n, y, t, :, lanes] * present
        cells[n] = cross[n, y, t, :, lanes]
        cells[2 + n] = middle[n, y, t, :, lanes]

    def store(n, v):
        out[n, y, t, :, lanes] = before[n, y, t, :, lanes] - v

    x_row(cells, [0, 1], store, coef, True)


def in_x(high, inside, middle, before, out, y, t, lanes, coef):
    last = middle.shape[0]
    cells = {}
    for n in range(2):
        cells[n] = middle[last - 2 + n, y, t, :, lanes]
        cells[2 + n] = inside[n, y, t, :, lanes]
        cells[4 + n] = high[1 - n, y, t, :, lanes]

    def store(n, v):
        out[n - 2, y, t, :, lanes] = before[n - 2, y, t, :, lanes] - v

    x_row(cells, [2, 3], store, coef, True)


def each_place(middle, coef_ref, work):
    def one(i, carry):
        lanes = lanes_of(i // 16)
        coef = coefs_of(coef_ref, lanes)
        for t in range(2):
            work(i % 16, t, lanes, coef)
        return carry

    lax.fori_loop(0, middle.shape[-1] // LANES * 16, one, 0, unroll=4)


def first_in_kernel(high, inside, e_in, middle, coef_ref, weights, out, sums):
    each_place(middle, coef_ref, lambda *at: in_x(high, inside, middle, e_in, out, *at))
    row_moments([(out.at[r], r) for r in range(2)], weights, sums)


def first_cross_kernel(line, low, cross, e_cross, middle, coef_ref, weights, inner_sums, in_sums,
                       out, sums):
    present = presence(line)
    each_place(
        middle, coef_ref, lambda *at: cross_x(low, cross, middle, e_cross, out, *at, present)
    )
    rows = sums.shape[1]
    for m in range(5):
        sums[m, 2 : rows - 2, :] = inner_sums[m]
        sums[m, rows - 2 :, :] = in_sums[m]
    row_moments([(out.at[r], r) for r in range(2)], weights, sums)


def edge_kernel(rows, line, h_cross, h_in, p_cross, p_in, table, factor, cross, middle, inside,
                e_cross, e_in, coef_ref, weights, inner_sums, out_cross, out_in, sums,
                wide, tall, kept, low, high):
    params = [jnp.concatenate([p_cross[k], p_in[k]], axis=0) for k in range(6)]
    spread_features(params, wide, tall, 4)
    group = [(r, h_cross.at[r], into(low.at[r])) for r in range(2)]
    group += [(2 + r, h_in.at[r], into(high.at[r])) for r in range(2)]
    relax_group(group, tall, table, factor, kept)
    present = presence(line)

    def work(*at):
        cross_x(low, cross, middle, e_cross, out_cross, *at, present)
        in_x(high, inside, middle, e_in, out_in, *at)

    each_place(middle, coef_ref, work)
    for m in range(5):
        sums[m, 2 : rows - 2, :] = inner_sums[m]
    edges = [(out_cross.at[r], r) for r in range(2)]
    edges += [(out_in.at[r], rows - 2 + r) for r in range(2)]
    row_moments(edges, weights, sums)


def final_kernel(rows, m_cross, m_mid, m_in, params, table, factor, out,
                 wide, tall, kept, staged, sems):
    mirrored = lax.axis_index("gx") % 2
    spread_features([params[k] for k in range(6)], wide, tall, rows)
    moved = [m_cross.at[r] for r in range(2)] + [m_mid.at[r] for r in range(rows - 4)]
    moved += [m_in.at[r] for r in range(2)]
    copies = []
    for first in range(0, rows, 2):
        near = staged.at[pl.ds(first, 2)]
        group = []
        for r in range(2):

            def store(chunk, v, row=near.at[r]):
                for y in range(16):
                    for t in range(2):
                        row[y, chunk, pl.ds(t, SUB, stride=2), :] = v[y, t]

            group.append((first + r, moved[first + r], store))
        relax_group(group, tall, table, factor, kept)
        more = row_copies(mirrored, out, near, first, sems.at[pl.ds(first, 2)], True)
        for copy in more:
            copy.start()
        copies += more
    for copy in copies:
        copy.wait()


def body(distribution, velocity_order, cell_codes, knudsen, inflow):
    rows, count_y, count_z, width = distribution.shape
    peers = lax.axis_size("vert")
    line = lax.axis_size("gx")
    total = width * peers
    cells = count_y * count_z
    chunks = width // LANES

    vmem = pl.BlockSpec(memory_space=pltpu.VMEM)
    smem = pl.BlockSpec(memory_space=pltpu.SMEM)
    hbm = pl.BlockSpec(memory_space=pltpu.HBM)

    def slab(n):
        return jax.ShapeDtypeStruct((n, count_y, 2, SUB, width), F32)

    def slab_scratch(n):
        return pltpu.VMEM((n, count_y, 2, SUB, width), F32)

    def feature_scratch(n):
        return [
            pltpu.VMEM((n, FEATURES, cells), F32),
            pltpu.VMEM((n, cells, FEATURES), BF16),
            pltpu.VMEM((n, count_y, 2, SUB, LANES), F32),
        ]

    def staging(n):
        return [
            pltpu.VMEM((n, count_y, chunks, count_z, LANES), F32),
            pltpu.SemaphoreType.DMA((n, chunks)),
        ]

    def limits(mib):
        return pltpu.CompilerParams(vmem_limit_bytes=mib * 1024 * 1024)

    def in_hbm(array):
        return pltpu.with_memory_space_constraint(array, pltpu.HBM)

    def load():
        return pl.pallas_call(
            load_kernel,
            in_specs=[hbm] * 3,
            out_specs=[vmem] * 7,
            out_shape=[
                slab(2),
                slab(2),
                jax.ShapeDtypeStruct((rows, cells), jnp.int32),
                jax.ShapeDtypeStruct((FEATURES, width), BF16),
                jax.ShapeDtypeStruct((FEATURES, LANES), BF16),
                jax.ShapeDtypeStruct((16, 2 * width), BF16),
                jax.ShapeDtypeStruct((9, SUB, width), F32),
            ],
            scratch_shapes=[
                pltpu.VMEM((1, width), jnp.int32),
                pltpu.VMEM((rows, count_y, count_z), jnp.int32),
                pltpu.VMEM((rows, cells), jnp.int32),
                staging(2)[0],
                staging(2)[0],
                staging(2)[1],
                staging(2)[1],
                pltpu.SemaphoreType.DMA((2,)),
            ],
            compiler_params=limits(6),
            name="load_edges",
        )(in_hbm(velocity_order.reshape(1, width)), in_hbm(cell_codes), in_hbm(distribution))

    def inner(relax, state, params):
        sums = jax.ShapeDtypeStruct((5, rows - 4, cells), F32)
        out_shape = [slab(rows - 4), slab(2), slab(2), sums]
        scratch = []
        if relax:
            out_shape = [slab(2), slab(rows - 4), slab(2)] + out_shape
            scratch = feature_scratch(rows)
            args = (*state, params, table, factor, coef, weights)
        else:
            out_shape = [slab(rows - 4)] + out_shape
            scratch = staging(rows - 4)
            args = (*state, coef, weights)
        return pl.pallas_call(
            functools.partial(inner_kernel, relax, rows),
            in_specs=[vmem if relax or n != 2 else hbm for n in range(len(args))],
            out_specs=[vmem] * len(out_shape),
            out_shape=out_shape,
            scratch_shapes=scratch,
            compiler_params=limits(LIMIT_MIB),
            name="inner_relax" if relax else "inner_first",
        )(*args)

    whole_sums = jax.ShapeDtypeStruct((5, rows, cells), F32)
    edge_sums = jax.ShapeDtypeStruct((5, 2, cells), F32)

    def first_in(*args):
        return pl.pallas_call(
            first_in_kernel,
            in_specs=[vmem] * 6,
            out_specs=[vmem] * 2,
            out_shape=[slab(2), edge_sums],
            compiler_params=limits(LIMIT_MIB),
            name="first_in",
        )(*args, middle, coef, weights)

    def first_cross(*args):
        return pl.pallas_call(
            functools.partial(first_cross_kernel, line),
            in_specs=[vmem] * 8,
            out_specs=[vmem] * 2,
            out_shape=[slab(2), whole_sums],
            compiler_params=limits(LIMIT_MIB),
            name="first_cross",
        )(*args)

    def edge(halos, params, state, edges, sums):
        args = (*halos, *params, table, factor, *state, *edges, coef, weights, sums)
        return pl.pallas_call(
            functools.partial(edge_kernel, rows, line),
            in_specs=[vmem] * len(args),
            out_specs=[vmem] * 3,
            out_shape=[slab(2), slab(2), whole_sums],
            scratch_shapes=feature_scratch(4) + [slab_scratch(2)] * 2,
            compiler_params=limits(LIMIT_MIB),
            name="edge_relax",
        )(*args)

    def cell_params(parts, *sizes):
        return pl.pallas_call(
            functools.partial(param_kernel, total, len(parts)),
            in_specs=[vmem] * (len(parts) + 1) + [smem, smem],
            out_specs=[vmem] * len(sizes),
            out_shape=[jax.ShapeDtypeStruct((6, n, cells), F32) for n in sizes],
            compiler_params=limits(4),
            name="cell_params",
        )(*parts, codes, knudsen, inflow)

    def final(moved, params):
        return pl.pallas_call(
            functools.partial(final_kernel, rows),
            in_specs=[vmem] * 6,
            out_specs=hbm,
            out_shape=jax.ShapeDtypeStruct(distribution.shape, F32),
            scratch_shapes=feature_scratch(rows) + staging(rows),
            compiler_params=limits(LIMIT_MIB),
            name="final_relax",
        )(*moved, params, table, factor)

    parts = lax.axis_size("groups")
    across = []
    for p in range(parts):
        for i in (0, line - 1):
            other = p ^ 1 if (p ^ 1) < parts else p
            across.append((p * line + i, other * line + i))
        for i in range(1, line - 1, 2):
            across += [(p * line + i, p * line + i + 1), (p * line + i + 1, p * line + i)]
    within = []
    for i in range(0, line, 2):
        within += [(i, i + 1), (i + 1, i)]

    def exchange(cross, inside):
        return (
            lax.ppermute(cross, ("groups", "gx"), across),
            lax.ppermute(inside, "gx", within),
        )

    def gather(part):
        parts = [part]
        for shift in range(1, peers):
            pairs = [(i, (i + shift) % peers) for i in range(peers)]
            parts.append(lax.ppermute(part, "vert", pairs))
        return parts

    cross, inside, codes, table, factor, weights, coef = load()
    halos = exchange(cross, inside)
    middle, m_mid, e_cross, e_in, sums = inner(False, (cross, inside, in_hbm(distribution)), None)
    m_in, in_sums = first_in(halos[1], inside, e_in)
    m_cross, sums = first_cross(halos[0], cross, e_cross, middle, coef, weights, sums, in_sums)
    m_cross, m_in, sums = lax.optimization_barrier((m_cross, m_in, sums))
    for _ in range(1, STEPS):
        halos = exchange(m_cross, m_in)
        params, p_cross, p_in = cell_params(gather(sums), rows, 2, 2)
        p_halos = exchange(p_cross, p_in)
        moved = (m_cross, m_mid, m_in)
        *state, m_mid, e_cross, e_in, sums = inner(True, moved, params)
        m_cross, m_in, sums = edge(halos, p_halos, state, (e_cross, e_in), sums)
    (params,) = cell_params(gather(sums), rows)
    return final((m_cross, m_mid, m_in), params)


def solution(mesh):
    placed = (
        P(("groups", "gx"), None, None, "vert"),
        P("vert"),
        P(("groups", "gx"), None, None),
        P("groups"),
        P("groups"),
    )
    return jax.shard_map(
        body,
        mesh=mesh,
        in_specs=placed,
        out_specs=P(("groups", "gx"), None, None, "vert"),
        check_vma=False,
    )
```

```python
import functools

import jax
import jax.numpy as jnp
from jax import lax
from jax.experimental import pallas as pl
from jax.experimental.pallas import tpu as pltpu
from jax.sharding import PartitionSpec as P

VGX = 16
VGY = 16
VGZ = 8
STEPS = 3
LANES = 128
SUB = 8
FEATURES = 32
PAIR = 2 * LANES
UNIT = 3.0 / 16.0
LOG2E = 1.4426950408889634
LIMIT_MIB = 10
F32 = jnp.float32
BF16 = jnp.bfloat16


def minmod(lower, upper):
    return jnp.maximum(
        jnp.minimum(lower, upper), jnp.minimum(jnp.maximum(lower, upper), 0.0)
    )


def lanes_of(chunk):
    return pl.ds(pl.multiple_of(chunk * LANES, LANES), LANES)


def coefs_of(coef_ref, lanes):
    return [coef_ref[k, :, lanes] for k in range(9)]


def x_row(cells, rows, store, coef, change=False):
    reach, lean, ahead = coef[0], coef[1], coef[2] > 0.0
    first, last = rows[0], rows[-1]
    steps = {n: cells[n + 1] - cells[n] for n in range(first - 2, last + 2)}
    faces = {
        n: cells[n] + lean * minmod(steps[n - 1], steps[n])
        for n in range(first - 1, last + 2)
    }
    for n in rows:
        source = jnp.where(ahead, faces[n - 1], faces[n + 1])
        v = reach * (faces[n] - source)
        store(n, v if change else cells[n] - v)


def yz_row(source, out, fresh, row, lanes, coef):
    reach_y, lean_y, ahead_y = coef[3], coef[4], coef[5] > 0.0
    reach_z, lean_z, ahead_z = coef[6], coef[7], coef[8] > 0.0
    count = 16
    cells, steps, faces = {}, {}, {}

    def cell(y, t):
        y %= count
        if (y, t) not in cells:
            cells[y, t] = source[row, y, t, :, lanes]
        return cells[y, t]

    def step(y, t):
        y %= count
        if (y, t) not in steps:
            steps[y, t] = cell(y + 1, t) - cell(y, t)
        return steps[y, t]

    def face(y, t):
        y %= count
        if (y, t) not in faces:
            faces[y, t] = cell(y, t) + lean_y * minmod(step(y - 1, t), step(y, t))
        return faces[y, t]

    def up(v):
        return pltpu.roll(v, SUB - 1, 0)

    def down(v):
        return pltpu.roll(v, 1, 0)

    for y in range(count):
        even, odd = cell(y, 0), cell(y, 1)
        step_even = odd - even
        step_odd = up(even) - odd
        face_even = even + lean_z * minmod(down(step_odd), step_even)
        face_odd = odd + lean_z * minmod(step_even, step_odd)
        winds = (
            jnp.where(ahead_z, down(face_odd), face_odd),
            jnp.where(ahead_z, face_even, up(face_even)),
        )
        for t, z_face in enumerate((face_even, face_odd)):
            v = cell(y, t) if fresh else out[row, y, t, :, lanes]
            v -= reach_z * (z_face - winds[t])
            upwind = jnp.where(ahead_y, face(y - 1, t), face(y + 1, t))
            v -= reach_y * (face(y, t) - upwind)
            out[row, y, t, :, lanes] = v


def yz_rows(source, out, fresh, rows, coef_ref):
    chunks = source.shape[-1] // LANES

    def one(i, carry):
        chunk, row = i // rows, i % rows
        lanes = lanes_of(chunk)
        yz_row(source, out, fresh, row, lanes, coefs_of(coef_ref, lanes))
        return carry

    lax.fori_loop(0, chunks * rows, one, 0, unroll=4)


def row_moments(rows, weights, sums):
    for row, place in rows:
        flat = row[...].reshape(256, row.shape[-1])
        high = flat.astype(BF16)
        rest = (flat - high.astype(F32)).astype(BF16)
        both = jnp.concatenate([high, rest], axis=1)
        contract = (((1,), (1,)), ((), ()))
        part = lax.dot_general(weights[...], both, contract, preferred_element_type=F32)
        for m in range(4):
            sums[m, place : place + 1, :] = part[m : m + 1]
        sums[4, place : place + 1, :] = part[4:5] + part[5:6]


def three_parts(value):
    high = value.astype(BF16).astype(F32)
    rest = value - high
    middle = rest.astype(BF16).astype(F32)
    low = (rest - middle).astype(BF16).astype(F32)
    return high, middle, low


def spread_features(params, wide, tall, rows):
    alpha, beta_x, beta_y, beta_z, gamma, keep = params
    alpha = jnp.where(gamma == 0.0, -10000.0, alpha)
    zero = jnp.zeros_like(alpha)
    columns = []
    for value in (alpha, beta_x, beta_y, beta_z, gamma, gamma, keep):
        columns.extend(three_parts(value))
    columns.extend([zero] * (FEATURES - len(columns)))
    for k, value in enumerate(columns):
        for r in range(rows):
            wide[r, k : k + 1, :] = value[r : r + 1]
    for r in range(rows):
        tall[r] = wide[r].T.astype(BF16)


def relax_group(group, tall, table, factor, kept):
    for u, (place, _, _) in enumerate(group):
        keep = jnp.dot(tall[place], factor[...], preferred_element_type=F32)
        kept[u] = keep.reshape(16, 2, SUB, LANES)
    for u, (place, moved, store) in enumerate(group):
        for pair in range(moved.shape[-1] // PAIR):
            columns = table[:, pair * PAIR : (pair + 1) * PAIR]
            power = jnp.dot(tall[place], columns, preferred_element_type=F32)
            for half in range(2):
                chunk = 2 * pair + half
                shape = jnp.exp2(power[:, half * LANES : (half + 1) * LANES])
                shape = shape.reshape(16, 2, SUB, LANES)
                lanes = pl.ds(chunk * LANES, LANES)
                store(chunk, kept[u] * moved[:, :, :, lanes] + shape)


def into(row):
    def store(chunk, v):
        row[:, :, :, pl.ds(chunk * LANES, LANES)] = v

    return store


def param_kernel(total, count, *refs):
    parts = refs[:count]
    codes, knudsen, inflow, out, *edges = refs[count:]
    sums = [parts[0][m] for m in range(5)]
    for part in parts[1:]:
        sums = [s + part[m] for m, s in enumerate(sums)]
    density = sums[0] * (1.0 / total)
    scale = UNIT / sums[0]
    u_x, u_y, u_z = (sums[m] * scale for m in (1, 2, 3))
    heat = (UNIT * sums[4] * scale - (u_x * u_x + u_y * u_y + u_z * u_z)) * (1.0 / 3.0)
    rate = 0.5 * density / (density + knudsen[0])
    code = codes[...]
    flowing, wall = code == 1, code == 2
    closed = flowing | wall
    u_x = jnp.where(flowing, inflow[1], jnp.where(wall, 0.0, u_x))
    u_y = jnp.where(closed, 0.0, u_y)
    u_z = jnp.where(closed, 0.0, u_z)
    heat = jnp.where(flowing, inflow[2], jnp.where(wall, inflow[3], heat))
    amount = jnp.where(flowing, inflow[0], jnp.where(wall, density, rate * density))
    keep = jnp.where(closed, 0.0, 1.0 - rate)
    g = (-0.5 * LOG2E) / heat

    def line(u, n, unit):
        s = None
        for i in range(n):
            gap = (i + 0.5 - n / 2) * unit - u
            e = jnp.exp2(g * (gap * gap))
            s = e if s is None else s + e
        return s

    norm = line(u_x, VGX, 6.0 / VGX) * line(u_y, VGY, 6.0 / VGY)
    norm = norm * line(u_z, VGZ, 6.0 / VGZ) * (1.0 / total)
    alpha = (jnp.log(amount) - jnp.log(norm)) * LOG2E
    alpha = alpha + g * (u_x * u_x + u_y * u_y + u_z * u_z)
    lean = (-2.0 * UNIT) * g
    params = (alpha, lean * u_x, lean * u_y, lean * u_z, g * (UNIT * UNIT), keep)
    rows = code.shape[0]
    for k, value in enumerate(params):
        out[k] = value
        if edges:
            edges[0][k] = value[:2]
            edges[1][k] = value[rows - 2 :]


def row_copies(mirrored, whole, staged, first, sems, out=False):
    rows = whole.shape[0]
    copies = []
    for n in range(staged.shape[0]):
        place = jnp.where(mirrored > 0, rows - 1 - first - n, first + n)
        for c in range(staged.shape[2]):
            far = whole.at[place, :, :, pl.ds(c * LANES, LANES)]
            near = staged.at[n, :, c]
            pair = (near, far) if out else (far, near)
            copies.append(pltpu.make_async_copy(*pair, sems.at[n, c]))
    return copies


def unstage(staged, out):
    count = staged.shape[1]

    def one(i, carry):
        n, y = i // count, i % count
        for c in range(staged.shape[2]):
            for t in range(2):
                v = staged[n, y, c, pl.ds(t, SUB, stride=2), :]
                out[n, y, t, :, pl.ds(c * LANES, LANES)] = v
        return carry

    lax.fori_loop(0, staged.shape[0] * count, one, 0, unroll=4)


def load_kernel(order_in, codes_in, state, cross, inside, codes, table, factor, weights, coef,
                order, raw, flat, near_cross, near_inside, cross_sems, inside_sems, more_sems):
    rows, width = state.shape[0], order.shape[-1]
    mirrored = lax.axis_index("gx") % 2
    more = [
        pltpu.make_async_copy(order_in, order, more_sems.at[0]),
        pltpu.make_async_copy(codes_in, raw, more_sems.at[1]),
    ]
    copies = row_copies(mirrored, state, near_cross, 0, cross_sems)
    copies += row_copies(mirrored, state, near_inside, rows - 2, inside_sems)
    for copy in more + copies:
        copy.start()
    for copy in more:
        copy.wait()

    slots = jnp.broadcast_to(order[...], (SUB, width))
    n_x = 2 * (slots // (VGY * VGZ)) - (VGX - 1)
    n_y = 2 * (slots // VGZ % VGY) - (VGY - 1)
    n_z = 2 * (2 * (slots % VGZ) - (VGZ - 1))
    square = n_x * n_x + n_y * n_y + n_z * n_z
    low_part = square % 8
    whole = [n.astype(F32) for n in (n_x, n_y, n_z, square - low_part, low_part)]
    whole = [jnp.ones_like(whole[0])] + whole

    def pick(values, index):
        out = jnp.zeros_like(values[0])
        for k, value in enumerate(values):
            out = jnp.where(index == k, value, out)
        return out

    line = lax.broadcasted_iota(jnp.int32, (SUB, width), 0)
    moments = jnp.concatenate([pick(whole, line), jnp.zeros((SUB, width), F32)], axis=0)
    moments = moments.astype(BF16)
    weights[:, :width] = moments
    weights[:, width:] = moments
    table[...] = jnp.concatenate(
        [pick(whole, (line + SUB * g) // 3) for g in range(FEATURES // SUB)], axis=0
    ).astype(BF16)
    slot = lax.broadcasted_iota(jnp.int32, (FEATURES, LANES), 0)
    factor[...] = jnp.where((slot >= 18) & (slot < 21), 1.0, 0.0).astype(BF16)
    turn = jnp.where(mirrored > 0, -1.0, 1.0)
    for k, (n, scale) in enumerate(
        ((whole[1] * turn, 0.1), (whole[2], 1.0 / 30.0), (whole[3], 1.0 / 30.0))
    ):
        reach = jnp.abs(n * UNIT * scale)
        sign = jnp.where(n > 0.0, 1.0, -1.0)
        coef[3 * k] = reach
        coef[3 * k + 1] = 0.5 * sign * (1.0 - reach)
        coef[3 * k + 2] = sign

    span = raw.shape[2]
    z = lax.broadcasted_iota(jnp.int32, (span, span), 0)
    goes = lax.broadcasted_iota(jnp.int32, (span, span), 1)
    shuffle = jnp.where(goes == z % 2 * SUB + z // 2, 1.0, 0.0).astype(BF16)
    lined = raw[...].reshape(rows * raw.shape[1], span).astype(F32).astype(BF16)
    lined = jnp.dot(lined, shuffle, preferred_element_type=F32).astype(jnp.int32)
    raw[...] = lined.reshape(rows, raw.shape[1], span)
    for y in range(raw.shape[1]):
        flat[:, y * span : (y + 1) * span] = raw[:, y, :]
    for r in range(rows):
        place = jnp.where(mirrored > 0, rows - 1 - r, r)
        codes[r : r + 1, :] = flat[pl.ds(place, 1), :]
    half = len(copies) // 2
    for copy in copies[:half]:
        copy.wait()
    unstage(near_cross, cross)
    for copy in copies[half:]:
        copy.wait()
    unstage(near_inside, inside)


def inner_kernel(relax, rows, *refs):
    if relax:
        (m_cross, m_mid, m_in, params, table, factor, coef_ref, weights,
         cross, middle, inside, out, e_cross, e_in, sums, wide, tall, kept) = refs
        spread_features([params[k] for k in range(6)], wide, tall, rows)
        group = [(r, m_cross.at[r], into(cross.at[r])) for r in range(2)]
        group += [(2 + r, m_mid.at[r], into(middle.at[r])) for r in range(rows - 4)]
        group += [(rows - 2 + r, m_in.at[r], into(inside.at[r])) for r in range(2)]
        relax_group(group, tall, table, factor, kept)
    else:
        (cross, inside, state, coef_ref, weights, middle, out, e_cross, e_in, sums,
         near, sems) = refs
        mirrored = lax.axis_index("gx") % 2
        copies = row_copies(mirrored, state, near, 2, sems)
        for copy in copies:
            copy.start()
    yz_rows(cross, e_cross, True, 2, coef_ref)
    yz_rows(inside, e_in, True, 2, coef_ref)
    if not relax:
        for copy in copies:
            copy.wait()
        unstage(near, middle)
    chunks = middle.shape[-1] // LANES
    inner = rows - 4

    def along_x(i, carry):
        chunk, y = i // 16, i % 16
        lanes = lanes_of(chunk)
        coef = coefs_of(coef_ref, lanes)
        for t in range(2):
            cells = {}
            for n in range(rows):
                if n < 2:
                    cells[n] = cross[n, y, t, :, lanes]
                elif n < rows - 2:
                    cells[n] = middle[n - 2, y, t, :, lanes]
                else:
                    cells[n] = inside[n - rows + 2, y, t, :, lanes]

            def store(n, v, t=t):
                out[n - 2, y, t, :, lanes] = v

            x_row(cells, list(range(2, rows - 2)), store, coef)
        return carry

    lax.fori_loop(0, chunks * 16, along_x, 0, unroll=8)
    yz_rows(middle, out, False, inner, coef_ref)
    row_moments([(out.at[r], r) for r in range(inner)], weights, sums)


def presence(line):
    place = lax.axis_index("gx")
    return jnp.where((place == 0) | (place == line - 1), 0.0, 1.0)


def cross_x(low, cross, middle, before, out, y, t, lanes, coef, present):
    cells = {}
    for n in range(2):
        cells[-1 - n] = low[n, y, t, :, lanes] * present
        cells[n] = cross[n, y, t, :, lanes]
        cells[2 + n] = middle[n, y, t, :, lanes]

    def store(n, v):
        out[n, y, t, :, lanes] = before[n, y, t, :, lanes] - v

    x_row(cells, [0, 1], store, coef, True)


def in_x(high, inside, middle, before, out, y, t, lanes, coef):
    last = middle.shape[0]
    cells = {}
    for n in range(2):
        cells[n] = middle[last - 2 + n, y, t, :, lanes]
        cells[2 + n] = inside[n, y, t, :, lanes]
        cells[4 + n] = high[1 - n, y, t, :, lanes]

    def store(n, v):
        out[n - 2, y, t, :, lanes] = before[n - 2, y, t, :, lanes] - v

    x_row(cells, [2, 3], store, coef, True)


def each_place(middle, coef_ref, work):
    def one(i, carry):
        lanes = lanes_of(i // 16)
        coef = coefs_of(coef_ref, lanes)
        for t in range(2):
            work(i % 16, t, lanes, coef)
        return carry

    lax.fori_loop(0, middle.shape[-1] // LANES * 16, one, 0, unroll=8)


def first_in_kernel(high, inside, e_in, middle, coef_ref, weights, out, sums):
    each_place(middle, coef_ref, lambda *at: in_x(high, inside, middle, e_in, out, *at))
    row_moments([(out.at[r], r) for r in range(2)], weights, sums)


def first_cross_kernel(line, low, cross, e_cross, middle, coef_ref, weights, inner_sums, in_sums,
                       out, sums):
    present = presence(line)
    each_place(
        middle, coef_ref, lambda *at: cross_x(low, cross, middle, e_cross, out, *at, present)
    )
    rows = sums.shape[1]
    for m in range(5):
        sums[m, 2 : rows - 2, :] = inner_sums[m]
        sums[m, rows - 2 :, :] = in_sums[m]
    row_moments([(out.at[r], r) for r in range(2)], weights, sums)


def edge_kernel(rows, line, h_cross, h_in, p_cross, p_in, table, factor, cross, middle, inside,
                e_cross, e_in, coef_ref, weights, inner_sums, out_cross, out_in, sums,
                wide, tall, kept, low, high):
    params = [jnp.concatenate([p_cross[k], p_in[k]], axis=0) for k in range(6)]
    spread_features(params, wide, tall, 4)
    group = [(r, h_cross.at[r], into(low.at[r])) for r in range(2)]
    group += [(2 + r, h_in.at[r], into(high.at[r])) for r in range(2)]
    relax_group(group, tall, table, factor, kept)
    present = presence(line)

    def work(*at):
        cross_x(low, cross, middle, e_cross, out_cross, *at, present)
        in_x(high, inside, middle, e_in, out_in, *at)

    each_place(middle, coef_ref, work)
    for m in range(5):
        sums[m, 2 : rows - 2, :] = inner_sums[m]
    edges = [(out_cross.at[r], r) for r in range(2)]
    edges += [(out_in.at[r], rows - 2 + r) for r in range(2)]
    row_moments(edges, weights, sums)


def final_kernel(rows, m_cross, m_mid, m_in, params, table, factor, out,
                 wide, tall, kept, staged, sems):
    mirrored = lax.axis_index("gx") % 2
    spread_features([params[k] for k in range(6)], wide, tall, rows)
    moved = [m_cross.at[r] for r in range(2)] + [m_mid.at[r] for r in range(rows - 4)]
    moved += [m_in.at[r] for r in range(2)]
    copies = []
    for first in range(0, rows, 2):
        near = staged.at[pl.ds(first, 2)]
        group = []
        for r in range(2):

            def store(chunk, v, row=near.at[r]):
                for y in range(16):
                    for t in range(2):
                        row[y, chunk, pl.ds(t, SUB, stride=2), :] = v[y, t]

            group.append((first + r, moved[first + r], store))
        relax_group(group, tall, table, factor, kept)
        more = row_copies(mirrored, out, near, first, sems.at[pl.ds(first, 2)], True)
        for copy in more:
            copy.start()
        copies += more
    for copy in copies:
        copy.wait()


def body(distribution, velocity_order, cell_codes, knudsen, inflow):
    rows, count_y, count_z, width = distribution.shape
    peers = lax.axis_size("vert")
    line = lax.axis_size("gx")
    total = width * peers
    cells = count_y * count_z
    chunks = width // LANES

    vmem = pl.BlockSpec(memory_space=pltpu.VMEM)
    smem = pl.BlockSpec(memory_space=pltpu.SMEM)
    hbm = pl.BlockSpec(memory_space=pltpu.HBM)

    def slab(n):
        return jax.ShapeDtypeStruct((n, count_y, 2, SUB, width), F32)

    def slab_scratch(n):
        return pltpu.VMEM((n, count_y, 2, SUB, width), F32)

    def feature_scratch(n):
        return [
            pltpu.VMEM((n, FEATURES, cells), F32),
            pltpu.VMEM((n, cells, FEATURES), BF16),
            pltpu.VMEM((n, count_y, 2, SUB, LANES), F32),
        ]

    def staging(n):
        return [
            pltpu.VMEM((n, count_y, chunks, count_z, LANES), F32),
            pltpu.SemaphoreType.DMA((n, chunks)),
        ]

    def limits(mib):
        return pltpu.CompilerParams(vmem_limit_bytes=mib * 1024 * 1024)

    def in_hbm(array):
        return pltpu.with_memory_space_constraint(array, pltpu.HBM)

    def load():
        return pl.pallas_call(
            load_kernel,
            in_specs=[hbm] * 3,
            out_specs=[vmem] * 7,
            out_shape=[
                slab(2),
                slab(2),
                jax.ShapeDtypeStruct((rows, cells), jnp.int32),
                jax.ShapeDtypeStruct((FEATURES, width), BF16),
                jax.ShapeDtypeStruct((FEATURES, LANES), BF16),
                jax.ShapeDtypeStruct((16, 2 * width), BF16),
                jax.ShapeDtypeStruct((9, SUB, width), F32),
            ],
            scratch_shapes=[
                pltpu.VMEM((1, width), jnp.int32),
                pltpu.VMEM((rows, count_y, count_z), jnp.int32),
                pltpu.VMEM((rows, cells), jnp.int32),
                staging(2)[0],
                staging(2)[0],
                staging(2)[1],
                staging(2)[1],
                pltpu.SemaphoreType.DMA((2,)),
            ],
            compiler_params=limits(6),
            name="load_edges",
        )(in_hbm(velocity_order.reshape(1, width)), in_hbm(cell_codes), in_hbm(distribution))

    def inner(relax, state, params):
        sums = jax.ShapeDtypeStruct((5, rows - 4, cells), F32)
        out_shape = [slab(rows - 4), slab(2), slab(2), sums]
        scratch = []
        if relax:
            out_shape = [slab(2), slab(rows - 4), slab(2)] + out_shape
            scratch = feature_scratch(rows)
            args = (*state, params, table, factor, coef, weights)
        else:
            out_shape = [slab(rows - 4)] + out_shape
            scratch = staging(rows - 4)
            args = (*state, coef, weights)
        return pl.pallas_call(
            functools.partial(inner_kernel, relax, rows),
            in_specs=[vmem if relax or n != 2 else hbm for n in range(len(args))],
            out_specs=[vmem] * len(out_shape),
            out_shape=out_shape,
            scratch_shapes=scratch,
            compiler_params=limits(LIMIT_MIB),
            name="inner_relax" if relax else "inner_first",
        )(*args)

    whole_sums = jax.ShapeDtypeStruct((5, rows, cells), F32)
    edge_sums = jax.ShapeDtypeStruct((5, 2, cells), F32)

    def first_in(*args):
        return pl.pallas_call(
            first_in_kernel,
            in_specs=[vmem] * 6,
            out_specs=[vmem] * 2,
            out_shape=[slab(2), edge_sums],
            compiler_params=limits(LIMIT_MIB),
            name="first_in",
        )(*args, middle, coef, weights)

    def first_cross(*args):
        return pl.pallas_call(
            functools.partial(first_cross_kernel, line),
            in_specs=[vmem] * 8,
            out_specs=[vmem] * 2,
            out_shape=[slab(2), whole_sums],
            compiler_params=limits(LIMIT_MIB),
            name="first_cross",
        )(*args)

    def edge(halos, params, state, edges, sums):
        args = (*halos, *params, table, factor, *state, *edges, coef, weights, sums)
        return pl.pallas_call(
            functools.partial(edge_kernel, rows, line),
            in_specs=[vmem] * len(args),
            out_specs=[vmem] * 3,
            out_shape=[slab(2), slab(2), whole_sums],
            scratch_shapes=feature_scratch(4) + [slab_scratch(2)] * 2,
            compiler_params=limits(LIMIT_MIB),
            name="edge_relax",
        )(*args)

    def cell_params(parts, *sizes):
        return pl.pallas_call(
            functools.partial(param_kernel, total, len(parts)),
            in_specs=[vmem] * (len(parts) + 1) + [smem, smem],
            out_specs=[vmem] * len(sizes),
            out_shape=[jax.ShapeDtypeStruct((6, n, cells), F32) for n in sizes],
            compiler_params=limits(4),
            name="cell_params",
        )(*parts, codes, knudsen, inflow)

    def final(moved, params):
        return pl.pallas_call(
            functools.partial(final_kernel, rows),
            in_specs=[vmem] * 6,
            out_specs=hbm,
            out_shape=jax.ShapeDtypeStruct(distribution.shape, F32),
            scratch_shapes=feature_scratch(rows) + staging(rows),
            compiler_params=limits(LIMIT_MIB),
            name="final_relax",
        )(*moved, params, table, factor)

    parts = lax.axis_size("groups")
    across = []
    for p in range(parts):
        for i in (0, line - 1):
            other = p ^ 1 if (p ^ 1) < parts else p
            across.append((p * line + i, other * line + i))
        for i in range(1, line - 1, 2):
            across += [(p * line + i, p * line + i + 1), (p * line + i + 1, p * line + i)]
    within = []
    for i in range(0, line, 2):
        within += [(i, i + 1), (i + 1, i)]

    def exchange(cross, inside):
        return (
            lax.ppermute(cross, ("groups", "gx"), across),
            lax.ppermute(inside, "gx", within),
        )

    def gather(part):
        parts = [part]
        for shift in range(1, peers):
            pairs = [(i, (i + shift) % peers) for i in range(peers)]
            parts.append(lax.ppermute(part, "vert", pairs))
        return parts

    cross, inside, codes, table, factor, weights, coef = load()
    halos = exchange(cross, inside)
    middle, m_mid, e_cross, e_in, sums = inner(False, (cross, inside, in_hbm(distribution)), None)
    m_in, in_sums = first_in(halos[1], inside, e_in)
    m_cross, sums = first_cross(halos[0], cross, e_cross, middle, coef, weights, sums, in_sums)
    m_cross, m_in, sums = lax.optimization_barrier((m_cross, m_in, sums))
    for _ in range(1, STEPS):
        halos = exchange(m_cross, m_in)
        params, p_cross, p_in = cell_params(gather(sums), rows, 2, 2)
        p_halos = exchange(p_cross, p_in)
        moved = (m_cross, m_mid, m_in)
        *state, m_mid, e_cross, e_in, sums = inner(True, moved, params)
        m_cross, m_in, sums = edge(halos, p_halos, state, (e_cross, e_in), sums)
    (params,) = cell_params(gather(sums), rows)
    return final((m_cross, m_mid, m_in), params)


def solution(mesh):
    placed = (
        P(("groups", "gx"), None, None, "vert"),
        P("vert"),
        P(("groups", "gx"), None, None),
        P("groups"),
        P("groups"),
    )
    return jax.shard_map(
        body,
        mesh=mesh,
        in_specs=placed,
        out_specs=P(("groups", "gx"), None, None, "vert"),
        check_vma=False,
    )
```
